32 devices in a mesh: group: 4 (over y, x), dev: 8 (over z, core).
Axes of the slice: x: 2, y: 2, z: 4, core: 2. Of those that a mesh axis runs over, the one named last changes fastest.
Arguments:
- q_compressed: bfloat16 [32, 1536], P('group'), may hold values from -6 to 6
- w_q_nope: bfloat16 [1536, 16384], P(None, 'dev'), may hold values from -0.15625 to 0.15625
- w_q_rope: bfloat16 [1536, 8192], P(None, 'dev'), may hold values from -0.15625 to 0.15625
- w_uk: bfloat16 [128, 128, 512], P('dev'), may hold values from -0.5 to 0.5
- w_uv: bfloat16 [128, 512, 128], P('dev'), may hold values from -0.25 to 0.25
- w_o: bfloat16 [16384, 7168], P('dev'), may hold values from -0.046875 to 0.046875
- kv_cache: bfloat16 [4, 8, 2, 2048, 576], P('group', 'dev'), may hold values from -320 to 320
- draft_kv: bfloat16 [32, 576], P('group'), may hold values from -18 to 18
- context_length: int32 [8], replicated, may hold values from 6145 to 24576
- slot_sequence: int32 [4, 8, 2], replicated, may hold values from -1 to 7, as said below
- slot_slab: int32 [4, 8, 2], replicated, may hold values from -1 to 11
Outputs:
- attn_output: float32 [32, 7168], P(('group', 'dev'))
The draws below stay inside these ranges and needn't reach their ends.
Inputs may be any that keep to these rules, and one draw needn't show every extreme that they name: For each sequence s, slabs 0 to ceil(context_length[s] / 2048) - 1 each stand in exactly one slot of the pool, slot_sequence naming s and slot_slab the slab's number; all other slots hold -1 in both tables. The sequences' slab counts are, in some order, 4 + floor(i * 8 / 7) for i from 0 to 7. A group's slots take the slabs of its own sequences first; slabs beyond a group's 8 * 2 slots stand in free slots of other groups.
All inputs are finite; a program needn't handle non-finite values.
Results may differ from the reference program's by a relative error of at most 0.02.
The reference program's roundings to bfloat16 on the way (of `q_nope`, `queries`, `attended` and `head_values`) count: a program that leaves them out, or rounds other values in their place, can miss the bound.
Values may be sent and summed in bfloat16 or wider, within the bound.
A program may use at most 128 MiB of HBM per device.

```python
import jax
import jax.numpy as jnp
from jax import lax

D = 7168
HEADS = 128
QRANK = 1536
NOPE = 128
ROPE = 64
LATENT = 512
VDIM = 128
DRAFT = 4
SLOTS = 2
MIN_SLABS = 4
MAX_SLABS = 12
SLAB = 2048
GROUPS = 4
HOLDERS = 8
SEQ_GRP = 2
SEQS = 8
TOKENS = 32
KV = 576


def placement(key):
    base_key = jax.random.fold_in(key, 5)
    key_heavy, key_order, key_tail, key_spread = jax.random.split(base_key, 4)
    seq_count = SEQ_GRP * GROUPS
    capacity = HOLDERS * SLOTS
    heavy = jax.random.randint(key_heavy, (), 0, GROUPS)
    home_group = jnp.arange(seq_count, dtype=jnp.int32) // SEQ_GRP
    score = jnp.where(home_group == heavy, seq_count, 0) + jax.random.permutation(key_order, seq_count).astype(jnp.int32)
    ranking = jnp.argsort(jnp.argsort(score, stable=True), stable=True).astype(jnp.int32)
    slab_count = MIN_SLABS + ranking * (MAX_SLABS - MIN_SLABS) // (seq_count - 1)
    tail_tokens = jax.random.randint(key_tail, (seq_count,), 1, SLAB + 1)
    tail_tokens = jnp.where(ranking == 0, 1, jnp.where(ranking == seq_count - 1, SLAB, tail_tokens))
    lengths = ((slab_count - 1) * SLAB + tail_tokens).astype(jnp.int32)
    per_group = slab_count.reshape(GROUPS, SEQ_GRP)
    starts = jnp.cumsum(per_group, axis=1) - per_group
    load = jnp.sum(per_group, axis=1)
    kept = jnp.minimum(load, capacity)
    spill = load - kept
    free_slots = capacity - kept
    spill_start = jnp.cumsum(spill) - spill
    free_start = jnp.cumsum(free_slots) - free_slots
    position = jnp.arange(capacity, dtype=jnp.int32)
    at_home = position[None, :] < kept[:, None]
    free_rank = free_start[:, None] + position[None, :] - kept[:, None]
    used_spill = jnp.logical_not(at_home) & (free_rank < jnp.sum(spill))
    inside = (spill_start[None, None, :] <= free_rank[:, :, None]) & (free_rank[:, :, None] < (spill_start + spill)[None, None, :])
    source = jnp.sum(inside.astype(jnp.int32) * jnp.arange(GROUPS, dtype=jnp.int32)[None, None, :], axis=2)
    owner_group = jnp.where(at_home, jnp.arange(GROUPS, dtype=jnp.int32)[:, None], source)
    group_rank = jnp.where(at_home, position[None, :], capacity + free_rank - spill_start[source])
    owner_starts = starts[owner_group]
    member = jnp.sum((owner_starts <= group_rank[:, :, None]).astype(jnp.int32), axis=2) - 1
    member = jnp.clip(member, 0, SEQ_GRP - 1)
    sequence = owner_group * SEQ_GRP + member
    slab_number = group_rank - jnp.take_along_axis(owner_starts, member[..., None], axis=2)[..., 0]
    live = at_home | used_spill
    sequence = jnp.where(live, sequence, -1)
    slab_number = jnp.where(live, slab_number, -1)
    perms = jnp.stack([jax.random.permutation(jax.random.fold_in(key_spread, group_id), HOLDERS) for group_id in range(GROUPS)])
    inverse = jnp.argsort(perms, axis=1).astype(jnp.int32)
    spot = jnp.arange(SLOTS, dtype=jnp.int32)[None, None, :] * HOLDERS + inverse[:, :, None]
    spot = spot.reshape(GROUPS, -1)
    table_sequence = jnp.take_along_axis(sequence, spot, axis=1).reshape(GROUPS, HOLDERS, SLOTS)
    table_slab = jnp.take_along_axis(slab_number, spot, axis=1).reshape(GROUPS, HOLDERS, SLOTS)
    return (lengths, table_sequence.astype(jnp.int32), table_slab.astype(jnp.int32))


def draw_context_length(key, part):
    return placement(key)[0]


def draw_slot_sequence(key, part):
    return placement(key)[1]


def draw_slot_slab(key, part):
    return placement(key)[2]


def draw_kv_cache(key, part):
    shape = (GROUPS, HOLDERS, SLOTS, SLAB, LATENT + ROPE)
    key_base = jax.random.fold_in(jax.random.fold_in(key, 11), 0)
    drawn = jnp.clip(1.5 * jax.random.normal(key_base, shape, jnp.float32), -9.0, 9.0)
    return drawn.astype(jnp.bfloat16)


def block_levels(key, shape, shards, smallest, largest):
    gain, own = 1.0, jax.random.fold_in(key, 6)
    for axis_at, blocks in shards:
        heights = jnp.exp(jax.random.uniform(jax.random.fold_in(own, axis_at), (blocks,), jnp.float32, smallest / len(shards), largest / len(shards)))
        gain = gain * jnp.repeat(heights, shape[axis_at] // blocks).reshape([-1 if axis == axis_at else 1 for axis in range(len(shape))])
    return gain


def noise(rng, extent, spread, limit, cuts=(), held_as=jnp.bfloat16):
    result = jax.random.normal(rng, extent, jnp.float32) * spread
    if len(cuts) > 0:
        result = block_levels(rng, extent, cuts, -0.22, 0.18) * result
    return jnp.clip(result, min=-limit, max=limit).astype(held_as)


def setup_inputs(seed: int = 0) -> dict:
    keys = jax.random.split(jax.random.key(seed), 12)
    return {
        "q_compressed": noise(keys[0], (TOKENS, QRANK), 1.0, 6.0, ((0, 4),)),
        "w_q_nope": noise(keys[1], (QRANK, HEADS * NOPE), QRANK ** -0.5, 0.15625, ((1, 8),)),
        "w_q_rope": noise(keys[2], (QRANK, HEADS * ROPE), QRANK ** -0.5, 0.15625, ((1, 8),)),
        "w_uk": noise(keys[3], (HEADS, NOPE, LATENT), NOPE ** -0.5, 0.5, ((0, 8),)),
        "w_uv": noise(keys[4], (HEADS, LATENT, VDIM), LATENT ** -0.5, 0.25, ((0, 8),)),
        "w_o": noise(keys[5], (HEADS * VDIM, D), (HEADS * VDIM) ** -0.5, 0.046875, ((0, 8),)),
        "kv_cache": draw_kv_cache(jax.random.fold_in(keys[11], 71), 0),
        "draft_kv": noise(keys[7], (TOKENS, KV), 3.0, 18.0, ((0, 4),)),
        "context_length": draw_context_length(jax.random.fold_in(keys[11], 71), 0),
        "slot_sequence": draw_slot_sequence(jax.random.fold_in(keys[11], 71), 0),
        "slot_slab": draw_slot_slab(jax.random.fold_in(keys[11], 71), 0),
    }


EMPTY = -1e30


def slot_partial(row_block, slab_keys, valid_count):
    scores = lax.dot_general(row_block, slab_keys, (((1,), (1,)), ((), ())), preferred_element_type=jnp.float32)
    is_valid = jnp.arange(slab_keys.shape[0], dtype=jnp.int32) < valid_count
    masked = jnp.where(is_valid[None, :], scores, EMPTY)
    row_peak = jnp.max(masked, axis=1)
    weights = jnp.where(is_valid[None, :], jnp.exp(masked - row_peak[:, None]), 0.0)
    row_total = jnp.maximum(jnp.sum(weights, axis=1), 1.0)
    mixture = jnp.dot(weights.astype(jnp.bfloat16), slab_keys[:, :LATENT], preferred_element_type=jnp.float32)
    return row_peak + jnp.log(row_total), mixture / row_total[:, None]


def merge_blocks(block_log, block_out, block_owner, own_log, own_out):
    owners_count = own_log.shape[0]
    matches = block_owner[None, :] == jnp.arange(owners_count, dtype=jnp.int32)[:, None]
    picked = jnp.where(matches[:, :, None, None], block_log[None], EMPTY)
    top_log = jnp.maximum(jnp.max(picked, axis=1), own_log)
    weights = jnp.where(matches[:, :, None, None], jnp.exp(picked - top_log[:, None]), 0.0)
    own_weight = jnp.exp(own_log - top_log)
    weight_sum = jnp.sum(weights, axis=1) + own_weight
    summed = jnp.einsum('sbtx,btxl->stxl', weights, block_out, precision=lax.Precision.HIGHEST)
    summed = summed + own_weight[..., None] * own_out
    return top_log + jnp.log(weight_sum), summed / weight_sum[..., None]


def reference(q_compressed, w_q_nope, w_q_rope, w_uk, w_uv, w_o, kv_cache, draft_kv, context_length, slot_sequence, slot_slab):
    token_count = q_compressed.shape[0]
    key_width = LATENT + ROPE
    q_nope = jnp.dot(q_compressed, w_q_nope, preferred_element_type=jnp.float32).astype(jnp.bfloat16)
    q_nope = q_nope.reshape(token_count, HEADS, NOPE)
    q_rope = jnp.dot(q_compressed, w_q_rope, preferred_element_type=jnp.float32).reshape(token_count, HEADS, ROPE)
    absorbed = jnp.einsum('thn,hnl->thl', q_nope.astype(jnp.float32), w_uk.astype(jnp.float32), precision=lax.Precision.HIGHEST)
    queries = (jnp.concatenate([absorbed, q_rope], axis=2) * (NOPE + ROPE) ** -0.5).astype(jnp.bfloat16)
    by_sequence = queries.reshape(SEQS, DRAFT * HEADS, key_width)
    pool_owner = slot_sequence.reshape(-1).astype(jnp.int32)
    pool_number = slot_slab.reshape(-1).astype(jnp.int32)
    slabs_flat = kv_cache.reshape(-1, SLAB, key_width)

    def one_slot(slot_number):
        slot_owner = pool_owner[slot_number]
        chosen = jnp.maximum(slot_owner, 0)
        row_block = lax.dynamic_index_in_dim(by_sequence, chosen, 0, keepdims=False)
        valid_count = jnp.where(slot_owner >= 0, context_length[chosen] - pool_number[slot_number] * SLAB, 0)
        slab_keys = lax.dynamic_index_in_dim(slabs_flat, slot_number, 0, keepdims=False)
        return slot_partial(row_block, slab_keys, valid_count)

    slot_log, slot_out = lax.map(one_slot, jnp.arange(pool_owner.shape[0], dtype=jnp.int32))
    slot_log = slot_log.reshape(-1, DRAFT, HEADS)
    slot_out = slot_out.reshape(-1, DRAFT, HEADS, LATENT)

    draft_rows = queries.reshape(SEQS, DRAFT, HEADS, key_width).astype(jnp.float32)
    draft_keys = draft_kv.reshape(SEQS, DRAFT, key_width).astype(jnp.float32)
    scores = jnp.einsum('sthk,suk->sthu', draft_rows, draft_keys, precision=lax.Precision.HIGHEST)
    causal = jnp.arange(DRAFT)[None, :] <= jnp.arange(DRAFT)[:, None]
    masked = jnp.where(causal[None, :, None, :], scores, EMPTY)
    draft_peak = jnp.max(masked, axis=3)
    weights = jnp.where(causal[None, :, None, :], jnp.exp(masked - draft_peak[..., None]), 0.0)
    draft_total = jnp.sum(weights, axis=3)
    rounded = lax.optimization_barrier(weights.astype(jnp.bfloat16)).astype(jnp.float32)
    mixture = jnp.einsum('sthu,sul->sthl', rounded, draft_keys[..., :LATENT], precision=lax.Precision.HIGHEST)
    draft_log = draft_peak + jnp.log(draft_total)
    draft_out = mixture / draft_total[..., None]

    final_log, final_out = merge_blocks(slot_log, slot_out, pool_owner, draft_log, draft_out)
    attended = final_out.astype(jnp.bfloat16).reshape(token_count, HEADS, LATENT)
    head_values = jnp.einsum('thl,hlv->thv', attended.astype(jnp.float32), w_uv.astype(jnp.float32), precision=lax.Precision.HIGHEST)
    head_values = head_values.astype(jnp.bfloat16).reshape(token_count, HEADS * VDIM)
    return jnp.dot(head_values, w_o, preferred_element_type=jnp.float32)
```

```python
import jax
import jax.numpy as jnp
from jax import lax
from jax.experimental import pallas as pl
from jax.experimental.pallas import tpu as pltpu
from jax.sharding import PartitionSpec as P

NOPE = 128
ROPE = 64
LATENT = 512
VDIM = 128
DRAFT = 4


EMPTY = -1e30


def exchange(axis, call_id, *blocks):
    count = lax.axis_size(axis)
    number = len(blocks)

    def body(*refs):
        sent, got = refs[:number], refs[number : 2 * number]
        send_sems, recv_sems, local_sems = refs[2 * number :]
        me = lax.axis_index(axis)
        barrier = pltpu.get_barrier_semaphore()
        for step in range(1, count):
            pl.semaphore_signal(
                barrier,
                inc=1,
                device_id={axis: lax.rem(me + step, count)},
                device_id_type=pl.DeviceIdType.MESH,
            )
        pl.semaphore_wait(barrier, count - 1)
        started = []
        for step in range(1, count):
            peer = lax.rem(me + step, count)
            for which in range(number):
                copy = pltpu.make_async_remote_copy(
                    src_ref=sent[which].at[peer],
                    dst_ref=got[which].at[me],
                    send_sem=send_sems.at[which, step],
                    recv_sem=recv_sems.at[which, step],
                    device_id={axis: peer},
                    device_id_type=pl.DeviceIdType.MESH,
                )
                copy.start()
                started.append(copy)
        own = []
        for which in range(number):
            copy = pltpu.make_async_copy(
                sent[which].at[me], got[which].at[me], local_sems.at[which]
            )
            copy.start()
            own.append(copy)
        for copy in own:
            copy.wait()
        for copy in started:
            copy.wait()

    vmem = pl.BlockSpec(memory_space=pltpu.VMEM)
    return pl.pallas_call(
        body,
        out_shape=tuple(jax.ShapeDtypeStruct(block.shape, block.dtype) for block in blocks),
        in_specs=[vmem] * number,
        out_specs=tuple([vmem] * number),
        scratch_shapes=[
            pltpu.SemaphoreType.DMA((number, count)),
            pltpu.SemaphoreType.DMA((number, count)),
            pltpu.SemaphoreType.DMA((number,)),
        ],
        compiler_params=pltpu.CompilerParams(
            collective_id=call_id, has_side_effects=True, vmem_limit_bytes=8 * 1024 * 1024
        ),
        name="exchange_%d" % call_id,
    )(*blocks)


def exchange_partials(axis, call_id, block_log, block_mix):
    count = lax.axis_size(axis)
    flat_log = block_log.reshape(count, 1, -1)
    width = flat_log.shape[2]
    padded = -(-width // 128) * 128
    flat_log = jnp.pad(flat_log, ((0, 0), (0, 0), (0, padded - width)))
    flat_mix = block_mix.astype(jnp.bfloat16).reshape(count, -1, block_mix.shape[-1])
    got_log, got_mix = exchange(axis, call_id, flat_log, flat_mix)
    return (
        got_log[:, :, :width].reshape(block_log.shape),
        got_mix.reshape(block_mix.shape).astype(jnp.float32),
    )


def attend_slots(call_id, every_seq, cache_slots, context_length, slot_sequence, slot_slab):
    count = lax.axis_size("dev")
    slot_count, key_width, slab_length = cache_slots.shape
    seq_total, rows, _ = every_seq.shape
    chunk = min(count, max(1, 128 // rows))
    while count % chunk:
        chunk -= 1
    steps = count // chunk
    lanes = -(-rows // 128) * 128
    log_rows = -(-slot_count // 8) * 8

    def body(
        lengths, owners, slabs, every, cache, got_log, got_mix,
        staged, arrived, keys, log_stage, mix_stage,
        key_sems, send_sems, arrive_sems, back_send, back_recv,
    ):
        group = lax.axis_index("group")
        me = lax.axis_index("dev")
        barrier = pltpu.get_barrier_semaphore()

        def greet(step, carry):
            pl.semaphore_signal(
                barrier,
                inc=1,
                device_id={"dev": lax.rem(me + step, count)},
                device_id_type=pl.DeviceIdType.MESH,
            )
            return carry

        lax.fori_loop(1, count, greet, 0)
        for slot in range(slot_count):
            pltpu.make_async_copy(cache.at[slot], keys.at[slot], key_sems.at[slot]).start()
        pl.semaphore_wait(barrier, count - 1)

        def row_copy(peer, source):
            return pltpu.make_async_remote_copy(
                src_ref=staged.at[peer],
                dst_ref=arrived.at[source],
                send_sem=send_sems.at[peer],
                recv_sem=arrive_sems.at[source],
                device_id={"dev": peer},
                device_id_type=pl.DeviceIdType.MESH,
            )

        def back_copies(peer, source):
            return [
                pltpu.make_async_remote_copy(
                    src_ref=stage.at[peer],
                    dst_ref=target.at[source],
                    send_sem=back_send.at[which, peer],
                    recv_sem=back_recv.at[which, source],
                    device_id={"dev": peer},
                    device_id_type=pl.DeviceIdType.MESH,
                )
                for which, (stage, target) in enumerate([(log_stage, got_log), (mix_stage, got_mix)])
            ]

        def send_rows(step, carry):
            peer = lax.rem(me + step, count)
            for slot in range(slot_count):
                owner = jnp.maximum(owners[group, peer, slot], 0)
                staged[peer, slot] = every[owner]
            row_copy(peer, me).start()
            return carry

        lax.fori_loop(1, count, send_rows, 0)
        limits = []
        for slot in range(slot_count):
            owner = owners[group, me, slot]
            arrived[me, slot] = every[jnp.maximum(owner, 0)]
            left = lengths[jnp.maximum(owner, 0)] - slabs[group, me, slot] * slab_length
            limits.append(jnp.where(owner >= 0, left, 0))
        for slot in range(slot_count):
            pltpu.make_async_copy(cache.at[slot], keys.at[slot], key_sems.at[slot]).wait()

        def one_step(step, carry):
            first = lax.rem(me // chunk + steps - step, steps) * chunk
            for at in range(chunk):
                source = first + at

                @pl.when(source != me)
                def _():
                    row_copy(source, source).wait_recv()

            for slot in range(slot_count):
                block = arrived[pl.ds(first, chunk), slot].reshape(chunk * rows, key_width)
                scores = lax.dot_general(
                    block, keys[slot], (((1,), (0,)), ((), ())), preferred_element_type=jnp.float32
                )
                place = lax.broadcasted_iota(jnp.int32, (1, slab_length), 1)
                is_valid = place < limits[slot]
                masked = jnp.where(is_valid, scores, EMPTY)
                peak = jnp.max(masked, axis=1, keepdims=True)
                weights = jnp.where(is_valid, jnp.exp(masked - peak), 0.0)
                total = jnp.maximum(jnp.sum(weights, axis=1, keepdims=True), 1.0)
                mixture = lax.dot_general(
                    weights.astype(jnp.bfloat16),
                    keys[slot, :LATENT],
                    (((1,), (1,)), ((), ())),
                    preferred_element_type=jnp.float32,
                )
                log = jnp.broadcast_to(peak + jnp.log(total), (chunk * rows, 128))
                mix = (mixture / total).astype(jnp.bfloat16).reshape(chunk, rows, LATENT)
                for at in range(chunk):
                    mix_stage[first + at, slot] = mix[at]
                    turned = jnp.transpose(log[at * rows : (at + 1) * rows])
                    log_stage[first + at, slot : slot + 1, :rows] = turned[:1]
            for at in range(chunk):
                source = first + at

                @pl.when(source != me)
                def _():
                    for copy in back_copies(source, me):
                        copy.start()

            return carry

        lax.fori_loop(0, steps, one_step, 0)
        got_log[me] = log_stage[me]
        got_mix[me] = mix_stage[me]

        def finish(step, carry):
            peer = lax.rem(me + step, count)
            row_copy(peer, peer).wait_send()
            for copy in back_copies(peer, peer):
                copy.wait_send()
                copy.wait_recv()
            return carry

        lax.fori_loop(1, count, finish, 0)

    smem = pl.BlockSpec(memory_space=pltpu.SMEM)
    vmem = pl.BlockSpec(memory_space=pltpu.VMEM)
    log_shape = (count, log_rows, lanes)
    mix_shape = (count, slot_count, rows, LATENT)
    got_log, got_mix = pl.pallas_call(
        body,
        out_shape=(
            jax.ShapeDtypeStruct(log_shape, jnp.float32),
            jax.ShapeDtypeStruct(mix_shape, jnp.bfloat16),
        ),
        in_specs=[smem, smem, smem, vmem, pl.BlockSpec(memory_space=pl.ANY)],
        out_specs=(vmem, vmem),
        scratch_shapes=[
            pltpu.VMEM((count, slot_count, rows, key_width), jnp.bfloat16),
            pltpu.VMEM((count, slot_count, rows, key_width), jnp.bfloat16),
            pltpu.VMEM((slot_count, key_width, slab_length), jnp.bfloat16),
            pltpu.VMEM(log_shape, jnp.float32),
            pltpu.VMEM(mix_shape, jnp.bfloat16),
            pltpu.SemaphoreType.DMA((slot_count,)),
            pltpu.SemaphoreType.DMA((count,)),
            pltpu.SemaphoreType.DMA((count,)),
            pltpu.SemaphoreType.DMA((2, count)),
            pltpu.SemaphoreType.DMA((2, count)),
        ],
        compiler_params=pltpu.CompilerParams(
            collective_id=call_id, has_side_effects=True, vmem_limit_bytes=24 * 1024 * 1024
        ),
        name="attend_slots",
    )(
        context_length,
        slot_sequence,
        slot_slab,
        every_seq,
        cache_slots,
    )
    return got_log[:, :slot_count, :rows], got_mix.astype(jnp.float32)


def merge_blocks(block_log, block_out, block_owner, own_log, own_out):
    owners_count = own_log.shape[0]
    matches = block_owner[None, :] == jnp.arange(owners_count, dtype=jnp.int32)[:, None]
    picked = jnp.where(matches[:, :, None, None], block_log[None], EMPTY)
    top_log = jnp.maximum(jnp.max(picked, axis=1), own_log)
    weights = jnp.where(matches[:, :, None, None], jnp.exp(picked - top_log[:, None]), 0.0)
    own_weight = jnp.exp(own_log - top_log)
    weight_sum = jnp.sum(weights, axis=1) + own_weight
    summed = jnp.einsum("sbtx,btxl->stxl", weights, block_out, precision=lax.Precision.HIGHEST)
    summed = summed + own_weight[..., None] * own_out
    return (top_log + jnp.log(weight_sum), summed / weight_sum[..., None])


def draft_partials(queries_seq, draft_rows):
    scores = jnp.einsum(
        "sthk,suk->sthu", queries_seq, draft_rows, preferred_element_type=jnp.float32
    )
    causal = jnp.arange(DRAFT)[None, :] <= jnp.arange(DRAFT)[:, None]
    masked = jnp.where(causal[None, :, None, :], scores, EMPTY)
    draft_peak = jnp.max(masked, axis=3)
    weights = jnp.where(causal[None, :, None, :], jnp.exp(masked - draft_peak[..., None]), 0.0)
    draft_total = jnp.sum(weights, axis=3)
    mixture = jnp.einsum(
        "sthu,sul->sthl",
        weights.astype(jnp.bfloat16),
        draft_rows[..., :LATENT],
        preferred_element_type=jnp.float32,
    )
    return (draft_peak + jnp.log(draft_total), mixture / draft_total[..., None])


def shards_general(
    q_compressed,
    w_q_nope,
    w_q_rope,
    w_uk,
    w_uv,
    w_o,
    kv_cache,
    draft_kv,
    context_length,
    slot_sequence,
    slot_slab,
):
    group_count = lax.axis_size("group")
    holder_count = lax.axis_size("dev")
    group_index = lax.axis_index("group")
    token_count = q_compressed.shape[0]
    seq_group = token_count // DRAFT
    heads_here = w_uk.shape[0]
    key_width = LATENT + ROPE
    q_nope = jnp.dot(q_compressed, w_q_nope, preferred_element_type=jnp.float32).astype(
        jnp.bfloat16
    )
    q_nope = q_nope.reshape(token_count, heads_here, NOPE)
    q_rope = jnp.dot(q_compressed, w_q_rope, preferred_element_type=jnp.float32).reshape(
        token_count, heads_here, ROPE
    )
    absorbed = jnp.einsum("thn,hnl->thl", q_nope, w_uk, preferred_element_type=jnp.float32)
    queries = (jnp.concatenate([absorbed, q_rope], axis=2) * (NOPE + ROPE) ** (-0.5)).astype(
        jnp.bfloat16
    )
    queries_seq = queries.reshape(seq_group, DRAFT, heads_here, key_width)
    draft_log, draft_mix = draft_partials(
        queries_seq, draft_kv.reshape(seq_group, DRAFT, key_width)
    )
    group_table = lax.dynamic_index_in_dim(slot_sequence, group_index, 0, keepdims=False)
    outgoing = jnp.broadcast_to(
        queries_seq.reshape(1, -1, key_width), (group_count, token_count * heads_here, key_width)
    )
    (gathered,) = exchange("group", 0, outgoing)
    back_log, back_mix = attend_slots(
        1,
        gathered.reshape(group_count * seq_group, DRAFT * heads_here, key_width),
        jnp.swapaxes(kv_cache[0, 0], 1, 2),
        context_length,
        slot_sequence,
        slot_slab,
    )
    seq_total = group_count * seq_group
    group_log, group_mix = merge_blocks(
        back_log.reshape(-1, DRAFT, heads_here),
        back_mix.reshape(-1, DRAFT, heads_here, LATENT),
        group_table.reshape(-1),
        jnp.full((seq_total, DRAFT, heads_here), EMPTY, jnp.float32),
        jnp.zeros((seq_total, DRAFT, heads_here, LATENT), jnp.float32),
    )
    home_log, home_mix = exchange_partials(
        "group",
        3,
        group_log.reshape(group_count, seq_group, DRAFT, heads_here),
        group_mix.reshape(group_count, seq_group, DRAFT, heads_here, LATENT),
    )
    home_owner = jnp.tile(jnp.arange(seq_group, dtype=jnp.int32), group_count)
    final_log, final_mix = merge_blocks(
        home_log.reshape(-1, DRAFT, heads_here),
        home_mix.reshape(-1, DRAFT, heads_here, LATENT),
        home_owner,
        draft_log,
        draft_mix,
    )
    attended = final_mix.astype(jnp.bfloat16).reshape(token_count, heads_here, LATENT)
    head_values = jnp.einsum("thl,hlv->thv", attended, w_uv, preferred_element_type=jnp.float32)
    head_values = head_values.astype(jnp.bfloat16).reshape(token_count, heads_here * VDIM)
    partial = jnp.dot(head_values, w_o, preferred_element_type=jnp.float32)
    (terms,) = exchange(
        "dev", 4, partial.reshape(holder_count, token_count // holder_count, -1)
    )
    return jnp.sum(terms, axis=0)


PHASES = {2: ((0, 1),), 4: ((0, 1), (2, 3))}
CHUNKS = 4


def flip(value, mask, extent):
    result, bit = 0, 1
    while bit < extent:
        own = lax.rem(lax.div(value, bit), 2)
        result = result + bit * (1 - own if mask & bit else own)
        bit *= 2
    return result


def fused(
    q_compressed, w_q_nope, w_q_rope, w_uk, w_uv, w_o, keys_hbm, draft_kv,
    context_length, slot_sequence, slot_slab,
):
    groups, count = lax.axis_size("group"), lax.axis_size("dev")
    planes = count // 2
    around = groups * 2
    phases = PHASES[planes]
    home_tokens, q_rank = q_compressed.shape
    tokens = groups * home_tokens
    seqs = tokens // DRAFT
    heads = w_uk.shape[0] // groups
    unit = heads * DRAFT
    rows = seqs * unit
    slots, key_width, slab_length = keys_hbm.shape
    width = w_o.shape[1]
    nope_cols, rope_cols, out_rows = heads * NOPE, heads * ROPE, heads * VDIM
    cut = width // CHUNKS
    bf16, f32 = jnp.bfloat16, jnp.float32
    number = len(phases)

    def body(
        lengths, owners, slabs, qc, dkv, wqn_hbm, wqr_hbm, wuk_hbm, wuv_hbm, wo_hbm, cache, out,
        qall, dall, wqn, wqr, wuk, wuv, wo, keys, *rest,
    ):
        rest = list(rest)
        take = lambda n: [rest.pop(0) for _ in range(n)]
        zb = take(planes)
        staged = take(planes)
        arrived, mixs, mixg, logs, logg = (take(number) for _ in range(5))
        zms, zmg, zls, zlg = (take(planes) for _ in range(4))
        parts, partg, fin, fing = take(4)
        (
            local, g_send, g_recv, z_send, z_recv, p_send, p_recv, b_send, b_recv,
            y_send, y_recv, r_send, r_recv, f_send, f_recv,
        ) = rest
        g = lax.axis_index("group")
        d = lax.axis_index("dev")
        z, c = lax.div(d, 2), lax.rem(d, 2)
        me = g * 2 + c

        def remote(src, dst, send, recv, to_g, to_d):
            return pltpu.make_async_remote_copy(
                src_ref=src, dst_ref=dst, send_sem=send, recv_sem=recv,
                device_id=(to_g, to_d), device_id_type=pl.DeviceIdType.MESH,
            )

        def plane_peer(step):
            return lax.rem(me + step, around)

        def plane_device(j):
            return lax.div(j, 2), z * 2 + lax.rem(j, 2)

        columns = lambda size: pl.ds(pl.multiple_of(g * size, size), size)
        loads = [
            pltpu.make_async_copy(wqn_hbm.at[:, columns(nope_cols)], wqn, local.at[0]),
            pltpu.make_async_copy(wqr_hbm.at[:, columns(rope_cols)], wqr, local.at[1]),
            pltpu.make_async_copy(wuk_hbm.at[pl.ds(g * heads, heads)], wuk, local.at[2]),
            pltpu.make_async_copy(cache, keys, local.at[3]),
            pltpu.make_async_copy(wuv_hbm.at[pl.ds(g * heads, heads)], wuv, local.at[4]),
            pltpu.make_async_copy(wo_hbm.at[columns(out_rows)], wo, local.at[5]),
        ]
        for copy in loads:
            copy.start()

        barrier = pltpu.get_barrier_semaphore()

        def greet(to_g, to_d):
            pl.semaphore_signal(
                barrier, inc=1, device_id=(to_g, to_d), device_id_type=pl.DeviceIdType.MESH
            )

        for step in range(1, around):
            greet(*plane_device(plane_peer(step)))
        for step in range(1, planes):
            for core in range(2):
                greet(g, lax.rem(z + step, planes) * 2 + core)
        pl.semaphore_wait(barrier, around - 1 + 2 * (planes - 1))

        def group_copies(step):
            to = lax.rem(g + step, groups)
            return [
                remote(qc, qall.at[g], g_send.at[0, step], g_recv.at[0, step], to, d),
                remote(dkv, dall.at[g], g_send.at[1, step], g_recv.at[1, step], to, d),
            ]

        for step in range(1, groups):
            for copy in group_copies(step):
                copy.start()
        qall[g] = qc[...]
        dall[g] = dkv[...]
        for step in range(1, groups):
            for copy in group_copies(step):
                copy.wait()

        def joined(ref):
            pieces = [ref[i].astype(f32) for i in range(groups)]
            return jnp.concatenate(pieces, axis=0).astype(bf16)

        q_tokens = joined(qall)
        draft = joined(dall)
        for copy in loads[:3]:
            copy.wait()
        nope = jnp.dot(q_tokens, wqn[...], preferred_element_type=f32).astype(bf16)
        rope = jnp.dot(q_tokens, wqr[...], preferred_element_type=f32)
        by_head = []
        for h in range(heads):
            absorbed = jnp.dot(
                nope[:, h * NOPE : (h + 1) * NOPE], wuk[h], preferred_element_type=f32
            )
            pair = jnp.concatenate([absorbed, rope[:, h * ROPE : (h + 1) * ROPE]], axis=1)
            by_head.append((pair * (NOPE + ROPE) ** (-0.5)).astype(bf16))
        stacked = jnp.concatenate(by_head, axis=0)
        row = lax.broadcasted_iota(jnp.int32, (rows, rows), 0)
        col = lax.broadcasted_iota(jnp.int32, (rows, rows), 1)
        spot = lax.rem(lax.div(row, DRAFT), heads) * tokens
        spot = spot + lax.div(row, unit) * DRAFT + lax.rem(row, DRAFT)
        order = jnp.where(col == spot, 1.0, 0.0).astype(bf16)
        queries = jnp.dot(order, stacked, preferred_element_type=f32).astype(bf16)
        zb[0][...] = queries.reshape(seqs, unit, key_width)

        def z_copy(s):
            relay = s & 1 and s > 1
            source, over = (zb[s ^ 1], 1) if relay else (zb[0], s)
            return remote(
                source, zb[s], z_send.at[s], z_recv.at[s], g, flip(z, over, planes) * 2 + c
            )

        for s in range(1, planes):
            if not (s & 1 and s > 1):
                z_copy(s).start()

        place = [(p, phases[p].index(s)) for s in range(planes) for p in range(number) if s in phases[p]]

        def p_copy(s, to):
            p, at = place[s]
            return remote(
                staged[s].at[to], arrived[p].at[me, :, at], p_send.at[s, to], p_recv.at[s, me],
                *plane_device(to),
            )

        def p_arrival(s, source):
            p, at = place[s]
            return remote(
                staged[s].at[source], arrived[p].at[source, :, at], p_send.at[s, source],
                p_recv.at[s, source], *plane_device(source),
            )

        def dispatch(s):
            p, at = place[s]
            if s > 0:
                z_copy(s).wait_recv()
                if s % 2 == 0 and s + 1 < planes:
                    z_copy(s + 1).start()

            def fill(step, carry):
                to = plane_peer(step)
                to_g, to_d = plane_device(to)
                for k in range(slots):
                    staged[s][to, k] = zb[s][jnp.maximum(owners[to_g, to_d, k], 0)]
                return carry

            def send(step, carry):
                p_copy(s, plane_peer(step)).start()
                return carry

            lax.fori_loop(1, around, fill, 0)
            lax.fori_loop(1, around, send, 0)
            for k in range(slots):
                arrived[p][me, k, at] = zb[s][jnp.maximum(owners[g, d, k], 0)]

        def b_copies(p, k, to, source):
            return [
                remote(
                    mixs[p].at[k, to], mixg[p].at[source, k], b_send.at[p, 0, k, to],
                    b_recv.at[p, 0, k, source], *plane_device(to),
                ),
                remote(
                    logs[p].at[k, to], logg[p].at[source, k], b_send.at[p, 1, k, to],
                    b_recv.at[p, 1, k, source], *plane_device(to),
                ),
            ]

        def await_rows(p):
            for s in phases[p]:

                def one(step, carry):
                    p_arrival(s, plane_peer(step)).wait_recv()
                    return carry

                lax.fori_loop(1, around, one, 0)

        def attend(p, k):
            some = len(phases[p])
            per = some * unit
            total_rows = around * per
            owner = owners[g, d, k]
            left = lengths[jnp.maximum(owner, 0)] - slabs[g, d, k] * slab_length
            limit = jnp.where(owner >= 0, left, 0)
            block = arrived[p][:, k].reshape(total_rows, key_width)
            scores = lax.dot_general(
                block, keys[k], (((1,), (0,)), ((), ())), preferred_element_type=f32
            )
            position = lax.broadcasted_iota(jnp.int32, (1, slab_length), 1)
            is_valid = position < limit
            masked = jnp.where(is_valid, scores, EMPTY)
            peak = jnp.max(masked, axis=1, keepdims=True)
            weights = jnp.where(is_valid, jnp.exp(masked - peak), 0.0)
            total = jnp.maximum(jnp.sum(weights, axis=1, keepdims=True), 1.0)
            mixture = lax.dot_general(
                weights.astype(bf16), keys[k, :LATENT], (((1,), (1,)), ((), ())),
                preferred_element_type=f32,
            )
            mixs[p][k] = (mixture / total).astype(bf16).reshape(around, some, unit, LATENT)
            log = jnp.broadcast_to(peak + jnp.log(total), (total_rows, 128))
            log = jnp.transpose(log)[:1]
            for j in range(around):
                logs[p][k, j, :, :per] = log[:, j * per : (j + 1) * per]

            def send(step, carry):
                for copy in b_copies(p, k, plane_peer(step), me):
                    copy.start()
                return carry

            lax.fori_loop(1, around, send, 0)
            mixg[p][me, k] = mixs[p][k, me]
            logg[p][me, k] = logs[p][k, me]

        def split_dot(weights, block):
            high = weights.astype(bf16)
            low = (weights - high.astype(f32)).astype(bf16)
            return jnp.dot(high, block, preferred_element_type=f32) + jnp.dot(
                low, block, preferred_element_type=f32
            )

        def y_copy(s):
            to = flip(z, s, planes) * 2 + c
            return [
                remote(zms[s], zmg[s], y_send.at[0, s], y_recv.at[0, s], g, to),
                remote(zls[s], zlg[s], y_send.at[1, s], y_recv.at[1, s], g, to),
            ]

        def merge_plane(p):
            some = len(phases[p])
            per = some * unit
            blocks = around * slots

            def one(step, carry):
                source = plane_peer(step)
                for k in range(slots):
                    for copy in b_copies(p, k, source, source):
                        copy.wait_recv()
                return carry

            lax.fori_loop(1, around, one, 0)
            wide = blocks * per
            cells = [logg[p][j, k, :, :per] for j in range(around) for k in range(slots)]
            log = jnp.concatenate(cells, axis=1)
            lane = lax.broadcasted_iota(jnp.int32, (1, wide), 1)
            owner = jnp.full((1, wide), -1, jnp.int32)
            for j in range(around):
                for k in range(slots):
                    here = owners[j // 2, z * 2 + j % 2, k]
                    owner = jnp.where(lax.div(lane, per) == j * slots + k, here, owner)
            tag = owner * per + lax.rem(lane, per)
            height = some * rows
            line = lax.broadcasted_iota(jnp.int32, (height, 1), 0)
            inner = lax.div(line, rows) * unit + lax.rem(line, unit)
            mark = lax.rem(lax.div(line, unit), seqs) * per + inner
            match = tag == mark
            picked = jnp.where(match, log, EMPTY)
            top = jnp.max(picked, axis=1, keepdims=True)
            weights = jnp.where(match, jnp.exp(picked - top), 0.0)
            total = jnp.maximum(jnp.sum(weights, axis=1, keepdims=True), 1.0)
            block = mixg[p][...].reshape(wide, LATENT)
            mixed = (split_dot(weights, block) / total).astype(bf16)
            logged = jnp.broadcast_to(top + jnp.log(total), (height, 128))
            logged = jnp.transpose(logged)[:1]
            for at, s in enumerate(phases[p]):
                mix_to, log_to = (zms[s], zls[s]) if s > 0 else (zmg[s], zlg[s])
                mix_to[...] = mixed[at * rows : (at + 1) * rows]
                log_to[...] = logged[:, at * rows : (at + 1) * rows]
            for s in phases[p]:
                if s > 0:
                    for copy in y_copy(s):
                        copy.start()

        def attend_slot(p):
            def one(k, carry):
                attend(p, k)
                return carry

            return one

        for s in phases[0]:
            dispatch(s)

        scores = lax.dot_general(
            queries, draft, (((1,), (1,)), ((), ())), preferred_element_type=f32
        )
        row = lax.broadcasted_iota(jnp.int32, (rows, tokens), 0)
        col = lax.broadcasted_iota(jnp.int32, (rows, tokens), 1)
        seen = (lax.div(row, unit) == lax.div(col, DRAFT)) & (
            lax.rem(col, DRAFT) <= lax.rem(row, DRAFT)
        )
        masked = jnp.where(seen, scores, EMPTY)
        draft_peak = jnp.max(masked, axis=1, keepdims=True)
        weights = jnp.where(seen, jnp.exp(masked - draft_peak), 0.0)
        draft_total = jnp.sum(weights, axis=1, keepdims=True)
        draft_mix = jnp.dot(weights.astype(bf16), draft[:, :LATENT], preferred_element_type=f32)
        draft_mix = draft_mix / draft_total
        draft_log = draft_peak + jnp.log(draft_total)

        loads[3].wait()
        await_rows(0)
        if number == 1:
            lax.fori_loop(0, slots, attend_slot(0), 0)
        else:
            attend(0, 0)
            for s in phases[1]:
                dispatch(s)
            lax.fori_loop(1, slots, attend_slot(0), 0)
            await_rows(1)
            attend(1, 0)
            merge_plane(0)
            lax.fori_loop(1, slots, attend_slot(1), 0)
        merge_plane(number - 1)

        for s in range(1, planes):
            for copy in y_copy(s):
                copy.wait_recv()
        wide = planes * rows
        log = jnp.concatenate([zlg[s][...] for s in range(planes)], axis=1)
        lane = lax.broadcasted_iota(jnp.int32, (1, wide), 1)
        line = lax.broadcasted_iota(jnp.int32, (rows, 1), 0)
        match = lax.rem(lane, rows) == line
        picked = jnp.where(match, log, EMPTY)
        top = jnp.maximum(jnp.max(picked, axis=1, keepdims=True), draft_log)
        weights = jnp.where(match, jnp.exp(picked - top), 0.0)
        own = jnp.exp(draft_log - top)
        total = jnp.sum(weights, axis=1, keepdims=True) + own
        block = jnp.concatenate([zmg[s][...] for s in range(planes)], axis=0)
        summed = split_dot(weights, block) + own * draft_mix
        attended = (summed / total).astype(bf16)
        row = lax.broadcasted_iota(jnp.int32, (rows, rows), 0)
        col = lax.broadcasted_iota(jnp.int32, (rows, rows), 1)
        token = lax.rem(row, tokens)
        spot = lax.div(token, DRAFT) * unit + lax.div(row, tokens) * DRAFT + lax.rem(token, DRAFT)
        order = jnp.where(col == spot, 1.0, 0.0).astype(bf16)
        attended = jnp.dot(order, attended, preferred_element_type=f32).astype(bf16)
        loads[4].wait()
        loads[5].wait()
        values = [
            jnp.dot(attended[h * tokens : (h + 1) * tokens], wuv[h], preferred_element_type=f32)
            for h in range(heads)
        ]
        values = jnp.concatenate(values, axis=1).astype(bf16)

        def r_copy(n, step):
            to = lax.rem(g + step, groups)
            return remote(
                parts.at[n, to], partg.at[n, g], r_send.at[n, step], r_recv.at[n, step], to, d
            )

        def project(n, carry):
            span = pl.ds(pl.multiple_of(n * cut, 128), cut)
            part = jnp.dot(values, wo[:, span], preferred_element_type=f32)
            for i in range(groups):
                parts[n, i] = part[i * home_tokens : (i + 1) * home_tokens].astype(bf16)
            for step in range(1, groups):
                r_copy(n, step).start()
            partg[n, g] = parts[n, g]
            return carry

        lax.fori_loop(0, CHUNKS, project, 0)

        def f_copy(n, to, source):
            return remote(
                fin.at[n, to], fing.at[n, source], f_send.at[n, to], f_recv.at[n, source], g, to
            )

        own_tokens = home_tokens // count

        def gather(n, carry):
            for step in range(1, groups):
                r_copy(n, step).wait_recv()
            summed = partg[n, 0].astype(f32)
            for i in range(1, groups):
                summed = summed + partg[n, i].astype(f32)
            for t in range(count):
                fin[n, t] = summed[t * own_tokens : (t + 1) * own_tokens]

            def send(step, carry):
                f_copy(n, lax.rem(d + step, count), d).start()
                return carry

            lax.fori_loop(1, count, send, 0)
            fing[n, d] = fin[n, d]
            return carry

        lax.fori_loop(0, CHUNKS, gather, 0)

        for n in range(CHUNKS):

            def one(step, carry):
                source = lax.rem(d + step, count)
                f_copy(n, source, source).wait_recv()
                return carry

            lax.fori_loop(1, count, one, 0)
            summed = fing[n, 0]
            for t in range(1, count):
                summed = summed + fing[n, t]
            out[:, n * cut : (n + 1) * cut] = summed

        for s in range(1, planes):
            z_copy(s).wait_send()
            for copy in y_copy(s):
                copy.wait_send()

        def finish(step, carry):
            to = plane_peer(step)
            for s in range(planes):
                p_copy(s, to).wait_send()
            for p in range(number):
                for k in range(slots):
                    for copy in b_copies(p, k, to, me):
                        copy.wait_send()
            return carry

        lax.fori_loop(1, around, finish, 0)

        def finish_chunk(n, carry):
            for step in range(1, groups):
                r_copy(n, step).wait_send()
            for step in range(1, count):
                f_copy(n, lax.rem(d + step, count), d).wait_send()
            return carry

        lax.fori_loop(0, CHUNKS, finish_chunk, 0)

    smem = pl.BlockSpec(memory_space=pltpu.SMEM)
    vmem = pl.BlockSpec(memory_space=pltpu.VMEM)
    hbm = pl.BlockSpec(memory_space=pl.ANY)
    own_tokens = home_tokens // count
    scratch = [
        pltpu.VMEM((groups, home_tokens, q_rank), bf16),
        pltpu.VMEM((groups, home_tokens, key_width), bf16),
        pltpu.VMEM((q_rank, nope_cols), bf16),
        pltpu.VMEM((q_rank, rope_cols), bf16),
        pltpu.VMEM((heads, NOPE, LATENT), bf16),
        pltpu.VMEM((heads, LATENT, VDIM), bf16),
        pltpu.VMEM((out_rows, width), bf16),
        pltpu.VMEM((slots, key_width, slab_length), bf16),
    ]
    scratch += [pltpu.VMEM((seqs, unit, key_width), bf16) for _ in range(planes)]
    scratch += [pltpu.VMEM((around, slots, unit, key_width), bf16) for _ in range(planes)]
    sizes = [len(phase) for phase in phases]
    scratch += [pltpu.VMEM((around, slots, n, unit, key_width), bf16) for n in sizes]
    scratch += [pltpu.VMEM((slots, around, n, unit, LATENT), bf16) for n in sizes]
    scratch += [pltpu.VMEM((around, slots, n, unit, LATENT), bf16) for n in sizes]
    lanes = [-(-n * unit // 128) * 128 for n in sizes]
    scratch += [pltpu.VMEM((slots, around, 1, n), f32) for n in lanes]
    scratch += [pltpu.VMEM((around, slots, 1, n), f32) for n in lanes]
    scratch += [pltpu.VMEM((rows, LATENT), bf16) for _ in range(2 * planes)]
    scratch += [pltpu.VMEM((1, rows), f32) for _ in range(2 * planes)]
    scratch += [pltpu.VMEM((CHUNKS, groups, home_tokens, cut), bf16) for _ in range(2)]
    scratch += [pltpu.VMEM((CHUNKS, count, own_tokens, cut), f32) for _ in range(2)]
    dma = pltpu.SemaphoreType.DMA
    scratch += [
        dma((6,)),
        dma((2, groups)), dma((2, groups)),
        dma((planes,)), dma((planes,)),
        dma((planes, around)), dma((planes, around)),
        dma((number, 2, slots, around)), dma((number, 2, slots, around)),
        dma((2, planes)), dma((2, planes)),
        dma((CHUNKS, groups)), dma((CHUNKS, groups)),
        dma((CHUNKS, count)), dma((CHUNKS, count)),
    ]
    return pl.pallas_call(
        body,
        out_shape=jax.ShapeDtypeStruct((own_tokens, width), f32),
        in_specs=[smem] * 3 + [vmem] * 2 + [hbm] * 6,
        out_specs=vmem,
        scratch_shapes=scratch,
        compiler_params=pltpu.CompilerParams(
            collective_id=0, has_side_effects=True, vmem_limit_bytes=56 * 1024 * 1024
        ),
        name="fused",
    )(
        context_length, slot_sequence, slot_slab, q_compressed, draft_kv,
        w_q_nope, w_q_rope, w_uk, w_uv, w_o, keys_hbm,
    )


def shards(
    q_compressed, w_q_nope, w_q_rope, w_uk, w_uv, w_o, kv_cache, draft_kv,
    context_length, slot_sequence, slot_slab,
):
    args = (
        q_compressed, w_q_nope, w_q_rope, w_uk, w_uv, w_o, kv_cache, draft_kv,
        context_length, slot_sequence, slot_slab,
    )
    groups, count = lax.axis_size("group"), lax.axis_size("dev")
    heads = w_uk.shape[0] // groups
    fits = (
        w_uk.shape[0] % groups == 0
        and heads * DRAFT % 16 == 0
        and count % 2 == 0
        and count // 2 in PHASES
        and q_compressed.shape[0] % count == 0
        and w_o.shape[1] % (128 * CHUNKS) == 0
    )
    if not fits:
        return shards_general(*args)
    keys = jnp.swapaxes(kv_cache[0, 0], 1, 2)
    return fused(
        q_compressed, w_q_nope, w_q_rope, w_uk, w_uv, w_o, keys, draft_kv,
        context_length, slot_sequence, slot_slab,
    )


def solution(mesh):
    placed = (
        P("group", None),
        P(None, "dev"),
        P(None, "dev"),
        P("dev", None, None),
        P("dev", None, None),
        P("dev", None),
        P("group", "dev", None, None, None),
        P("group", None),
        P(),
        P(),
        P(),
    )
    return jax.shard_map(
        shards, mesh=mesh, in_specs=placed, out_specs=P(("group", "dev"), None), check_vma=False
    )
```

```python
import jax
import jax.numpy as jnp
from jax import lax
from jax.experimental import pallas as pl
from jax.experimental.pallas import tpu as pltpu
from jax.sharding import PartitionSpec as P

NOPE = 128
ROPE = 64
LATENT = 512
VDIM = 128
DRAFT = 4


EMPTY = -1e30


def exchange(axis, call_id, *blocks):
    count = lax.axis_size(axis)
    number = len(blocks)

    def body(*refs):
        sent, got = refs[:number], refs[number : 2 * number]
        send_sems, recv_sems, local_sems = refs[2 * number :]
        me = lax.axis_index(axis)
        barrier = pltpu.get_barrier_semaphore()
        for step in range(1, count):
            pl.semaphore_signal(
                barrier,
                inc=1,
                device_id={axis: lax.rem(me + step, count)},
                device_id_type=pl.DeviceIdType.MESH,
            )
        pl.semaphore_wait(barrier, count - 1)
        started = []
        for step in range(1, count):
            peer = lax.rem(me + step, count)
            for which in range(number):
                copy = pltpu.make_async_remote_copy(
                    src_ref=sent[which].at[peer],
                    dst_ref=got[which].at[me],
                    send_sem=send_sems.at[which, step],
                    recv_sem=recv_sems.at[which, step],
                    device_id={axis: peer},
                    device_id_type=pl.DeviceIdType.MESH,
                )
                copy.start()
                started.append(copy)
        own = []
        for which in range(number):
            copy = pltpu.make_async_copy(
                sent[which].at[me], got[which].at[me], local_sems.at[which]
            )
            copy.start()
            own.append(copy)
        for copy in own:
            copy.wait()
        for copy in started:
            copy.wait()

    vmem = pl.BlockSpec(memory_space=pltpu.VMEM)
    return pl.pallas_call(
        body,
        out_shape=tuple(jax.ShapeDtypeStruct(block.shape, block.dtype) for block in blocks),
        in_specs=[vmem] * number,
        out_specs=tuple([vmem] * number),
        scratch_shapes=[
            pltpu.SemaphoreType.DMA((number, count)),
            pltpu.SemaphoreType.DMA((number, count)),
            pltpu.SemaphoreType.DMA((number,)),
        ],
        compiler_params=pltpu.CompilerParams(
            collective_id=call_id, has_side_effects=True, vmem_limit_bytes=8 * 1024 * 1024
        ),
        name="exchange_%d" % call_id,
    )(*blocks)


def exchange_partials(axis, call_id, block_log, block_mix):
    count = lax.axis_size(axis)
    flat_log = block_log.reshape(count, 1, -1)
    width = flat_log.shape[2]
    padded = -(-width // 128) * 128
    flat_log = jnp.pad(flat_log, ((0, 0), (0, 0), (0, padded - width)))
    flat_mix = block_mix.astype(jnp.bfloat16).reshape(count, -1, block_mix.shape[-1])
    got_log, got_mix = exchange(axis, call_id, flat_log, flat_mix)
    return (
        got_log[:, :, :width].reshape(block_log.shape),
        got_mix.reshape(block_mix.shape).astype(jnp.float32),
    )


def attend_slots(call_id, every_seq, cache_slots, context_length, slot_sequence, slot_slab):
    count = lax.axis_size("dev")
    slot_count, key_width, slab_length = cache_slots.shape
    seq_total, rows, _ = every_seq.shape
    chunk = min(count, max(1, 128 // rows))
    while count % chunk:
        chunk -= 1
    steps = count // chunk
    lanes = -(-rows // 128) * 128
    log_rows = -(-slot_count // 8) * 8

    def body(
        lengths, owners, slabs, every, cache, got_log, got_mix,
        staged, arrived, keys, log_stage, mix_stage,
        key_sems, send_sems, arrive_sems, back_send, back_recv,
    ):
        group = lax.axis_index("group")
        me = lax.axis_index("dev")
        barrier = pltpu.get_barrier_semaphore()

        def greet(step, carry):
            pl.semaphore_signal(
                barrier,
                inc=1,
                device_id={"dev": lax.rem(me + step, count)},
                device_id_type=pl.DeviceIdType.MESH,
            )
            return carry

        lax.fori_loop(1, count, greet, 0)
        for slot in range(slot_count):
            pltpu.make_async_copy(cache.at[slot], keys.at[slot], key_sems.at[slot]).start()
        pl.semaphore_wait(barrier, count - 1)

        def row_copy(peer, source):
            return pltpu.make_async_remote_copy(
                src_ref=staged.at[peer],
                dst_ref=arrived.at[source],
                send_sem=send_sems.at[peer],
                recv_sem=arrive_sems.at[source],
                device_id={"dev": peer},
                device_id_type=pl.DeviceIdType.MESH,
            )

        def back_copies(peer, source):
            return [
                pltpu.make_async_remote_copy(
                    src_ref=stage.at[peer],
                    dst_ref=target.at[source],
                    send_sem=back_send.at[which, peer],
                    recv_sem=back_recv.at[which, source],
                    device_id={"dev": peer},
                    device_id_type=pl.DeviceIdType.MESH,
                )
                for which, (stage, target) in enumerate([(log_stage, got_log), (mix_stage, got_mix)])
            ]

        def send_rows(step, carry):
            peer = lax.rem(me + step, count)
            for slot in range(slot_count):
                owner = jnp.maximum(owners[group, peer, slot], 0)
                staged[peer, slot] = every[owner]
            row_copy(peer, me).start()
            return carry

        lax.fori_loop(1, count, send_rows, 0)
        limits = []
        for slot in range(slot_count):
            owner = owners[group, me, slot]
            arrived[me, slot] = every[jnp.maximum(owner, 0)]
            left = lengths[jnp.maximum(owner, 0)] - slabs[group, me, slot] * slab_length
            limits.append(jnp.where(owner >= 0, left, 0))
        for slot in range(slot_count):
            pltpu.make_async_copy(cache.at[slot], keys.at[slot], key_sems.at[slot]).wait()

        def one_step(step, carry):
            first = lax.rem(me // chunk + steps - step, steps) * chunk
            for at in range(chunk):
                source = first + at

                @pl.when(source != me)
                def _():
                    row_copy(source, source).wait_recv()

            for slot in range(slot_count):
                block = arrived[pl.ds(first, chunk), slot].reshape(chunk * rows, key_width)
                scores = lax.dot_general(
                    block, keys[slot], (((1,), (0,)), ((), ())), preferred_element_type=jnp.float32
                )
                place = lax.broadcasted_iota(jnp.int32, (1, slab_length), 1)
                is_valid = place < limits[slot]
                masked = jnp.where(is_valid, scores, EMPTY)
                peak = jnp.max(masked, axis=1, keepdims=True)
                weights = jnp.where(is_valid, jnp.exp(masked - peak), 0.0)
                total = jnp.maximum(jnp.sum(weights, axis=1, keepdims=True), 1.0)
                mixture = lax.dot_general(
                    weights.astype(jnp.bfloat16),
                    keys[slot, :LATENT],
                    (((1,), (1,)), ((), ())),
                    preferred_element_type=jnp.float32,
                )
                log = jnp.broadcast_to(peak + jnp.log(total), (chunk * rows, 128))
                mix = (mixture / total).astype(jnp.bfloat16).reshape(chunk, rows, LATENT)
                for at in range(chunk):
                    mix_stage[first + at, slot] = mix[at]
                    turned = jnp.transpose(log[at * rows : (at + 1) * rows])
                    log_stage[first + at, slot : slot + 1, :rows] = turned[:1]
            for at in range(chunk):
                source = first + at

                @pl.when(source != me)
                def _():
                    for copy in back_copies(source, me):
                        copy.start()

            return carry

        lax.fori_loop(0, steps, one_step, 0)
        got_log[me] = log_stage[me]
        got_mix[me] = mix_stage[me]

        def finish(step, carry):
            peer = lax.rem(me + step, count)
            row_copy(peer, peer).wait_send()
            for copy in back_copies(peer, peer):
                copy.wait_send()
                copy.wait_recv()
            return carry

        lax.fori_loop(1, count, finish, 0)

    smem = pl.BlockSpec(memory_space=pltpu.SMEM)
    vmem = pl.BlockSpec(memory_space=pltpu.VMEM)
    log_shape = (count, log_rows, lanes)
    mix_shape = (count, slot_count, rows, LATENT)
    got_log, got_mix = pl.pallas_call(
        body,
        out_shape=(
            jax.ShapeDtypeStruct(log_shape, jnp.float32),
            jax.ShapeDtypeStruct(mix_shape, jnp.bfloat16),
        ),
        in_specs=[smem, smem, smem, vmem, pl.BlockSpec(memory_space=pl.ANY)],
        out_specs=(vmem, vmem),
        scratch_shapes=[
            pltpu.VMEM((count, slot_count, rows, key_width), jnp.bfloat16),
            pltpu.VMEM((count, slot_count, rows, key_width), jnp.bfloat16),
            pltpu.VMEM((slot_count, key_width, slab_length), jnp.bfloat16),
            pltpu.VMEM(log_shape, jnp.float32),
            pltpu.VMEM(mix_shape, jnp.bfloat16),
            pltpu.SemaphoreType.DMA((slot_count,)),
            pltpu.SemaphoreType.DMA((count,)),
            pltpu.SemaphoreType.DMA((count,)),
            pltpu.SemaphoreType.DMA((2, count)),
            pltpu.SemaphoreType.DMA((2, count)),
        ],
        compiler_params=pltpu.CompilerParams(
            collective_id=call_id, has_side_effects=True, vmem_limit_bytes=24 * 1024 * 1024
        ),
        name="attend_slots",
    )(
        context_length,
        slot_sequence,
        slot_slab,
        every_seq,
        cache_slots,
    )
    return got_log[:, :slot_count, :rows], got_mix.astype(jnp.float32)


def merge_blocks(block_log, block_out, block_owner, own_log, own_out):
    owners_count = own_log.shape[0]
    matches = block_owner[None, :] == jnp.arange(owners_count, dtype=jnp.int32)[:, None]
    picked = jnp.where(matches[:, :, None, None], block_log[None], EMPTY)
    top_log = jnp.maximum(jnp.max(picked, axis=1), own_log)
    weights = jnp.where(matches[:, :, None, None], jnp.exp(picked - top_log[:, None]), 0.0)
    own_weight = jnp.exp(own_log - top_log)
    weight_sum = jnp.sum(weights, axis=1) + own_weight
    summed = jnp.einsum("sbtx,btxl->stxl", weights, block_out, precision=lax.Precision.HIGHEST)
    summed = summed + own_weight[..., None] * own_out
    return (top_log + jnp.log(weight_sum), summed / weight_sum[..., None])


def draft_partials(queries_seq, draft_rows):
    scores = jnp.einsum(
        "sthk,suk->sthu", queries_seq, draft_rows, preferred_element_type=jnp.float32
    )
    causal = jnp.arange(DRAFT)[None, :] <= jnp.arange(DRAFT)[:, None]
    masked = jnp.where(causal[None, :, None, :], scores, EMPTY)
    draft_peak = jnp.max(masked, axis=3)
    weights = jnp.where(causal[None, :, None, :], jnp.exp(masked - draft_peak[..., None]), 0.0)
    draft_total = jnp.sum(weights, axis=3)
    mixture = jnp.einsum(
        "sthu,sul->sthl",
        weights.astype(jnp.bfloat16),
        draft_rows[..., :LATENT],
        preferred_element_type=jnp.float32,
    )
    return (draft_peak + jnp.log(draft_total), mixture / draft_total[..., None])


def shards_general(
    q_compressed,
    w_q_nope,
    w_q_rope,
    w_uk,
    w_uv,
    w_o,
    kv_cache,
    draft_kv,
    context_length,
    slot_sequence,
    slot_slab,
):
    group_count = lax.axis_size("group")
    holder_count = lax.axis_size("dev")
    group_index = lax.axis_index("group")
    token_count = q_compressed.shape[0]
    seq_group = token_count // DRAFT
    heads_here = w_uk.shape[0]
    key_width = LATENT + ROPE
    q_nope = jnp.dot(q_compressed, w_q_nope, preferred_element_type=jnp.float32).astype(
        jnp.bfloat16
    )
    q_nope = q_nope.reshape(token_count, heads_here, NOPE)
    q_rope = jnp.dot(q_compressed, w_q_rope, preferred_element_type=jnp.float32).reshape(
        token_count, heads_here, ROPE
    )
    absorbed = jnp.einsum("thn,hnl->thl", q_nope, w_uk, preferred_element_type=jnp.float32)
    queries = (jnp.concatenate([absorbed, q_rope], axis=2) * (NOPE + ROPE) ** (-0.5)).astype(
        jnp.bfloat16
    )
    queries_seq = queries.reshape(seq_group, DRAFT, heads_here, key_width)
    draft_log, draft_mix = draft_partials(
        queries_seq, draft_kv.reshape(seq_group, DRAFT, key_width)
    )
    group_table = lax.dynamic_index_in_dim(slot_sequence, group_index, 0, keepdims=False)
    outgoing = jnp.broadcast_to(
        queries_seq.reshape(1, -1, key_width), (group_count, token_count * heads_here, key_width)
    )
    (gathered,) = exchange("group", 0, outgoing)
    back_log, back_mix = attend_slots(
        1,
        gathered.reshape(group_count * seq_group, DRAFT * heads_here, key_width),
        jnp.swapaxes(kv_cache[0, 0], 1, 2),
        context_length,
        slot_sequence,
        slot_slab,
    )
    seq_total = group_count * seq_group
    group_log, group_mix = merge_blocks(
        back_log.reshape(-1, DRAFT, heads_here),
        back_mix.reshape(-1, DRAFT, heads_here, LATENT),
        group_table.reshape(-1),
        jnp.full((seq_total, DRAFT, heads_here), EMPTY, jnp.float32),
        jnp.zeros((seq_total, DRAFT, heads_here, LATENT), jnp.float32),
    )
    home_log, home_mix = exchange_partials(
        "group",
        3,
        group_log.reshape(group_count, seq_group, DRAFT, heads_here),
        group_mix.reshape(group_count, seq_group, DRAFT, heads_here, LATENT),
    )
    home_owner = jnp.tile(jnp.arange(seq_group, dtype=jnp.int32), group_count)
    final_log, final_mix = merge_blocks(
        home_log.reshape(-1, DRAFT, heads_here),
        home_mix.reshape(-1, DRAFT, heads_here, LATENT),
        home_owner,
        draft_log,
        draft_mix,
    )
    attended = final_mix.astype(jnp.bfloat16).reshape(token_count, heads_here, LATENT)
    head_values = jnp.einsum("thl,hlv->thv", attended, w_uv, preferred_element_type=jnp.float32)
    head_values = head_values.astype(jnp.bfloat16).reshape(token_count, heads_here * VDIM)
    partial = jnp.dot(head_values, w_o, preferred_element_type=jnp.float32)
    (terms,) = exchange(
        "dev", 4, partial.reshape(holder_count, token_count // holder_count, -1)
    )
    return jnp.sum(terms, axis=0)


PLANES = (2, 4)
HALVES = 2
CHUNKS = 4


def flip(value, mask, extent):
    result, bit = 0, 1
    while bit < extent:
        own = lax.rem(lax.div(value, bit), 2)
        result = result + bit * (1 - own if mask & bit else own)
        bit *= 2
    return result


def fused(
    q_compressed, w_q_nope, w_q_rope, w_uk, w_uv, w_o, keys_hbm, draft_kv,
    context_length, slot_sequence, slot_slab,
):
    groups, count = lax.axis_size("group"), lax.axis_size("dev")
    planes = count // 2
    around = groups * 2
    phases = tuple((s,) for s in range(planes))
    home_tokens, q_rank = q_compressed.shape
    tokens = groups * home_tokens
    seqs = tokens // DRAFT
    heads = w_uk.shape[0] // groups
    unit = heads * DRAFT
    rows = seqs * unit
    slots, key_width, slab_length = keys_hbm.shape
    width = w_o.shape[1]
    nope_cols, rope_cols, out_rows = heads * NOPE, heads * ROPE, heads * VDIM
    cut = width // CHUNKS
    bf16, f32 = jnp.bfloat16, jnp.float32
    number = len(phases)

    def body(
        lengths, owners, slabs, qc, dkv, wqn_hbm, wqr_hbm, wuk_hbm, wuv_hbm, wo_hbm, cache, out,
        qall, dall, wqn, wqr, wuk, wuv, wo, keys, *rest,
    ):
        rest = list(rest)
        take = lambda n: [rest.pop(0) for _ in range(n)]
        zb = take(planes)
        staged = take(planes)
        arrived, mixs, mixg, logs, logg = (take(number) for _ in range(5))
        zms, zmg, zls, zlg = (take(planes) for _ in range(4))
        parts, partg, fin = take(3)
        (
            local, g_send, g_recv, z_send, z_recv, p_send, p_recv, b_send, b_recv,
            y_send, y_recv, r_send, r_recv, f_send, f_recv,
        ) = rest
        g = lax.axis_index("group")
        d = lax.axis_index("dev")
        z, c = lax.div(d, 2), lax.rem(d, 2)
        me = g * 2 + c

        def remote(src, dst, send, recv, to_g, to_d):
            return pltpu.make_async_remote_copy(
                src_ref=src, dst_ref=dst, send_sem=send, recv_sem=recv,
                device_id=(to_g, to_d), device_id_type=pl.DeviceIdType.MESH,
            )

        def plane_peer(step):
            return lax.rem(me + step, around)

        def plane_device(j):
            return lax.div(j, 2), z * 2 + lax.rem(j, 2)

        columns = lambda size: pl.ds(pl.multiple_of(g * size, size), size)
        early = [
            pltpu.make_async_copy(qc, qall.at[g], local.at[6]),
            pltpu.make_async_copy(dkv, dall.at[g], local.at[7]),
        ]
        for copy in early:
            copy.start()
        loads = [
            pltpu.make_async_copy(wqn_hbm.at[:, columns(nope_cols)], wqn, local.at[0]),
            pltpu.make_async_copy(wqr_hbm.at[:, columns(rope_cols)], wqr, local.at[1]),
            pltpu.make_async_copy(wuk_hbm.at[pl.ds(g * heads, heads)], wuk, local.at[2]),
            pltpu.make_async_copy(cache, keys, local.at[3]),
            pltpu.make_async_copy(wuv_hbm.at[pl.ds(g * heads, heads)], wuv, local.at[4]),
            pltpu.make_async_copy(wo_hbm.at[columns(out_rows)], wo, local.at[5]),
        ]
        for copy in loads:
            copy.start()

        barrier = pltpu.get_barrier_semaphore()

        def greet(to_g, to_d):
            pl.semaphore_signal(
                barrier, inc=1, device_id=(to_g, to_d), device_id_type=pl.DeviceIdType.MESH
            )

        for step in range(1, around):
            greet(*plane_device(plane_peer(step)))
        for step in range(1, planes):
            for core in range(2):
                greet(g, lax.rem(z + step, planes) * 2 + core)
        pl.semaphore_wait(barrier, around - 1 + 2 * (planes - 1))

        def group_copies(step):
            to = lax.rem(g + step, groups)
            return [
                remote(qall.at[g], qall.at[g], g_send.at[0, step], g_recv.at[0, step], to, d),
                remote(dall.at[g], dall.at[g], g_send.at[1, step], g_recv.at[1, step], to, d),
            ]

        for copy in early:
            copy.wait()
        for step in range(1, groups):
            for copy in group_copies(step):
                copy.start()
        for step in range(1, groups):
            for copy in group_copies(step):
                copy.wait()

        def joined(ref):
            pieces = [ref[i].astype(f32) for i in range(groups)]
            return jnp.concatenate(pieces, axis=0).astype(bf16)

        q_tokens = joined(qall)
        draft = joined(dall)
        for copy in loads[:3]:
            copy.wait()
        nope = jnp.dot(q_tokens, wqn[...], preferred_element_type=f32).astype(bf16)
        rope = jnp.dot(q_tokens, wqr[...], preferred_element_type=f32)
        by_head = []
        for h in range(heads):
            absorbed = jnp.dot(
                nope[:, h * NOPE : (h + 1) * NOPE], wuk[h], preferred_element_type=f32
            )
            pair = jnp.concatenate([absorbed, rope[:, h * ROPE : (h + 1) * ROPE]], axis=1)
            by_head.append((pair * (NOPE + ROPE) ** (-0.5)).astype(bf16))
        stacked = jnp.concatenate(by_head, axis=0)
        row = lax.broadcasted_iota(jnp.int32, (rows, rows), 0)
        col = lax.broadcasted_iota(jnp.int32, (rows, rows), 1)
        spot = lax.rem(lax.div(row, DRAFT), heads) * tokens
        spot = spot + lax.div(row, unit) * DRAFT + lax.rem(row, DRAFT)
        order = jnp.where(col == spot, 1.0, 0.0).astype(bf16)
        queries = jnp.dot(order, stacked, preferred_element_type=f32).astype(bf16)
        zb[0][...] = queries.reshape(seqs, unit, key_width)

        def z_copy(s, half):
            relay = s & 1 and s > 1
            source, over = (zb[s ^ 1], 1) if relay else (zb[0], s)
            span = pl.ds(half * seqs // HALVES, seqs // HALVES)
            return remote(
                source.at[span], zb[s].at[span], z_send.at[s, half], z_recv.at[s, half],
                g, flip(z, over, planes) * 2 + c,
            )

        for half in range(HALVES):
            for s in reversed(range(1, planes)):
                if not (s & 1 and s > 1):
                    z_copy(s, half).start()

        place = [(p, phases[p].index(s)) for s in range(planes) for p in range(number) if s in phases[p]]

        def p_copy(s, to):
            p, at = place[s]
            return remote(
                staged[s].at[to], arrived[p].at[me, :, at], p_send.at[s, to], p_recv.at[s, me],
                *plane_device(to),
            )

        def p_arrival(s, source):
            p, at = place[s]
            return remote(
                staged[s].at[source], arrived[p].at[source, :, at], p_send.at[s, source],
                p_recv.at[s, source], *plane_device(source),
            )

        def dispatch(s):
            p, at = place[s]
            if s > 0:
                for half in range(HALVES):
                    z_copy(s, half).wait_recv()
                    if s % 2 == 0 and s + 1 < planes:
                        z_copy(s + 1, half).start()

            def fill(step, carry):
                to = plane_peer(step)
                to_g, to_d = plane_device(to)
                for k in range(slots):
                    staged[s][to, k] = zb[s][jnp.maximum(owners[to_g, k, to_d], 0)]
                return carry

            def send(step, carry):
                p_copy(s, plane_peer(step)).start()
                return carry

            lax.fori_loop(1, around, fill, 0)
            lax.fori_loop(1, around, send, 0)
            for k in range(slots):
                arrived[p][me, k, at] = zb[s][jnp.maximum(owners[g, k, d], 0)]

        def b_copies(p, k, to, source):
            return [
                remote(
                    mixs[p].at[k, to], mixg[p].at[source, k], b_send.at[p, 0, k, to],
                    b_recv.at[p, 0, k, source], *plane_device(to),
                ),
                remote(
                    logs[p].at[k, to], logg[p].at[source, k], b_send.at[p, 1, k, to],
                    b_recv.at[p, 1, k, source], *plane_device(to),
                ),
            ]

        def await_rows(p):
            for s in phases[p]:

                def one(step, carry):
                    p_arrival(s, plane_peer(step)).wait_recv()
                    return carry

                lax.fori_loop(1, around, one, 0)

        def attend(p, k):
            some = len(phases[p])
            per = some * unit
            total_rows = around * per
            owner = owners[g, k, d]
            left = lengths[jnp.maximum(owner, 0)] - slabs[g, k, d] * slab_length
            limit = jnp.where(owner >= 0, left, 0)
            block = arrived[p][:, k].reshape(total_rows, key_width)
            scores = lax.dot_general(
                block, keys[k], (((1,), (0,)), ((), ())), preferred_element_type=f32
            )
            position = lax.broadcasted_iota(jnp.int32, (1, slab_length), 1)
            is_valid = position < limit
            masked = jnp.where(is_valid, scores, EMPTY)
            peak = jnp.max(masked, axis=1, keepdims=True)
            weights = jnp.where(is_valid, jnp.exp(masked - peak), 0.0)
            total = jnp.maximum(jnp.sum(weights, axis=1, keepdims=True), 1.0)
            mixture = lax.dot_general(
                weights.astype(bf16), keys[k, :LATENT], (((1,), (1,)), ((), ())),
                preferred_element_type=f32,
            )
            mixs[p][k] = (mixture / total).astype(bf16).reshape(around, some, unit, LATENT)
            log = jnp.broadcast_to(peak + jnp.log(total), (total_rows, 128))
            log = jnp.transpose(log)[:1]
            for j in range(around):
                logs[p][k, j, :, :per] = log[:, j * per : (j + 1) * per]

            def send(step, carry):
                for copy in b_copies(p, k, plane_peer(step), me):
                    copy.start()
                return carry

            lax.fori_loop(1, around, send, 0)
            mixg[p][me, k] = mixs[p][k, me]
            logg[p][me, k] = logs[p][k, me]

        def split_dot(weights, block):
            high = weights.astype(bf16)
            low = (weights - high.astype(f32)).astype(bf16)
            return jnp.dot(high, block, preferred_element_type=f32) + jnp.dot(
                low, block, preferred_element_type=f32
            )

        def y_copy(s):
            to = flip(z, s, planes) * 2 + c
            return [
                remote(zms[s], zmg[s], y_send.at[0, s], y_recv.at[0, s], g, to),
                remote(zls[s], zlg[s], y_send.at[1, s], y_recv.at[1, s], g, to),
            ]

        def merge_plane(p):
            some = len(phases[p])
            per = some * unit
            blocks = around * slots

            def one(step, carry):
                source = plane_peer(step)
                for k in range(slots):
                    for copy in b_copies(p, k, source, source):
                        copy.wait_recv()
                return carry

            lax.fori_loop(1, around, one, 0)
            wide = blocks * per
            cells = [logg[p][j, k, :, :per] for j in range(around) for k in range(slots)]
            log = jnp.concatenate(cells, axis=1)
            lane = lax.broadcasted_iota(jnp.int32, (1, wide), 1)
            owner = jnp.full((1, wide), -1, jnp.int32)
            for j in range(around):
                for k in range(slots):
                    here = owners[j // 2, k, z * 2 + j % 2]
                    owner = jnp.where(lax.div(lane, per) == j * slots + k, here, owner)
            tag = owner * per + lax.rem(lane, per)
            height = some * rows
            line = lax.broadcasted_iota(jnp.int32, (height, 1), 0)
            inner = lax.div(line, rows) * unit + lax.rem(line, unit)
            mark = lax.rem(lax.div(line, unit), seqs) * per + inner
            match = tag == mark
            picked = jnp.where(match, log, EMPTY)
            top = jnp.max(picked, axis=1, keepdims=True)
            weights = jnp.where(match, jnp.exp(picked - top), 0.0)
            total = jnp.maximum(jnp.sum(weights, axis=1, keepdims=True), 1.0)
            block = mixg[p][...].reshape(wide, LATENT)
            mixed = (split_dot(weights, block) / total).astype(bf16)
            logged = jnp.broadcast_to(top + jnp.log(total), (height, 128))
            logged = jnp.transpose(logged)[:1]
            for at, s in enumerate(phases[p]):
                mix_to, log_to = (zms[s], zls[s]) if s > 0 else (zmg[s], zlg[s])
                mix_to[...] = mixed[at * rows : (at + 1) * rows]
                log_to[...] = logged[:, at * rows : (at + 1) * rows]
            for s in phases[p]:
                if s > 0:
                    for copy in y_copy(s):
                        copy.start()

        dispatch(0)
        scores = lax.dot_general(
            queries, draft, (((1,), (1,)), ((), ())), preferred_element_type=f32
        )
        row = lax.broadcasted_iota(jnp.int32, (rows, tokens), 0)
        col = lax.broadcasted_iota(jnp.int32, (rows, tokens), 1)
        seen = (lax.div(row, unit) == lax.div(col, DRAFT)) & (
            lax.rem(col, DRAFT) <= lax.rem(row, DRAFT)
        )
        masked = jnp.where(seen, scores, EMPTY)
        draft_peak = jnp.max(masked, axis=1, keepdims=True)
        weights = jnp.where(seen, jnp.exp(masked - draft_peak), 0.0)
        draft_total = jnp.sum(weights, axis=1, keepdims=True)
        draft_mix = jnp.dot(weights.astype(bf16), draft[:, :LATENT], preferred_element_type=f32)
        draft_mix = draft_mix / draft_total
        draft_log = draft_peak + jnp.log(draft_total)

        def attend_both(p):
            def one(k, carry):
                attend(p, k)
                return carry

            await_rows(p)
            lax.fori_loop(0, slots, one, 0)

        loads[3].wait()
        attend_both(0)
        for s in range(1, planes):
            dispatch(s)
        merge_plane(0)
        for p in range(1, number):
            attend_both(p)
            if p > 1:
                merge_plane(p - 1)
        merge_plane(number - 1)

        for s in range(1, planes):
            for copy in y_copy(s):
                copy.wait_recv()
        wide = planes * rows
        log = jnp.concatenate([zlg[s][...] for s in range(planes)], axis=1)
        lane = lax.broadcasted_iota(jnp.int32, (1, wide), 1)
        line = lax.broadcasted_iota(jnp.int32, (rows, 1), 0)
        match = lax.rem(lane, rows) == line
        picked = jnp.where(match, log, EMPTY)
        top = jnp.maximum(jnp.max(picked, axis=1, keepdims=True), draft_log)
        weights = jnp.where(match, jnp.exp(picked - top), 0.0)
        own = jnp.exp(draft_log - top)
        total = jnp.sum(weights, axis=1, keepdims=True) + own
        block = jnp.concatenate([zmg[s][...] for s in range(planes)], axis=0)
        summed = split_dot(weights, block) + own * draft_mix
        attended = (summed / total).astype(bf16)
        row = lax.broadcasted_iota(jnp.int32, (rows, rows), 0)
        col = lax.broadcasted_iota(jnp.int32, (rows, rows), 1)
        token = lax.rem(row, tokens)
        spot = lax.div(token, DRAFT) * unit + lax.div(row, tokens) * DRAFT + lax.rem(token, DRAFT)
        order = jnp.where(col == spot, 1.0, 0.0).astype(bf16)
        attended = jnp.dot(order, attended, preferred_element_type=f32).astype(bf16)
        loads[4].wait()
        loads[5].wait()
        values = [
            jnp.dot(attended[h * tokens : (h + 1) * tokens], wuv[h], preferred_element_type=f32)
            for h in range(heads)
        ]
        values = jnp.concatenate(values, axis=1).astype(bf16)

        def r_copy(n, step):
            to = lax.rem(g + step, groups)
            return remote(
                parts.at[n, to], partg.at[n, g], r_send.at[n, step], r_recv.at[n, step], to, d
            )

        def project(n, carry):
            span = pl.ds(pl.multiple_of(n * cut, 128), cut)
            part = jnp.dot(values, wo[:, span], preferred_element_type=f32)
            for i in range(groups):
                parts[n, i] = part[i * home_tokens : (i + 1) * home_tokens].astype(bf16)
            for step in range(1, groups):
                r_copy(n, step).start()
            partg[n, g] = parts[n, g]
            return carry

        lax.fori_loop(0, CHUNKS, project, 0)

        def f_copy(n, to, source):
            return remote(
                fin.at[n, to], out.at[n, source], f_send.at[n, to], f_recv.at[n, source], g, to
            )

        own_tokens = home_tokens // count

        def gather(n, carry):
            for step in range(1, groups):
                r_copy(n, step).wait_recv()
            summed = partg[n, 0].astype(f32)
            for i in range(1, groups):
                summed = summed + partg[n, i].astype(f32)
            for t in range(count):
                fin[n, t] = summed[t * own_tokens : (t + 1) * own_tokens].astype(bf16)

            def send(step, carry):
                f_copy(n, lax.rem(d + step, count), d).start()
                return carry

            lax.fori_loop(1, count, send, 0)
            out[n, d] = fin[n, d]
            return carry

        lax.fori_loop(0, CHUNKS, gather, 0)

        for n in range(CHUNKS):

            def one(step, carry):
                source = lax.rem(d + step, count)
                f_copy(n, source, source).wait_recv()
                return carry

            lax.fori_loop(1, count, one, 0)

        for s in range(1, planes):
            for half in range(HALVES):
                z_copy(s, half).wait_send()
            for copy in y_copy(s):
                copy.wait_send()

        def finish(step, carry):
            to = plane_peer(step)
            for s in range(planes):
                p_copy(s, to).wait_send()
            for p in range(number):
                for k in range(slots):
                    for copy in b_copies(p, k, to, me):
                        copy.wait_send()
            return carry

        lax.fori_loop(1, around, finish, 0)

        def finish_chunk(n, carry):
            for step in range(1, groups):
                r_copy(n, step).wait_send()
            for step in range(1, count):
                f_copy(n, lax.rem(d + step, count), d).wait_send()
            return carry

        lax.fori_loop(0, CHUNKS, finish_chunk, 0)

    smem = pl.BlockSpec(memory_space=pltpu.SMEM)
    vmem = pl.BlockSpec(memory_space=pltpu.VMEM)
    hbm = pl.BlockSpec(memory_space=pl.ANY)
    own_tokens = home_tokens // count
    scratch = [
        pltpu.VMEM((groups, home_tokens, q_rank), bf16),
        pltpu.VMEM((groups, home_tokens, key_width), bf16),
        pltpu.VMEM((q_rank, nope_cols), bf16),
        pltpu.VMEM((q_rank, rope_cols), bf16),
        pltpu.VMEM((heads, NOPE, LATENT), bf16),
        pltpu.VMEM((heads, LATENT, VDIM), bf16),
        pltpu.VMEM((out_rows, width), bf16),
        pltpu.VMEM((slots, key_width, slab_length), bf16),
    ]
    scratch += [pltpu.VMEM((seqs, unit, key_width), bf16) for _ in range(planes)]
    scratch += [pltpu.VMEM((around, slots, unit, key_width), bf16) for _ in range(planes)]
    sizes = [len(phase) for phase in phases]
    scratch += [pltpu.VMEM((around, slots, n, unit, key_width), bf16) for n in sizes]
    scratch += [pltpu.VMEM((slots, around, n, unit, LATENT), bf16) for n in sizes]
    scratch += [pltpu.VMEM((around, slots, n, unit, LATENT), bf16) for n in sizes]
    lanes = [-(-n * unit // 128) * 128 for n in sizes]
    scratch += [pltpu.VMEM((slots, around, 1, n), f32) for n in lanes]
    scratch += [pltpu.VMEM((around, slots, 1, n), f32) for n in lanes]
    scratch += [pltpu.VMEM((rows, LATENT), bf16) for _ in range(2 * planes)]
    scratch += [pltpu.VMEM((1, rows), f32) for _ in range(2 * planes)]
    scratch += [pltpu.VMEM((CHUNKS, groups, home_tokens, cut), bf16) for _ in range(2)]
    scratch += [pltpu.VMEM((CHUNKS, count, own_tokens, cut), bf16)]
    dma = pltpu.SemaphoreType.DMA
    scratch += [
        dma((8,)),
        dma((2, groups)), dma((2, groups)),
        dma((planes, HALVES)), dma((planes, HALVES)),
        dma((planes, around)), dma((planes, around)),
        dma((number, 2, slots, around)), dma((number, 2, slots, around)),
        dma((2, planes)), dma((2, planes)),
        dma((CHUNKS, groups)), dma((CHUNKS, groups)),
        dma((CHUNKS, count)), dma((CHUNKS, count)),
    ]
    terms = pl.pallas_call(
        body,
        out_shape=jax.ShapeDtypeStruct((CHUNKS, count, own_tokens, cut), bf16),
        in_specs=[smem] * 3 + [hbm] * 8,
        out_specs=vmem,
        scratch_shapes=scratch,
        compiler_params=pltpu.CompilerParams(
            collective_id=0, has_side_effects=True, vmem_limit_bytes=56 * 1024 * 1024
        ),
        name="fused",
    )(
        context_length, jnp.swapaxes(slot_sequence, 1, 2), jnp.swapaxes(slot_slab, 1, 2),
        q_compressed, draft_kv, w_q_nope, w_q_rope, w_uk, w_uv, w_o, keys_hbm,
    )
    summed = jnp.sum(terms.astype(f32), axis=1)
    return jnp.swapaxes(summed, 0, 1).reshape(own_tokens, width)


def shards(
    q_compressed, w_q_nope, w_q_rope, w_uk, w_uv, w_o, kv_cache, draft_kv,
    context_length, slot_sequence, slot_slab,
):
    args = (
        q_compressed, w_q_nope, w_q_rope, w_uk, w_uv, w_o, kv_cache, draft_kv,
        context_length, slot_sequence, slot_slab,
    )
    groups, count = lax.axis_size("group"), lax.axis_size("dev")
    heads = w_uk.shape[0] // groups
    fits = (
        w_uk.shape[0] % groups == 0
        and heads * DRAFT % 16 == 0
        and count % 2 == 0
        and count // 2 in PLANES
        and q_compressed.shape[0] % count == 0
        and groups * q_compressed.shape[0] // DRAFT % HALVES == 0
        and w_o.shape[1] % (128 * CHUNKS) == 0
    )
    if not fits:
        return shards_general(*args)
    keys = jnp.swapaxes(kv_cache[0, 0], 1, 2)
    return fused(
        q_compressed, w_q_nope, w_q_rope, w_uk, w_uv, w_o, keys, draft_kv,
        context_length, slot_sequence, slot_slab,
    )


def solution(mesh):
    placed = (
        P("group", None),
        P(None, "dev"),
        P(None, "dev"),
        P("dev", None, None),
        P("dev", None, None),
        P("dev", None),
        P("group", "dev", None, None, None),
        P("group", None),
        P(),
        P(),
        P(),
    )
    return jax.shard_map(
        shards, mesh=mesh, in_specs=placed, out_specs=P(("group", "dev"), None), check_vma=False
    )
```

```python
import jax
import jax.numpy as jnp
from jax import lax
from jax.experimental import pallas as pl
from jax.experimental.pallas import tpu as pltpu
from jax.sharding import PartitionSpec as P

NOPE = 128
ROPE = 64
LATENT = 512
VDIM = 128
DRAFT = 4


EMPTY = -1e30


def exchange(axis, call_id, *blocks):
    count = lax.axis_size(axis)
    number = len(blocks)

    def body(*refs):
        sent, got = refs[:number], refs[number : 2 * number]
        send_sems, recv_sems, local_sems = refs[2 * number :]
        me = lax.axis_index(axis)
        barrier = pltpu.get_barrier_semaphore()
        for step in range(1, count):
            pl.semaphore_signal(
                barrier,
                inc=1,
                device_id={axis: lax.rem(me + step, count)},
                device_id_type=pl.DeviceIdType.MESH,
            )
        pl.semaphore_wait(barrier, count - 1)
        started = []
        for step in range(1, count):
            peer = lax.rem(me + step, count)
            for which in range(number):
                copy = pltpu.make_async_remote_copy(
                    src_ref=sent[which].at[peer],
                    dst_ref=got[which].at[me],
                    send_sem=send_sems.at[which, step],
                    recv_sem=recv_sems.at[which, step],
                    device_id={axis: peer},
                    device_id_type=pl.DeviceIdType.MESH,
                )
                copy.start()
                started.append(copy)
        own = []
        for which in range(number):
            copy = pltpu.make_async_copy(
                sent[which].at[me], got[which].at[me], local_sems.at[which]
            )
            copy.start()
            own.append(copy)
        for copy in own:
            copy.wait()
        for copy in started:
            copy.wait()

    vmem = pl.BlockSpec(memory_space=pltpu.VMEM)
    return pl.pallas_call(
        body,
        out_shape=tuple(jax.ShapeDtypeStruct(block.shape, block.dtype) for block in blocks),
        in_specs=[vmem] * number,
        out_specs=tuple([vmem] * number),
        scratch_shapes=[
            pltpu.SemaphoreType.DMA((number, count)),
            pltpu.SemaphoreType.DMA((number, count)),
            pltpu.SemaphoreType.DMA((number,)),
        ],
        compiler_params=pltpu.CompilerParams(
            collective_id=call_id, has_side_effects=True, vmem_limit_bytes=8 * 1024 * 1024
        ),
        name="exchange_%d" % call_id,
    )(*blocks)


def exchange_partials(axis, call_id, block_log, block_mix):
    count = lax.axis_size(axis)
    flat_log = block_log.reshape(count, 1, -1)
    width = flat_log.shape[2]
    padded = -(-width // 128) * 128
    flat_log = jnp.pad(flat_log, ((0, 0), (0, 0), (0, padded - width)))
    flat_mix = block_mix.astype(jnp.bfloat16).reshape(count, -1, block_mix.shape[-1])
    got_log, got_mix = exchange(axis, call_id, flat_log, flat_mix)
    return (
        got_log[:, :, :width].reshape(block_log.shape),
        got_mix.reshape(block_mix.shape).astype(jnp.float32),
    )


def attend_slots(call_id, every_seq, cache_slots, context_length, slot_sequence, slot_slab):
    count = lax.axis_size("dev")
    slot_count, key_width, slab_length = cache_slots.shape
    seq_total, rows, _ = every_seq.shape
    chunk = min(count, max(1, 128 // rows))
    while count % chunk:
        chunk -= 1
    steps = count // chunk
    lanes = -(-rows // 128) * 128
    log_rows = -(-slot_count // 8) * 8

    def body(
        lengths, owners, slabs, every, cache, got_log, got_mix,
        staged, arrived, keys, log_stage, mix_stage,
        key_sems, send_sems, arrive_sems, back_send, back_recv,
    ):
        group = lax.axis_index("group")
        me = lax.axis_index("dev")
        barrier = pltpu.get_barrier_semaphore()

        def greet(step, carry):
            pl.semaphore_signal(
                barrier,
                inc=1,
                device_id={"dev": lax.rem(me + step, count)},
                device_id_type=pl.DeviceIdType.MESH,
            )
            return carry

        lax.fori_loop(1, count, greet, 0)
        for slot in range(slot_count):
            pltpu.make_async_copy(cache.at[slot], keys.at[slot], key_sems.at[slot]).start()
        pl.semaphore_wait(barrier, count - 1)

        def row_copy(peer, source):
            return pltpu.make_async_remote_copy(
                src_ref=staged.at[peer],
                dst_ref=arrived.at[source],
                send_sem=send_sems.at[peer],
                recv_sem=arrive_sems.at[source],
                device_id={"dev": peer},
                device_id_type=pl.DeviceIdType.MESH,
            )

        def back_copies(peer, source):
            return [
                pltpu.make_async_remote_copy(
                    src_ref=stage.at[peer],
                    dst_ref=target.at[source],
                    send_sem=back_send.at[which, peer],
                    recv_sem=back_recv.at[which, source],
                    device_id={"dev": peer},
                    device_id_type=pl.DeviceIdType.MESH,
                )
                for which, (stage, target) in enumerate([(log_stage, got_log), (mix_stage, got_mix)])
            ]

        def send_rows(step, carry):
            peer = lax.rem(me + step, count)
            for slot in range(slot_count):
                owner = jnp.maximum(owners[group, peer, slot], 0)
                staged[peer, slot] = every[owner]
            row_copy(peer, me).start()
            return carry

        lax.fori_loop(1, count, send_rows, 0)
        limits = []
        for slot in range(slot_count):
            owner = owners[group, me, slot]
            arrived[me, slot] = every[jnp.maximum(owner, 0)]
            left = lengths[jnp.maximum(owner, 0)] - slabs[group, me, slot] * slab_length
            limits.append(jnp.where(owner >= 0, left, 0))
        for slot in range(slot_count):
            pltpu.make_async_copy(cache.at[slot], keys.at[slot], key_sems.at[slot]).wait()

        def one_step(step, carry):
            first = lax.rem(me // chunk + steps - step, steps) * chunk
            for at in range(chunk):
                source = first + at

                @pl.when(source != me)
                def _():
                    row_copy(source, source).wait_recv()

            for slot in range(slot_count):
                block = arrived[pl.ds(first, chunk), slot].reshape(chunk * rows, key_width)
                scores = lax.dot_general(
                    block, keys[slot], (((1,), (0,)), ((), ())), preferred_element_type=jnp.float32
                )
                place = lax.broadcasted_iota(jnp.int32, (1, slab_length), 1)
                is_valid = place < limits[slot]
                masked = jnp.where(is_valid, scores, EMPTY)
                peak = jnp.max(masked, axis=1, keepdims=True)
                weights = jnp.where(is_valid, jnp.exp(masked - peak), 0.0)
                total = jnp.maximum(jnp.sum(weights, axis=1, keepdims=True), 1.0)
                mixture = lax.dot_general(
                    weights.astype(jnp.bfloat16),
                    keys[slot, :LATENT],
                    (((1,), (1,)), ((), ())),
                    preferred_element_type=jnp.float32,
                )
                log = jnp.broadcast_to(peak + jnp.log(total), (chunk * rows, 128))
                mix = (mixture / total).astype(jnp.bfloat16).reshape(chunk, rows, LATENT)
                for at in range(chunk):
                    mix_stage[first + at, slot] = mix[at]
                    turned = jnp.transpose(log[at * rows : (at + 1) * rows])
                    log_stage[first + at, slot : slot + 1, :rows] = turned[:1]
            for at in range(chunk):
                source = first + at

                @pl.when(source != me)
                def _():
                    for copy in back_copies(source, me):
                        copy.start()

            return carry

        lax.fori_loop(0, steps, one_step, 0)
        got_log[me] = log_stage[me]
        got_mix[me] = mix_stage[me]

        def finish(step, carry):
            peer = lax.rem(me + step, count)
            row_copy(peer, peer).wait_send()
            for copy in back_copies(peer, peer):
                copy.wait_send()
                copy.wait_recv()
            return carry

        lax.fori_loop(1, count, finish, 0)

    smem = pl.BlockSpec(memory_space=pltpu.SMEM)
    vmem = pl.BlockSpec(memory_space=pltpu.VMEM)
    log_shape = (count, log_rows, lanes)
    mix_shape = (count, slot_count, rows, LATENT)
    got_log, got_mix = pl.pallas_call(
        body,
        out_shape=(
            jax.ShapeDtypeStruct(log_shape, jnp.float32),
            jax.ShapeDtypeStruct(mix_shape, jnp.bfloat16),
        ),
        in_specs=[smem, smem, smem, vmem, pl.BlockSpec(memory_space=pl.ANY)],
        out_specs=(vmem, vmem),
        scratch_shapes=[
            pltpu.VMEM((count, slot_count, rows, key_width), jnp.bfloat16),
            pltpu.VMEM((count, slot_count, rows, key_width), jnp.bfloat16),
            pltpu.VMEM((slot_count, key_width, slab_length), jnp.bfloat16),
            pltpu.VMEM(log_shape, jnp.float32),
            pltpu.VMEM(mix_shape, jnp.bfloat16),
            pltpu.SemaphoreType.DMA((slot_count,)),
            pltpu.SemaphoreType.DMA((count,)),
            pltpu.SemaphoreType.DMA((count,)),
            pltpu.SemaphoreType.DMA((2, count)),
            pltpu.SemaphoreType.DMA((2, count)),
        ],
        compiler_params=pltpu.CompilerParams(
            collective_id=call_id, has_side_effects=True, vmem_limit_bytes=24 * 1024 * 1024
        ),
        name="attend_slots",
    )(
        context_length,
        slot_sequence,
        slot_slab,
        every_seq,
        cache_slots,
    )
    return got_log[:, :slot_count, :rows], got_mix.astype(jnp.float32)


def merge_blocks(block_log, block_out, block_owner, own_log, own_out):
    owners_count = own_log.shape[0]
    matches = block_owner[None, :] == jnp.arange(owners_count, dtype=jnp.int32)[:, None]
    picked = jnp.where(matches[:, :, None, None], block_log[None], EMPTY)
    top_log = jnp.maximum(jnp.max(picked, axis=1), own_log)
    weights = jnp.where(matches[:, :, None, None], jnp.exp(picked - top_log[:, None]), 0.0)
    own_weight = jnp.exp(own_log - top_log)
    weight_sum = jnp.sum(weights, axis=1) + own_weight
    summed = jnp.einsum("sbtx,btxl->stxl", weights, block_out, precision=lax.Precision.HIGHEST)
    summed = summed + own_weight[..., None] * own_out
    return (top_log + jnp.log(weight_sum), summed / weight_sum[..., None])


def draft_partials(queries_seq, draft_rows):
    scores = jnp.einsum(
        "sthk,suk->sthu", queries_seq, draft_rows, preferred_element_type=jnp.float32
    )
    causal = jnp.arange(DRAFT)[None, :] <= jnp.arange(DRAFT)[:, None]
    masked = jnp.where(causal[None, :, None, :], scores, EMPTY)
    draft_peak = jnp.max(masked, axis=3)
    weights = jnp.where(causal[None, :, None, :], jnp.exp(masked - draft_peak[..., None]), 0.0)
    draft_total = jnp.sum(weights, axis=3)
    mixture = jnp.einsum(
        "sthu,sul->sthl",
        weights.astype(jnp.bfloat16),
        draft_rows[..., :LATENT],
        preferred_element_type=jnp.float32,
    )
    return (draft_peak + jnp.log(draft_total), mixture / draft_total[..., None])


def shards_general(
    q_compressed,
    w_q_nope,
    w_q_rope,
    w_uk,
    w_uv,
    w_o,
    kv_cache,
    draft_kv,
    context_length,
    slot_sequence,
    slot_slab,
):
    group_count = lax.axis_size("group")
    holder_count = lax.axis_size("dev")
    group_index = lax.axis_index("group")
    token_count = q_compressed.shape[0]
    seq_group = token_count // DRAFT
    heads_here = w_uk.shape[0]
    key_width = LATENT + ROPE
    q_nope = jnp.dot(q_compressed, w_q_nope, preferred_element_type=jnp.float32).astype(
        jnp.bfloat16
    )
    q_nope = q_nope.reshape(token_count, heads_here, NOPE)
    q_rope = jnp.dot(q_compressed, w_q_rope, preferred_element_type=jnp.float32).reshape(
        token_count, heads_here, ROPE
    )
    absorbed = jnp.einsum("thn,hnl->thl", q_nope, w_uk, preferred_element_type=jnp.float32)
    queries = (jnp.concatenate([absorbed, q_rope], axis=2) * (NOPE + ROPE) ** (-0.5)).astype(
        jnp.bfloat16
    )
    queries_seq = queries.reshape(seq_group, DRAFT, heads_here, key_width)
    draft_log, draft_mix = draft_partials(
        queries_seq, draft_kv.reshape(seq_group, DRAFT, key_width)
    )
    group_table = lax.dynamic_index_in_dim(slot_sequence, group_index, 0, keepdims=False)
    outgoing = jnp.broadcast_to(
        queries_seq.reshape(1, -1, key_width), (group_count, token_count * heads_here, key_width)
    )
    (gathered,) = exchange("group", 0, outgoing)
    back_log, back_mix = attend_slots(
        1,
        gathered.reshape(group_count * seq_group, DRAFT * heads_here, key_width),
        jnp.swapaxes(kv_cache[0, 0], 1, 2),
        context_length,
        slot_sequence,
        slot_slab,
    )
    seq_total = group_count * seq_group
    group_log, group_mix = merge_blocks(
        back_log.reshape(-1, DRAFT, heads_here),
        back_mix.reshape(-1, DRAFT, heads_here, LATENT),
        group_table.reshape(-1),
        jnp.full((seq_total, DRAFT, heads_here), EMPTY, jnp.float32),
        jnp.zeros((seq_total, DRAFT, heads_here, LATENT), jnp.float32),
    )
    home_log, home_mix = exchange_partials(
        "group",
        3,
        group_log.reshape(group_count, seq_group, DRAFT, heads_here),
        group_mix.reshape(group_count, seq_group, DRAFT, heads_here, LATENT),
    )
    home_owner = jnp.tile(jnp.arange(seq_group, dtype=jnp.int32), group_count)
    final_log, final_mix = merge_blocks(
        home_log.reshape(-1, DRAFT, heads_here),
        home_mix.reshape(-1, DRAFT, heads_here, LATENT),
        home_owner,
        draft_log,
        draft_mix,
    )
    attended = final_mix.astype(jnp.bfloat16).reshape(token_count, heads_here, LATENT)
    head_values = jnp.einsum("thl,hlv->thv", attended, w_uv, preferred_element_type=jnp.float32)
    head_values = head_values.astype(jnp.bfloat16).reshape(token_count, heads_here * VDIM)
    partial = jnp.dot(head_values, w_o, preferred_element_type=jnp.float32)
    (terms,) = exchange(
        "dev", 4, partial.reshape(holder_count, token_count // holder_count, -1)
    )
    return jnp.sum(terms, axis=0)


PLANES = (2, 4)
HALVES = 2
CHUNKS = 4


def flip(value, mask, extent):
    result, bit = 0, 1
    while bit < extent:
        own = lax.rem(lax.div(value, bit), 2)
        result = result + bit * (1 - own if mask & bit else own)
        bit *= 2
    return result


def fused(
    q_compressed, w_q_nope, w_q_rope, w_uk, w_uv, w_o, keys_hbm, draft_kv,
    context_length, slot_sequence, slot_slab,
):
    groups, count = lax.axis_size("group"), lax.axis_size("dev")
    planes = count // 2
    around = groups * 2
    home_tokens, q_rank = q_compressed.shape
    tokens = groups * home_tokens
    seqs = tokens // DRAFT
    heads = w_uk.shape[0] // groups
    unit = heads * DRAFT
    rows = seqs * unit
    slots, key_width, slab_length = keys_hbm.shape
    width = w_o.shape[1]
    nope_cols, rope_cols, out_rows = heads * NOPE, heads * ROPE, heads * VDIM
    cut = width // CHUNKS
    own_tokens = home_tokens // count
    bf16, f32 = jnp.bfloat16, jnp.float32
    tiles = LATENT // 128
    all_tiles = slots * tiles + slots // 2

    def body(
        lengths, owners, slabs, qc, dkv, wqn_hbm, wqr_hbm, wuk_hbm, wuv_hbm, wo_hbm, cache, out,
        qall, dall, wqn, wqr, wuk, wuv, wo, keys, *rest,
    ):
        rest = list(rest)
        take = lambda n: [rest.pop(0) for _ in range(n)]
        lat, rot, sided, staged, arrived, mixs, mixg, logs, logg = (take(planes) for _ in range(9))
        zms, zmg, zls, zlg = (take(planes) for _ in range(4))
        parts, partg, fin = take(3)
        (
            local, g_send, g_recv, z_send, z_recv, p_send, p_recv, b_send, b_recv,
            y_send, y_recv, r_send, r_recv, f_send, f_recv,
        ) = rest
        g = lax.axis_index("group")
        d = lax.axis_index("dev")
        z, c = lax.div(d, 2), lax.rem(d, 2)
        me = g * 2 + c

        def remote(src, dst, send, recv, to_g, to_d):
            return pltpu.make_async_remote_copy(
                src_ref=src, dst_ref=dst, send_sem=send, recv_sem=recv,
                device_id=(to_g, to_d), device_id_type=pl.DeviceIdType.MESH,
            )

        def plane_peer(step):
            return lax.rem(me + step, around)

        def plane_device(j):
            return lax.div(j, 2), z * 2 + lax.rem(j, 2)

        columns = lambda size: pl.ds(pl.multiple_of(g * size, size), size)
        early = [
            pltpu.make_async_copy(qc, qall.at[g], local.at[6]),
            pltpu.make_async_copy(dkv, dall.at[g], local.at[7]),
        ]
        for copy in early:
            copy.start()
        loads = [
            pltpu.make_async_copy(wqn_hbm.at[:, columns(nope_cols)], wqn, local.at[0]),
            pltpu.make_async_copy(wqr_hbm.at[:, columns(rope_cols)], wqr, local.at[1]),
            pltpu.make_async_copy(wuk_hbm.at[pl.ds(g * heads, heads)], wuk, local.at[2]),
            pltpu.make_async_copy(cache, keys, local.at[3]),
            pltpu.make_async_copy(wuv_hbm.at[pl.ds(g * heads, heads)], wuv, local.at[4]),
            pltpu.make_async_copy(wo_hbm.at[columns(out_rows)], wo, local.at[5]),
        ]
        for copy in loads:
            copy.start()

        barrier = pltpu.get_barrier_semaphore()

        def greet(to_g, to_d):
            pl.semaphore_signal(
                barrier, inc=1, device_id=(to_g, to_d), device_id_type=pl.DeviceIdType.MESH
            )

        for step in range(1, around):
            greet(*plane_device(plane_peer(step)))
        for step in range(1, planes):
            greet(g, lax.rem(z + step, planes) * 2 + c)
        pl.semaphore_wait(barrier, around + planes - 2)

        def group_copy(ref, which, step):
            to = lax.rem(g + step, groups)
            return remote(
                ref.at[g], ref.at[g], g_send.at[which, step], g_recv.at[which, step], to, d
            )

        for which, ref in enumerate((qall, dall)):
            early[which].wait()
            for step in reversed(range(1, groups)):
                group_copy(ref, which, step).start()
        for step in range(1, groups):
            group_copy(qall, 0, step).wait()

        def joined(ref):
            pieces = [ref[i].astype(f32) for i in range(groups)]
            return jnp.concatenate(pieces, axis=0).astype(bf16)

        q_tokens = joined(qall)
        for copy in loads[:3]:
            copy.wait()
        nope = jnp.dot(q_tokens, wqn[...], preferred_element_type=f32).astype(bf16)
        rope = jnp.dot(q_tokens, wqr[...], preferred_element_type=f32)
        by_head = []
        for h in range(heads):
            absorbed = jnp.dot(
                nope[:, h * NOPE : (h + 1) * NOPE], wuk[h], preferred_element_type=f32
            )
            pair = jnp.concatenate([absorbed, rope[:, h * ROPE : (h + 1) * ROPE]], axis=1)
            by_head.append((pair * (NOPE + ROPE) ** (-0.5)).astype(bf16))
        stacked = jnp.concatenate(by_head, axis=0)
        row = lax.broadcasted_iota(jnp.int32, (rows, rows), 0)
        col = lax.broadcasted_iota(jnp.int32, (rows, rows), 1)
        spot = lax.rem(lax.div(row, DRAFT), heads) * tokens
        spot = spot + lax.div(row, unit) * DRAFT + lax.rem(row, DRAFT)
        order = jnp.where(col == spot, 1.0, 0.0).astype(bf16)
        queries = jnp.dot(order, stacked, preferred_element_type=f32).astype(bf16)
        for i in range(tiles):
            lat[0][:, i] = queries[:, i * 128 : (i + 1) * 128].reshape(seqs, unit, 128)
        turned = queries[:, LATENT:].astype(f32)
        for i in range(seqs // 2):
            halves = [turned[(2 * i + j) * unit : (2 * i + j + 1) * unit] for j in range(2)]
            rot[0][i] = jnp.concatenate(halves, axis=1).astype(bf16)

        def z_copies(s, half):
            relay = s & 1 and s > 1
            copies = []
            for which, ref in enumerate((lat, rot)):
                source, over = (ref[s ^ 1], 1) if relay else (ref[0], s)
                size = seqs // HALVES // (1 + which)
                span = pl.ds(half * size, size)
                copies.append(
                    remote(
                        source.at[span], ref[s].at[span], z_send.at[which, s, half],
                        z_recv.at[which, s, half], g, flip(z, over, planes) * 2 + c,
                    )
                )
            return copies

        for half in range(HALVES):
            for s in reversed(range(1, planes)):
                if not (s & 1 and s > 1):
                    for copy in z_copies(s, half):
                        copy.start()

        def p_copy(s, to, source):
            return remote(
                staged[s].at[to], arrived[s].at[source], p_send.at[s, to], p_recv.at[s, source],
                *plane_device(to),
            )

        lane_of = lax.broadcasted_iota(jnp.int32, (unit, 128), 1)

        def spread(s):
            for i in range(seqs // 2):
                tile = rot[s][i].astype(f32)
                swapped = jnp.concatenate([tile[:, ROPE:], tile[:, :ROPE]], axis=1).astype(bf16)
                for side in range(2):
                    sided[s][side, 2 * i + side] = rot[s][i]
                    sided[s][side, 2 * i + 1 - side] = swapped

        def pack(dest, at, s, chosen):
            for k in range(slots):
                dest[at, k * tiles : (k + 1) * tiles] = lat[s][chosen[k]]
            for k in range(0, slots, 2):
                sides = [sided[s][side, chosen[k + side]].astype(f32) for side in range(2)]
                both = jnp.where(lane_of < ROPE, sides[0], sides[1])
                dest[at, slots * tiles + k // 2] = both.astype(bf16)

        def dispatch(s):
            if s > 0 and (s % 2 == 1 or s + 1 == planes):
                for half in range(HALVES):
                    for copy in z_copies(s, half):
                        copy.wait_recv()

            spread(s)
            for step in range(1, around):
                to = plane_peer(step)
                to_g, to_d = plane_device(to)
                chosen = [jnp.maximum(owners[to_g, k, to_d], 0) for k in range(slots)]
                pack(staged[s], to, s, chosen)

            def send(step, carry):
                p_copy(s, plane_peer(step), me).start()
                return carry

            lax.fori_loop(1, around, send, 0)
            pack(arrived[s], me, s, [jnp.maximum(owners[g, k, d], 0) for k in range(slots)])

        def b_copies(p, to, source):
            return [
                remote(
                    stage.at[to], target.at[source], b_send.at[p, which, to],
                    b_recv.at[p, which, source], *plane_device(to),
                )
                for which, (stage, target) in enumerate(((mixs[p], mixg[p]), (logs[p], logg[p])))
            ]

        def await_rows(p):
            def one(step, carry):
                source = plane_peer(step)
                p_copy(p, source, source).wait_recv()
                return carry

            lax.fori_loop(1, around, one, 0)

        def attend(p, chosen):
            total_rows = around * unit
            position = lax.broadcasted_iota(jnp.int32, (1, slab_length), 1)
            scored = []
            for k in chosen:
                owner = owners[g, k, d]
                left = lengths[jnp.maximum(owner, 0)] - slabs[g, k, d] * slab_length
                cells = [arrived[p][:, k * tiles + i] for i in range(tiles)]
                cells = [cell.reshape(total_rows, 128) for cell in cells]
                turned = arrived[p][:, slots * tiles + k // 2].reshape(total_rows, 128)
                side = k % 2 * ROPE
                block = jnp.concatenate(cells + [turned[:, side : side + ROPE]], axis=1)
                scores = lax.dot_general(
                    block, keys[k], (((1,), (0,)), ((), ())), preferred_element_type=f32
                )
                scored.append((k, scores, position < jnp.where(owner >= 0, left, 0)))
            weighed = []
            for k, scores, is_valid in scored:
                masked = jnp.where(is_valid, scores, EMPTY)
                peak = jnp.max(masked, axis=1, keepdims=True)
                weights = jnp.where(is_valid, jnp.exp(masked - peak), 0.0)
                total = jnp.maximum(jnp.sum(weights, axis=1, keepdims=True), 1.0)
                weighed.append((k, weights.astype(bf16), peak, total))
            for k, weights, peak, total in weighed:
                mixture = lax.dot_general(
                    weights, keys[k, :LATENT], (((1,), (1,)), ((), ())),
                    preferred_element_type=f32,
                )
                mixs[p][:, k] = (mixture / total).astype(bf16).reshape(around, unit, LATENT)
                log = jnp.broadcast_to(peak + jnp.log(total), (total_rows, 128))
                log = jnp.transpose(log)[:1]
                for j in range(around):
                    logs[p][j, k : k + 1, :unit] = log[:, j * unit : (j + 1) * unit]

        def give_back(p):
            def send(step, carry):
                for copy in b_copies(p, plane_peer(step), me):
                    copy.start()
                return carry

            lax.fori_loop(1, around, send, 0)
            mixg[p][me] = mixs[p][me]
            logg[p][me] = logs[p][me]

        def split_dot(weights, block):
            high = weights.astype(bf16)
            low = (weights - high.astype(f32)).astype(bf16)
            return jnp.dot(high, block, preferred_element_type=f32) + jnp.dot(
                low, block, preferred_element_type=f32
            )

        def y_copy(s):
            to = flip(z, s, planes) * 2 + c
            return [
                remote(zms[s], zmg[s], y_send.at[0, s], y_recv.at[0, s], g, to),
                remote(zls[s], zlg[s], y_send.at[1, s], y_recv.at[1, s], g, to),
            ]

        def merge_plane(p):
            per = unit
            blocks = around * slots

            def one(step, carry):
                source = plane_peer(step)
                for copy in b_copies(p, source, source):
                    copy.wait_recv()
                return carry

            lax.fori_loop(1, around, one, 0)
            wide = blocks * per
            cells = [logg[p][j, k : k + 1, :per] for j in range(around) for k in range(slots)]
            log = jnp.concatenate(cells, axis=1)
            lane = lax.broadcasted_iota(jnp.int32, (1, wide), 1)
            owner = jnp.full((1, wide), -1, jnp.int32)
            for j in range(around):
                for k in range(slots):
                    here = owners[j // 2, k, z * 2 + j % 2]
                    owner = jnp.where(lax.div(lane, per) == j * slots + k, here, owner)
            tag = owner * per + lax.rem(lane, per)
            line = lax.broadcasted_iota(jnp.int32, (rows, 1), 0)
            match = tag == line
            picked = jnp.where(match, log, EMPTY)
            top = jnp.max(picked, axis=1, keepdims=True)
            weights = jnp.where(match, jnp.exp(picked - top), 0.0)
            total = jnp.maximum(jnp.sum(weights, axis=1, keepdims=True), 1.0)
            block = mixg[p][...].reshape(wide, LATENT)
            mixed = (split_dot(weights, block) / total).astype(bf16)
            logged = jnp.broadcast_to(top + jnp.log(total), (rows, 128))
            mix_to, log_to = (zms[p], zls[p]) if p > 0 else (zmg[p], zlg[p])
            mix_to[...] = mixed
            log_to[...] = jnp.transpose(logged)[:1]
            if p > 0:
                for copy in y_copy(p):
                    copy.start()

        def relay(half):
            for s in range(2, planes - 1, 2):
                for copy in z_copies(s, half):
                    copy.wait_recv()
                for copy in z_copies(s + 1, half):
                    copy.start()

        dispatch(0)
        for step in range(1, groups):
            group_copy(dall, 1, step).wait()
        draft = joined(dall)
        scores = lax.dot_general(
            queries, draft, (((1,), (1,)), ((), ())), preferred_element_type=f32
        )
        row = lax.broadcasted_iota(jnp.int32, (rows, tokens), 0)
        col = lax.broadcasted_iota(jnp.int32, (rows, tokens), 1)
        seen = (lax.div(row, unit) == lax.div(col, DRAFT)) & (
            lax.rem(col, DRAFT) <= lax.rem(row, DRAFT)
        )
        masked = jnp.where(seen, scores, EMPTY)
        draft_peak = jnp.max(masked, axis=1, keepdims=True)
        weights = jnp.where(seen, jnp.exp(masked - draft_peak), 0.0)
        draft_total = jnp.sum(weights, axis=1, keepdims=True)
        draft_mix = jnp.dot(weights.astype(bf16), draft[:, :LATENT], preferred_element_type=f32)
        draft_mix = draft_mix / draft_total
        draft_log = draft_peak + jnp.log(draft_total)

        every = range(slots)

        def attend_all(p):
            await_rows(p)
            attend(p, every)
            give_back(p)

        loads[3].wait()
        await_rows(0)
        attend(0, every)
        for half in range(HALVES):
            relay(half)
        if planes == 4:
            dispatch(2)
            dispatch(3)
            attend_all(2)
            dispatch(1)
            attend_all(3)
            merge_plane(2)
            attend_all(1)
            give_back(0)
            merge_plane(3)
            merge_plane(1)
            merge_plane(0)
        else:
            give_back(0)
            dispatch(1)
            merge_plane(0)
            attend_all(1)
            merge_plane(1)

        for s in range(1, planes):
            for copy in y_copy(s):
                copy.wait_recv()
        wide = planes * rows
        log = jnp.concatenate([zlg[s][...] for s in range(planes)], axis=1)
        lane = lax.broadcasted_iota(jnp.int32, (1, wide), 1)
        line = lax.broadcasted_iota(jnp.int32, (rows, 1), 0)
        match = lax.rem(lane, rows) == line
        picked = jnp.where(match, log, EMPTY)
        top = jnp.maximum(jnp.max(picked, axis=1, keepdims=True), draft_log)
        weights = jnp.where(match, jnp.exp(picked - top), 0.0)
        own = jnp.exp(draft_log - top)
        total = jnp.sum(weights, axis=1, keepdims=True) + own
        block = jnp.concatenate([zmg[s][...] for s in range(planes)], axis=0)
        summed = split_dot(weights, block) + own * draft_mix
        attended = (summed / total).astype(bf16)
        row = lax.broadcasted_iota(jnp.int32, (rows, rows), 0)
        col = lax.broadcasted_iota(jnp.int32, (rows, rows), 1)
        rank = lax.rem(row, tokens)
        share = planes * own_tokens
        line = lax.rem(lax.div(rank, own_tokens), planes) * 2 + lax.rem(lax.div(rank, share), 2)
        token = lax.div(rank, 2 * share) * home_tokens + line * own_tokens
        token = token + lax.rem(rank, own_tokens)
        spot = lax.div(token, DRAFT) * unit + lax.div(row, tokens) * DRAFT + lax.rem(token, DRAFT)
        order = jnp.where(col == spot, 1.0, 0.0).astype(bf16)
        attended = jnp.dot(order, attended, preferred_element_type=f32).astype(bf16)
        loads[4].wait()
        loads[5].wait()
        values = [
            jnp.dot(attended[h * tokens : (h + 1) * tokens], wuv[h], preferred_element_type=f32)
            for h in range(heads)
        ]
        values = jnp.concatenate(values, axis=1).astype(bf16)

        def r_copy(n, to, source):
            return remote(
                parts.at[n, to], partg.at[n, source], r_send.at[n, to], r_recv.at[n, source],
                *plane_device(to),
            )

        def project(n, carry):
            span = pl.ds(pl.multiple_of(n * cut, 128), cut)
            part = jnp.dot(values, wo[:, span], preferred_element_type=f32)
            for j in range(around):
                parts[n, j] = part[j * share : (j + 1) * share].astype(bf16)

            def send(step, carry):
                r_copy(n, plane_peer(step), me).start()
                return carry

            lax.fori_loop(1, around, send, 0)
            partg[n, me] = parts[n, me]
            return carry

        lax.fori_loop(0, CHUNKS, project, 0)

        def lane_span(n):
            return pl.ds(pl.multiple_of(n * cut, 128), cut)

        def f_copy(n, to, source):
            return remote(
                fin.at[n, to], out.at[source, :, lane_span(n)], f_send.at[n, to], f_recv.at[n, source],
                g, to * 2 + c,
            )

        def gather(n, carry):
            def arrive(step, carry):
                source = plane_peer(step)
                r_copy(n, source, source).wait_recv()
                return carry

            lax.fori_loop(1, around, arrive, 0)
            summed = partg[n, 0].astype(f32)
            for j in range(1, around):
                summed = summed + partg[n, j].astype(f32)
            for t in range(planes):
                fin[n, t] = summed[t * own_tokens : (t + 1) * own_tokens].astype(bf16)
            for step in range(1, planes):
                f_copy(n, lax.rem(z + step, planes), z).start()
            out[z, :, lane_span(n)] = fin[n, z]
            return carry

        lax.fori_loop(0, CHUNKS, gather, 0)

        for n in range(CHUNKS):
            for step in range(1, planes):
                source = lax.rem(z + step, planes)
                f_copy(n, source, source).wait_recv()

        for s in range(1, planes):
            for half in range(HALVES):
                for copy in z_copies(s, half):
                    copy.wait_send()
            for copy in y_copy(s):
                copy.wait_send()

        def finish(step, carry):
            to = plane_peer(step)
            for s in range(planes):
                p_copy(s, to, me).wait_send()
                for copy in b_copies(s, to, me):
                    copy.wait_send()
            return carry

        lax.fori_loop(1, around, finish, 0)

        def finish_chunk(n, carry):
            for step in range(1, around):
                r_copy(n, plane_peer(step), me).wait_send()
            for step in range(1, planes):
                f_copy(n, lax.rem(z + step, planes), z).wait_send()
            return carry

        lax.fori_loop(0, CHUNKS, finish_chunk, 0)

    smem = pl.BlockSpec(memory_space=pltpu.SMEM)
    vmem = pl.BlockSpec(memory_space=pltpu.VMEM)
    hbm = pl.BlockSpec(memory_space=pl.ANY)
    scratch = [
        pltpu.VMEM((groups, home_tokens, q_rank), bf16),
        pltpu.VMEM((groups, home_tokens, key_width), bf16),
        pltpu.VMEM((q_rank, nope_cols), bf16),
        pltpu.VMEM((q_rank, rope_cols), bf16),
        pltpu.VMEM((heads, NOPE, LATENT), bf16),
        pltpu.VMEM((heads, LATENT, VDIM), bf16),
        pltpu.VMEM((out_rows, width), bf16),
        pltpu.VMEM((slots, key_width, slab_length), bf16),
    ]
    shapes = [
        ((seqs, tiles, unit, 128), bf16),
        ((seqs // 2, unit, 128), bf16),
        ((2, seqs, unit, 128), bf16),
        ((around, all_tiles, unit, 128), bf16),
        ((around, all_tiles, unit, 128), bf16),
        ((around, slots, unit, LATENT), bf16),
        ((around, slots, unit, LATENT), bf16),
        ((around, slots, 128), f32),
        ((around, slots, 128), f32),
    ]
    scratch += [pltpu.VMEM(*shape) for shape in shapes for _ in range(planes)]
    scratch += [pltpu.VMEM((rows, LATENT), bf16) for _ in range(2 * planes)]
    scratch += [pltpu.VMEM((1, rows), f32) for _ in range(2 * planes)]
    scratch += [pltpu.VMEM((CHUNKS, around, planes * own_tokens, cut), bf16) for _ in range(2)]
    scratch += [pltpu.VMEM((CHUNKS, planes, own_tokens, cut), bf16)]
    dma = pltpu.SemaphoreType.DMA
    scratch += [
        dma((8,)),
        dma((2, groups)), dma((2, groups)),
        dma((2, planes, HALVES)), dma((2, planes, HALVES)),
        dma((planes, around)), dma((planes, around)),
        dma((planes, 2, around)), dma((planes, 2, around)),
        dma((2, planes)), dma((2, planes)),
        dma((CHUNKS, around)), dma((CHUNKS, around)),
        dma((CHUNKS, planes)), dma((CHUNKS, planes)),
    ]
    terms = pl.pallas_call(
        body,
        out_shape=jax.ShapeDtypeStruct((planes, own_tokens, width), bf16),
        in_specs=[smem] * 3 + [hbm] * 8,
        out_specs=vmem,
        scratch_shapes=scratch,
        compiler_params=pltpu.CompilerParams(
            collective_id=0, has_side_effects=True, vmem_limit_bytes=56 * 1024 * 1024
        ),
        name="fused",
    )(
        context_length, jnp.swapaxes(slot_sequence, 1, 2), jnp.swapaxes(slot_slab, 1, 2),
        q_compressed, draft_kv, w_q_nope, w_q_rope, w_uk, w_uv, w_o, keys_hbm,
    )
    return jnp.sum(terms.astype(f32), axis=0)


def shards(
    q_compressed, w_q_nope, w_q_rope, w_uk, w_uv, w_o, kv_cache, draft_kv,
    context_length, slot_sequence, slot_slab,
):
    args = (
        q_compressed, w_q_nope, w_q_rope, w_uk, w_uv, w_o, kv_cache, draft_kv,
        context_length, slot_sequence, slot_slab,
    )
    groups, count = lax.axis_size("group"), lax.axis_size("dev")
    heads = w_uk.shape[0] // groups
    fits = (
        w_uk.shape[0] % groups == 0
        and count % 2 == 0
        and count // 2 in PLANES
        and q_compressed.shape[0] % count == 0
        and groups * q_compressed.shape[0] // DRAFT % (2 * HALVES) == 0
        and kv_cache.shape[2] % 2 == 0
        and heads * DRAFT == 16
        and w_o.shape[1] % (128 * CHUNKS) == 0
    )
    if not fits:
        return shards_general(*args)
    keys = jnp.swapaxes(kv_cache[0, 0], 1, 2)
    return fused(
        q_compressed, w_q_nope, w_q_rope, w_uk, w_uv, w_o, keys, draft_kv,
        context_length, slot_sequence, slot_slab,
    )


def solution(mesh):
    placed = (
        P("group", None),
        P(None, "dev"),
        P(None, "dev"),
        P("dev", None, None),
        P("dev", None, None),
        P("dev", None),
        P("group", "dev", None, None, None),
        P("group", None),
        P(),
        P(),
        P(),
    )
    return jax.shard_map(
        shards, mesh=mesh, in_specs=placed, out_specs=P(("group", "dev"), None), check_vma=False
    )
```

```python
import jax
import jax.numpy as jnp
from jax import lax
from jax.experimental import pallas as pl
from jax.experimental.pallas import tpu as pltpu
from jax.sharding import PartitionSpec as P

NOPE = 128
ROPE = 64
LATENT = 512
VDIM = 128
DRAFT = 4


EMPTY = -1e30


def exchange(axis, call_id, *blocks):
    count = lax.axis_size(axis)
    number = len(blocks)

    def body(*refs):
        sent, got = refs[:number], refs[number : 2 * number]
        send_sems, recv_sems, local_sems = refs[2 * number :]
        me = lax.axis_index(axis)
        barrier = pltpu.get_barrier_semaphore()
        for step in range(1, count):
            pl.semaphore_signal(
                barrier,
                inc=1,
                device_id={axis: lax.rem(me + step, count)},
                device_id_type=pl.DeviceIdType.MESH,
            )
        pl.semaphore_wait(barrier, count - 1)
        started = []
        for step in range(1, count):
            peer = lax.rem(me + step, count)
            for which in range(number):
                copy = pltpu.make_async_remote_copy(
                    src_ref=sent[which].at[peer],
                    dst_ref=got[which].at[me],
                    send_sem=send_sems.at[which, step],
                    recv_sem=recv_sems.at[which, step],
                    device_id={axis: peer},
                    device_id_type=pl.DeviceIdType.MESH,
                )
                copy.start()
                started.append(copy)
        own = []
        for which in range(number):
            copy = pltpu.make_async_copy(
                sent[which].at[me], got[which].at[me], local_sems.at[which]
            )
            copy.start()
            own.append(copy)
        for copy in own:
            copy.wait()
        for copy in started:
            copy.wait()

    vmem = pl.BlockSpec(memory_space=pltpu.VMEM)
    return pl.pallas_call(
        body,
        out_shape=tuple(jax.ShapeDtypeStruct(block.shape, block.dtype) for block in blocks),
        in_specs=[vmem] * number,
        out_specs=tuple([vmem] * number),
        scratch_shapes=[
            pltpu.SemaphoreType.DMA((number, count)),
            pltpu.SemaphoreType.DMA((number, count)),
            pltpu.SemaphoreType.DMA((number,)),
        ],
        compiler_params=pltpu.CompilerParams(
            collective_id=call_id, has_side_effects=True, vmem_limit_bytes=8 * 1024 * 1024
        ),
        name="exchange_%d" % call_id,
    )(*blocks)


def exchange_partials(axis, call_id, block_log, block_mix):
    count = lax.axis_size(axis)
    flat_log = block_log.reshape(count, 1, -1)
    width = flat_log.shape[2]
    padded = -(-width // 128) * 128
    flat_log = jnp.pad(flat_log, ((0, 0), (0, 0), (0, padded - width)))
    flat_mix = block_mix.astype(jnp.bfloat16).reshape(count, -1, block_mix.shape[-1])
    got_log, got_mix = exchange(axis, call_id, flat_log, flat_mix)
    return (
        got_log[:, :, :width].reshape(block_log.shape),
        got_mix.reshape(block_mix.shape).astype(jnp.float32),
    )


def attend_slots(call_id, every_seq, cache_slots, context_length, slot_sequence, slot_slab):
    count = lax.axis_size("dev")
    slot_count, key_width, slab_length = cache_slots.shape
    seq_total, rows, _ = every_seq.shape
    chunk = min(count, max(1, 128 // rows))
    while count % chunk:
        chunk -= 1
    steps = count // chunk
    lanes = -(-rows // 128) * 128
    log_rows = -(-slot_count // 8) * 8

    def body(
        lengths, owners, slabs, every, cache, got_log, got_mix,
        staged, arrived, keys, log_stage, mix_stage,
        key_sems, send_sems, arrive_sems, back_send, back_recv,
    ):
        group = lax.axis_index("group")
        me = lax.axis_index("dev")
        barrier = pltpu.get_barrier_semaphore()

        def greet(step, carry):
            pl.semaphore_signal(
                barrier,
                inc=1,
                device_id={"dev": lax.rem(me + step, count)},
                device_id_type=pl.DeviceIdType.MESH,
            )
            return carry

        lax.fori_loop(1, count, greet, 0)
        for slot in range(slot_count):
            pltpu.make_async_copy(cache.at[slot], keys.at[slot], key_sems.at[slot]).start()
        pl.semaphore_wait(barrier, count - 1)

        def row_copy(peer, source):
            return pltpu.make_async_remote_copy(
                src_ref=staged.at[peer],
                dst_ref=arrived.at[source],
                send_sem=send_sems.at[peer],
                recv_sem=arrive_sems.at[source],
                device_id={"dev": peer},
                device_id_type=pl.DeviceIdType.MESH,
            )

        def back_copies(peer, source):
            return [
                pltpu.make_async_remote_copy(
                    src_ref=stage.at[peer],
                    dst_ref=target.at[source],
                    send_sem=back_send.at[which, peer],
                    recv_sem=back_recv.at[which, source],
                    device_id={"dev": peer},
                    device_id_type=pl.DeviceIdType.MESH,
                )
                for which, (stage, target) in enumerate([(log_stage, got_log), (mix_stage, got_mix)])
            ]

        def send_rows(step, carry):
            peer = lax.rem(me + step, count)
            for slot in range(slot_count):
                owner = jnp.maximum(owners[group, peer, slot], 0)
                staged[peer, slot] = every[owner]
            row_copy(peer, me).start()
            return carry

        lax.fori_loop(1, count, send_rows, 0)
        limits = []
        for slot in range(slot_count):
            owner = owners[group, me, slot]
            arrived[me, slot] = every[jnp.maximum(owner, 0)]
            left = lengths[jnp.maximum(owner, 0)] - slabs[group, me, slot] * slab_length
            limits.append(jnp.where(owner >= 0, left, 0))
        for slot in range(slot_count):
            pltpu.make_async_copy(cache.at[slot], keys.at[slot], key_sems.at[slot]).wait()

        def one_step(step, carry):
            first = lax.rem(me // chunk + steps - step, steps) * chunk
            for at in range(chunk):
                source = first + at

                @pl.when(source != me)
                def _():
                    row_copy(source, source).wait_recv()

            for slot in range(slot_count):
                block = arrived[pl.ds(first, chunk), slot].reshape(chunk * rows, key_width)
                scores = lax.dot_general(
                    block, keys[slot], (((1,), (0,)), ((), ())), preferred_element_type=jnp.float32
                )
                place = lax.broadcasted_iota(jnp.int32, (1, slab_length), 1)
                is_valid = place < limits[slot]
                masked = jnp.where(is_valid, scores, EMPTY)
                peak = jnp.max(masked, axis=1, keepdims=True)
                weights = jnp.where(is_valid, jnp.exp(masked - peak), 0.0)
                total = jnp.maximum(jnp.sum(weights, axis=1, keepdims=True), 1.0)
                mixture = lax.dot_general(
                    weights.astype(jnp.bfloat16),
                    keys[slot, :LATENT],
                    (((1,), (1,)), ((), ())),
                    preferred_element_type=jnp.float32,
                )
                log = jnp.broadcast_to(peak + jnp.log(total), (chunk * rows, 128))
                mix = (mixture / total).astype(jnp.bfloat16).reshape(chunk, rows, LATENT)
                for at in range(chunk):
                    mix_stage[first + at, slot] = mix[at]
                    turned = jnp.transpose(log[at * rows : (at + 1) * rows])
                    log_stage[first + at, slot : slot + 1, :rows] = turned[:1]
            for at in range(chunk):
                source = first + at

                @pl.when(source != me)
                def _():
                    for copy in back_copies(source, me):
                        copy.start()

            return carry

        lax.fori_loop(0, steps, one_step, 0)
        got_log[me] = log_stage[me]
        got_mix[me] = mix_stage[me]

        def finish(step, carry):
            peer = lax.rem(me + step, count)
            row_copy(peer, peer).wait_send()
            for copy in back_copies(peer, peer):
                copy.wait_send()
                copy.wait_recv()
            return carry

        lax.fori_loop(1, count, finish, 0)

    smem = pl.BlockSpec(memory_space=pltpu.SMEM)
    vmem = pl.BlockSpec(memory_space=pltpu.VMEM)
    log_shape = (count, log_rows, lanes)
    mix_shape = (count, slot_count, rows, LATENT)
    got_log, got_mix = pl.pallas_call(
        body,
        out_shape=(
            jax.ShapeDtypeStruct(log_shape, jnp.float32),
            jax.ShapeDtypeStruct(mix_shape, jnp.bfloat16),
        ),
        in_specs=[smem, smem, smem, vmem, pl.BlockSpec(memory_space=pl.ANY)],
        out_specs=(vmem, vmem),
        scratch_shapes=[
            pltpu.VMEM((count, slot_count, rows, key_width), jnp.bfloat16),
            pltpu.VMEM((count, slot_count, rows, key_width), jnp.bfloat16),
            pltpu.VMEM((slot_count, key_width, slab_length), jnp.bfloat16),
            pltpu.VMEM(log_shape, jnp.float32),
            pltpu.VMEM(mix_shape, jnp.bfloat16),
            pltpu.SemaphoreType.DMA((slot_count,)),
            pltpu.SemaphoreType.DMA((count,)),
            pltpu.SemaphoreType.DMA((count,)),
            pltpu.SemaphoreType.DMA((2, count)),
            pltpu.SemaphoreType.DMA((2, count)),
        ],
        compiler_params=pltpu.CompilerParams(
            collective_id=call_id, has_side_effects=True, vmem_limit_bytes=24 * 1024 * 1024
        ),
        name="attend_slots",
    )(
        context_length,
        slot_sequence,
        slot_slab,
        every_seq,
        cache_slots,
    )
    return got_log[:, :slot_count, :rows], got_mix.astype(jnp.float32)


def merge_blocks(block_log, block_out, block_owner, own_log, own_out):
    owners_count = own_log.shape[0]
    matches = block_owner[None, :] == jnp.arange(owners_count, dtype=jnp.int32)[:, None]
    picked = jnp.where(matches[:, :, None, None], block_log[None], EMPTY)
    top_log = jnp.maximum(jnp.max(picked, axis=1), own_log)
    weights = jnp.where(matches[:, :, None, None], jnp.exp(picked - top_log[:, None]), 0.0)
    own_weight = jnp.exp(own_log - top_log)
    weight_sum = jnp.sum(weights, axis=1) + own_weight
    summed = jnp.einsum("sbtx,btxl->stxl", weights, block_out, precision=lax.Precision.HIGHEST)
    summed = summed + own_weight[..., None] * own_out
    return (top_log + jnp.log(weight_sum), summed / weight_sum[..., None])


def draft_partials(queries_seq, draft_rows):
    scores = jnp.einsum(
        "sthk,suk->sthu", queries_seq, draft_rows, preferred_element_type=jnp.float32
    )
    causal = jnp.arange(DRAFT)[None, :] <= jnp.arange(DRAFT)[:, None]
    masked = jnp.where(causal[None, :, None, :], scores, EMPTY)
    draft_peak = jnp.max(masked, axis=3)
    weights = jnp.where(causal[None, :, None, :], jnp.exp(masked - draft_peak[..., None]), 0.0)
    draft_total = jnp.sum(weights, axis=3)
    mixture = jnp.einsum(
        "sthu,sul->sthl",
        weights.astype(jnp.bfloat16),
        draft_rows[..., :LATENT],
        preferred_element_type=jnp.float32,
    )
    return (draft_peak + jnp.log(draft_total), mixture / draft_total[..., None])


def shards_general(
    q_compressed,
    w_q_nope,
    w_q_rope,
    w_uk,
    w_uv,
    w_o,
    kv_cache,
    draft_kv,
    context_length,
    slot_sequence,
    slot_slab,
):
    group_count = lax.axis_size("group")
    holder_count = lax.axis_size("dev")
    group_index = lax.axis_index("group")
    token_count = q_compressed.shape[0]
    seq_group = token_count // DRAFT
    heads_here = w_uk.shape[0]
    key_width = LATENT + ROPE
    q_nope = jnp.dot(q_compressed, w_q_nope, preferred_element_type=jnp.float32).astype(
        jnp.bfloat16
    )
    q_nope = q_nope.reshape(token_count, heads_here, NOPE)
    q_rope = jnp.dot(q_compressed, w_q_rope, preferred_element_type=jnp.float32).reshape(
        token_count, heads_here, ROPE
    )
    absorbed = jnp.einsum("thn,hnl->thl", q_nope, w_uk, preferred_element_type=jnp.float32)
    queries = (jnp.concatenate([absorbed, q_rope], axis=2) * (NOPE + ROPE) ** (-0.5)).astype(
        jnp.bfloat16
    )
    queries_seq = queries.reshape(seq_group, DRAFT, heads_here, key_width)
    draft_log, draft_mix = draft_partials(
        queries_seq, draft_kv.reshape(seq_group, DRAFT, key_width)
    )
    group_table = lax.dynamic_index_in_dim(slot_sequence, group_index, 0, keepdims=False)
    outgoing = jnp.broadcast_to(
        queries_seq.reshape(1, -1, key_width), (group_count, token_count * heads_here, key_width)
    )
    (gathered,) = exchange("group", 0, outgoing)
    back_log, back_mix = attend_slots(
        1,
        gathered.reshape(group_count * seq_group, DRAFT * heads_here, key_width),
        jnp.swapaxes(kv_cache[0, 0], 1, 2),
        context_length,
        slot_sequence,
        slot_slab,
    )
    seq_total = group_count * seq_group
    group_log, group_mix = merge_blocks(
        back_log.reshape(-1, DRAFT, heads_here),
        back_mix.reshape(-1, DRAFT, heads_here, LATENT),
        group_table.reshape(-1),
        jnp.full((seq_total, DRAFT, heads_here), EMPTY, jnp.float32),
        jnp.zeros((seq_total, DRAFT, heads_here, LATENT), jnp.float32),
    )
    home_log, home_mix = exchange_partials(
        "group",
        3,
        group_log.reshape(group_count, seq_group, DRAFT, heads_here),
        group_mix.reshape(group_count, seq_group, DRAFT, heads_here, LATENT),
    )
    home_owner = jnp.tile(jnp.arange(seq_group, dtype=jnp.int32), group_count)
    final_log, final_mix = merge_blocks(
        home_log.reshape(-1, DRAFT, heads_here),
        home_mix.reshape(-1, DRAFT, heads_here, LATENT),
        home_owner,
        draft_log,
        draft_mix,
    )
    attended = final_mix.astype(jnp.bfloat16).reshape(token_count, heads_here, LATENT)
    head_values = jnp.einsum("thl,hlv->thv", attended, w_uv, preferred_element_type=jnp.float32)
    head_values = head_values.astype(jnp.bfloat16).reshape(token_count, heads_here * VDIM)
    partial = jnp.dot(head_values, w_o, preferred_element_type=jnp.float32)
    (terms,) = exchange(
        "dev", 4, partial.reshape(holder_count, token_count // holder_count, -1)
    )
    return jnp.sum(terms, axis=0)


PLANES = (2, 4)
HALVES = 2
CHUNKS = 4
VMEM_LIMIT = 56 * 1024 * 1024


def flip(value, mask, extent):
    result, bit = 0, 1
    while bit < extent:
        own = lax.rem(lax.div(value, bit), 2)
        result = result + bit * (1 - own if mask & bit else own)
        bit *= 2
    return result


def fused(
    q_compressed, w_q_nope, w_q_rope, w_uk, w_uv, w_o, keys_hbm, draft_kv,
    context_length, slot_sequence, slot_slab,
):
    groups, count = lax.axis_size("group"), lax.axis_size("dev")
    planes = count // 2
    around = groups * 2
    home_tokens, q_rank = q_compressed.shape
    tokens = groups * home_tokens
    seqs = tokens // DRAFT
    heads = w_uk.shape[0] // groups
    unit = heads * DRAFT
    rows = seqs * unit
    slots, key_width, slab_length = keys_hbm.shape
    width = w_o.shape[1]
    nope_cols, rope_cols, out_rows = heads * NOPE, heads * ROPE, heads * VDIM
    cut = width // CHUNKS
    own_tokens = home_tokens // count
    bf16, f32 = jnp.bfloat16, jnp.float32
    tiles = LATENT // 128
    all_tiles = slots * tiles + slots // 2

    def body(
        lengths, owners, slabs, qc, dkv, wqn_hbm, wqr_hbm, wuk_hbm, wuv_hbm, wo_hbm, cache, out,
        qall, dall, wqn, wqr, wuk, wuv, wo, keys, *rest,
    ):
        rest = list(rest)
        take = lambda n: [rest.pop(0) for _ in range(n)]
        lat, rot, sided, staged, arrived, mixs, mixg, logs, logg = (take(planes) for _ in range(9))
        zms, zmg, zls, zlg = (take(planes) for _ in range(4))
        parts, partg, fin = take(3)
        (
            local, g_send, g_recv, z_send, z_recv, p_send, p_recv, b_send, b_recv,
            y_send, y_recv, r_send, r_recv, f_send, f_recv,
        ) = rest
        g = lax.axis_index("group")
        d = lax.axis_index("dev")
        z, c = lax.div(d, 2), lax.rem(d, 2)
        me = g * 2 + c

        def remote(src, dst, send, recv, to_g, to_d):
            return pltpu.make_async_remote_copy(
                src_ref=src, dst_ref=dst, send_sem=send, recv_sem=recv,
                device_id=(to_g, to_d), device_id_type=pl.DeviceIdType.MESH,
            )

        def plane_peer(step):
            return lax.rem(me + step, around)

        def plane_device(j):
            return lax.div(j, 2), z * 2 + lax.rem(j, 2)

        columns = lambda size: pl.ds(pl.multiple_of(g * size, size), size)
        early = [
            pltpu.make_async_copy(qc, qall.at[g], local.at[6]),
            pltpu.make_async_copy(dkv, dall.at[g], local.at[7]),
        ]
        for copy in early:
            copy.start()
        loads = [
            pltpu.make_async_copy(wqn_hbm.at[:, columns(nope_cols)], wqn, local.at[0]),
            pltpu.make_async_copy(wqr_hbm.at[:, columns(rope_cols)], wqr, local.at[1]),
            pltpu.make_async_copy(wuk_hbm.at[pl.ds(g * heads, heads)], wuk, local.at[2]),
            pltpu.make_async_copy(cache, keys, local.at[3]),
            pltpu.make_async_copy(wuv_hbm.at[pl.ds(g * heads, heads)], wuv, local.at[4]),
            pltpu.make_async_copy(wo_hbm.at[columns(out_rows)], wo, local.at[5]),
        ]
        for copy in loads:
            copy.start()

        barrier = pltpu.get_barrier_semaphore()

        def greet(to_g, to_d):
            pl.semaphore_signal(
                barrier, inc=1, device_id=(to_g, to_d), device_id_type=pl.DeviceIdType.MESH
            )

        for step in range(1, around):
            greet(*plane_device(plane_peer(step)))
        for step in range(1, planes):
            greet(g, lax.rem(z + step, planes) * 2 + c)
        pl.semaphore_wait(barrier, around + planes - 2)

        def group_copy(ref, which, step):
            to = lax.rem(g + step, groups)
            return remote(
                ref.at[g], ref.at[g], g_send.at[which], g_recv.at[which], to, d
            )

        def group_wait(ref, which):
            most = ref.at[pl.ds(0, groups - 1)]
            remote(
                most, most, g_send.at[which], g_recv.at[which], lax.rem(g + 1, groups), d
            ).wait()

        for which, ref in enumerate((qall, dall)):
            early[which].wait()
            for step in reversed(range(1, groups)):
                group_copy(ref, which, step).start()
        group_wait(qall, 0)

        def joined(ref):
            pieces = [ref[i].astype(f32) for i in range(groups)]
            return jnp.concatenate(pieces, axis=0).astype(bf16)

        q_tokens = joined(qall)
        for copy in loads[:3]:
            copy.wait()
        nope = jnp.dot(q_tokens, wqn[...], preferred_element_type=f32).astype(bf16)
        rope = jnp.dot(q_tokens, wqr[...], preferred_element_type=f32)
        by_head = []
        for h in range(heads):
            absorbed = jnp.dot(
                nope[:, h * NOPE : (h + 1) * NOPE], wuk[h], preferred_element_type=f32
            )
            pair = jnp.concatenate([absorbed, rope[:, h * ROPE : (h + 1) * ROPE]], axis=1)
            by_head.append((pair * (NOPE + ROPE) ** (-0.5)).astype(bf16))
        stacked = jnp.concatenate(by_head, axis=0)
        row = lax.broadcasted_iota(jnp.int32, (rows, rows), 0)
        col = lax.broadcasted_iota(jnp.int32, (rows, rows), 1)
        spot = lax.rem(lax.div(row, DRAFT), heads) * tokens
        spot = spot + lax.div(row, unit) * DRAFT + lax.rem(row, DRAFT)
        order = jnp.where(col == spot, 1.0, 0.0).astype(bf16)
        queries = jnp.dot(order, stacked, preferred_element_type=f32).astype(bf16)
        for i in range(tiles):
            lat[0][:, i] = queries[:, i * 128 : (i + 1) * 128].reshape(seqs, unit, 128)
        turned = queries[:, LATENT:].astype(f32)
        for i in range(seqs // 2):
            halves = [turned[(2 * i + j) * unit : (2 * i + j + 1) * unit] for j in range(2)]
            rot[0][i] = jnp.concatenate(halves, axis=1).astype(bf16)

        def z_copies(s, half):
            relay = s & 1 and s > 1
            copies = []
            for which, ref in enumerate((lat, rot)):
                source, over = (ref[s ^ 1], 1) if relay else (ref[0], s)
                size = seqs // HALVES // (1 + which)
                span = pl.ds(half * size, size)
                copies.append(
                    remote(
                        source.at[span], ref[s].at[span], z_send.at[which, s, half],
                        z_recv.at[which, s, half], g, flip(z, over, planes) * 2 + c,
                    )
                )
            return copies

        for half in range(HALVES):
            for s in reversed(range(1, planes)):
                if not (s & 1 and s > 1):
                    for copy in z_copies(s, half):
                        copy.start()

        def p_copy(s, to, source):
            return remote(
                staged[s].at[to], arrived[s].at[source], p_send.at[s], p_recv.at[s],
                *plane_device(to),
            )

        most = pl.ds(0, around - 1)
        next_device = plane_device(plane_peer(1))

        def p_whole(s):
            return remote(
                staged[s].at[most], arrived[s].at[most], p_send.at[s], p_recv.at[s], *next_device
            )

        def b_whole(p):
            return [
                remote(
                    stage.at[most], target.at[most], b_send.at[p, which], b_recv.at[p, which],
                    *next_device,
                )
                for which, (stage, target) in enumerate(((mixs[p], mixg[p]), (logs[p], logg[p])))
            ]

        lane_of = lax.broadcasted_iota(jnp.int32, (unit, 128), 1)

        def spread(s):
            for i in range(seqs // 2):
                tile = rot[s][i].astype(f32)
                swapped = jnp.concatenate([tile[:, ROPE:], tile[:, :ROPE]], axis=1).astype(bf16)
                for side in range(2):
                    sided[s][side, 2 * i + side] = rot[s][i]
                    sided[s][side, 2 * i + 1 - side] = swapped

        def pack(dest, at, s, chosen):
            for k in range(slots):
                dest[at, k * tiles : (k + 1) * tiles] = lat[s][chosen[k]]
            for k in range(0, slots, 2):
                sides = [sided[s][side, chosen[k + side]].astype(f32) for side in range(2)]
                both = jnp.where(lane_of < ROPE, sides[0], sides[1])
                dest[at, slots * tiles + k // 2] = both.astype(bf16)

        def dispatch(s):
            if s > 0 and (s % 2 == 1 or s + 1 == planes):
                for half in range(HALVES):
                    for copy in z_copies(s, half):
                        copy.wait_recv()

            spread(s)
            for step in range(1, around):
                to = plane_peer(step)
                to_g, to_d = plane_device(to)
                chosen = [jnp.maximum(owners[to_g, k, to_d], 0) for k in range(slots)]
                pack(staged[s], to, s, chosen)

            def send(step, carry):
                p_copy(s, plane_peer(step), me).start()
                return carry

            lax.fori_loop(1, around, send, 0)
            pack(arrived[s], me, s, [jnp.maximum(owners[g, k, d], 0) for k in range(slots)])

        def b_copies(p, to, source):
            return [
                remote(
                    stage.at[to], target.at[source], b_send.at[p, which],
                    b_recv.at[p, which], *plane_device(to),
                )
                for which, (stage, target) in enumerate(((mixs[p], mixg[p]), (logs[p], logg[p])))
            ]

        def await_rows(p):
            p_whole(p).wait_recv()

        def attend(p, chosen):
            total_rows = around * unit
            position = lax.broadcasted_iota(jnp.int32, (1, slab_length), 1)
            scored = []
            for k in chosen:
                owner = owners[g, k, d]
                left = lengths[jnp.maximum(owner, 0)] - slabs[g, k, d] * slab_length
                cells = [arrived[p][:, k * tiles + i] for i in range(tiles)]
                cells = [cell.reshape(total_rows, 128) for cell in cells]
                turned = arrived[p][:, slots * tiles + k // 2].reshape(total_rows, 128)
                side = k % 2 * ROPE
                block = jnp.concatenate(cells + [turned[:, side : side + ROPE]], axis=1)
                scores = lax.dot_general(
                    block, keys[k], (((1,), (0,)), ((), ())), preferred_element_type=f32
                )
                scored.append((k, scores, position < jnp.where(owner >= 0, left, 0)))
            weighed = []
            for k, scores, is_valid in scored:
                masked = jnp.where(is_valid, scores, EMPTY)
                peak = jnp.max(masked, axis=1, keepdims=True)
                weights = jnp.where(is_valid, jnp.exp(masked - peak), 0.0)
                total = jnp.maximum(jnp.sum(weights, axis=1, keepdims=True), 1.0)
                weighed.append((k, weights.astype(bf16), peak, total))
            for k, weights, peak, total in weighed:
                mixture = lax.dot_general(
                    weights, keys[k, :LATENT], (((1,), (1,)), ((), ())),
                    preferred_element_type=f32,
                )
                mixs[p][:, k] = (mixture / total).astype(bf16).reshape(around, unit, LATENT)
                log = jnp.broadcast_to(peak + jnp.log(total), (total_rows, 128))
                log = jnp.transpose(log)[:1]
                for j in range(around):
                    logs[p][j, k : k + 1, :unit] = log[:, j * unit : (j + 1) * unit]

        def give_back(p):
            def send(step, carry):
                for copy in b_copies(p, plane_peer(step), me):
                    copy.start()
                return carry

            lax.fori_loop(1, around, send, 0)
            mixg[p][me] = mixs[p][me]
            logg[p][me] = logs[p][me]

        def split_dot(weights, block):
            high = weights.astype(bf16)
            low = (weights - high.astype(f32)).astype(bf16)
            return jnp.dot(high, block, preferred_element_type=f32) + jnp.dot(
                low, block, preferred_element_type=f32
            )

        def y_copy(s):
            to = flip(z, s, planes) * 2 + c
            return [
                remote(zms[s], zmg[s], y_send.at[0, s], y_recv.at[0, s], g, to),
                remote(zls[s], zlg[s], y_send.at[1, s], y_recv.at[1, s], g, to),
            ]

        def column_of(s):
            lane = lax.broadcasted_iota(jnp.int32, (rows, rows), 1)
            line = lax.broadcasted_iota(jnp.int32, (rows, rows), 0)
            return jnp.max(jnp.where(lane == line, zlg[s][...], EMPTY), axis=1, keepdims=True)

        def merge_plane(p):
            per = unit
            blocks = around * slots

            for copy in b_whole(p):
                copy.wait_recv()
            wide = blocks * per
            cells = [logg[p][j, k : k + 1, :per] for j in range(around) for k in range(slots)]
            log = jnp.concatenate(cells, axis=1)
            lane = lax.broadcasted_iota(jnp.int32, (1, wide), 1)
            owner = jnp.full((1, wide), -1, jnp.int32)
            for j in range(around):
                for k in range(slots):
                    here = owners[j // 2, k, z * 2 + j % 2]
                    owner = jnp.where(lax.div(lane, per) == j * slots + k, here, owner)
            tag = owner * per + lax.rem(lane, per)
            line = lax.broadcasted_iota(jnp.int32, (rows, 1), 0)
            match = tag == line
            picked = jnp.where(match, log, EMPTY)
            top = jnp.max(picked, axis=1, keepdims=True)
            weights = jnp.where(match, jnp.exp(picked - top), 0.0)
            total = jnp.maximum(jnp.sum(weights, axis=1, keepdims=True), 1.0)
            block = mixg[p][...].reshape(wide, LATENT)
            mixed = (split_dot(weights, block) / total).astype(bf16)
            logged = jnp.broadcast_to(top + jnp.log(total), (rows, 128))
            mix_to, log_to = (zms[p], zls[p]) if p > 0 else (zmg[p], zlg[p])
            mix_to[...] = mixed
            log_to[...] = jnp.transpose(logged)[:1]
            if p > 0:
                for copy in y_copy(p):
                    copy.start()

        def relay(half):
            for s in range(2, planes - 1, 2):
                for copy in z_copies(s, half):
                    copy.wait_recv()
                for copy in z_copies(s + 1, half):
                    copy.start()

        dispatch(0)
        group_wait(dall, 1)
        draft = joined(dall)
        scores = lax.dot_general(
            queries, draft, (((1,), (1,)), ((), ())), preferred_element_type=f32
        )
        row = lax.broadcasted_iota(jnp.int32, (rows, tokens), 0)
        col = lax.broadcasted_iota(jnp.int32, (rows, tokens), 1)
        seen = (lax.div(row, unit) == lax.div(col, DRAFT)) & (
            lax.rem(col, DRAFT) <= lax.rem(row, DRAFT)
        )
        masked = jnp.where(seen, scores, EMPTY)
        draft_peak = jnp.max(masked, axis=1, keepdims=True)
        weights = jnp.where(seen, jnp.exp(masked - draft_peak), 0.0)
        draft_total = jnp.sum(weights, axis=1, keepdims=True)
        draft_mix = jnp.dot(weights.astype(bf16), draft[:, :LATENT], preferred_element_type=f32)
        draft_mix = draft_mix / draft_total
        draft_log = draft_peak + jnp.log(draft_total)

        every = range(slots)

        def attend_only(p):
            await_rows(p)
            attend(p, every)

        def attend_all(p):
            attend_only(p)
            give_back(p)

        loads[3].wait()
        await_rows(0)
        attend(0, every)
        for half in range(HALVES):
            relay(half)
        if planes == 4:
            dispatch(2)
            dispatch(1)
            dispatch(3)
            attend_all(2)
            attend_all(1)
            attend_all(3)
            give_back(0)
            merge_plane(2)
            merge_plane(1)
            merge_plane(3)
            merge_plane(0)
        else:
            give_back(0)
            dispatch(1)
            merge_plane(0)
            attend_all(1)
            merge_plane(1)

        for s in range(planes):
            p_whole(s).wait_send()
            for copy in b_whole(s):
                copy.wait_send()
        for s in range(1, planes):
            for half in range(HALVES):
                for copy in z_copies(s, half):
                    copy.wait_send()

        all_planes = range(planes)
        for s in all_planes[1:]:
            for copy in y_copy(s):
                copy.wait_recv()
        tops = [column_of(s) for s in all_planes]
        top = draft_log
        for log in tops:
            top = jnp.maximum(top, log)
        total = jnp.exp(draft_log - top)
        summed = total * draft_mix
        for s in all_planes:
            weight = jnp.exp(tops[s] - top)
            total = total + weight
            summed = summed + weight * zmg[s][...].astype(f32)
        attended = (summed / total).astype(bf16)
        row = lax.broadcasted_iota(jnp.int32, (rows, rows), 0)
        col = lax.broadcasted_iota(jnp.int32, (rows, rows), 1)
        rank = lax.rem(row, tokens)
        share = planes * own_tokens
        line = lax.rem(lax.div(rank, own_tokens), planes) * 2 + lax.rem(lax.div(rank, share), 2)
        token = lax.div(rank, 2 * share) * home_tokens + line * own_tokens
        token = token + lax.rem(rank, own_tokens)
        spot = lax.div(token, DRAFT) * unit + lax.div(row, tokens) * DRAFT + lax.rem(token, DRAFT)
        order = jnp.where(col == spot, 1.0, 0.0).astype(bf16)
        attended = jnp.dot(order, attended, preferred_element_type=f32).astype(bf16)
        loads[4].wait()
        loads[5].wait()
        values = [
            jnp.dot(attended[h * tokens : (h + 1) * tokens], wuv[h], preferred_element_type=f32)
            for h in range(heads)
        ]
        values = jnp.concatenate(values, axis=1).astype(bf16)

        def r_copy(n, to, source):
            return remote(
                parts.at[n, to], partg.at[n, source], r_send.at[n], r_recv.at[n],
                *plane_device(to),
            )

        def r_whole(n):
            return remote(
                parts.at[n, most], partg.at[n, most], r_send.at[n], r_recv.at[n], *next_device
            )

        def project(n, carry):
            span = pl.ds(pl.multiple_of(n * cut, 128), cut)
            part = jnp.dot(values, wo[:, span], preferred_element_type=f32)
            for j in range(around):
                parts[n, j] = part[j * share : (j + 1) * share].astype(bf16)

            def send(step, carry):
                r_copy(n, plane_peer(step), me).start()
                return carry

            lax.fori_loop(1, around, send, 0)
            partg[n, me] = parts[n, me]
            return carry

        lax.fori_loop(0, CHUNKS, project, 0)

        def lane_span(n):
            return pl.ds(pl.multiple_of(n * cut, 128), cut)

        def f_copy(n, to, source):
            return remote(
                fin.at[n, to], out.at[source, :, lane_span(n)], f_send.at[n], f_recv.at[n],
                g, to * 2 + c,
            )

        def f_whole(n):
            rest = pl.ds(0, planes - 1)
            return remote(
                fin.at[n, rest], out.at[rest, :, lane_span(n)], f_send.at[n], f_recv.at[n],
                g, lax.rem(z + 1, planes) * 2 + c,
            )

        def gather(n, carry):
            r_whole(n).wait_recv()
            summed = partg[n, 0].astype(f32)
            for j in range(1, around):
                summed = summed + partg[n, j].astype(f32)
            for t in range(planes):
                fin[n, t] = summed[t * own_tokens : (t + 1) * own_tokens].astype(bf16)
            for step in range(1, planes):
                f_copy(n, lax.rem(z + step, planes), z).start()
            out[z, :, lane_span(n)] = fin[n, z]
            return carry

        lax.fori_loop(0, CHUNKS, gather, 0)

        for s in range(1, planes):
            for copy in y_copy(s):
                copy.wait_send()
        for n in range(CHUNKS):
            r_whole(n).wait_send()
            f_whole(n).wait_send()
        for n in range(CHUNKS):
            f_whole(n).wait_recv()

    smem = pl.BlockSpec(memory_space=pltpu.SMEM)
    vmem = pl.BlockSpec(memory_space=pltpu.VMEM)
    hbm = pl.BlockSpec(memory_space=pl.ANY)
    scratch = [
        pltpu.VMEM((groups, home_tokens, q_rank), bf16),
        pltpu.VMEM((groups, home_tokens, key_width), bf16),
        pltpu.VMEM((q_rank, nope_cols), bf16),
        pltpu.VMEM((q_rank, rope_cols), bf16),
        pltpu.VMEM((heads, NOPE, LATENT), bf16),
        pltpu.VMEM((heads, LATENT, VDIM), bf16),
        pltpu.VMEM((out_rows, width), bf16),
        pltpu.VMEM((slots, key_width, slab_length), bf16),
    ]
    shapes = [
        ((seqs, tiles, unit, 128), bf16),
        ((seqs // 2, unit, 128), bf16),
        ((2, seqs, unit, 128), bf16),
        ((around, all_tiles, unit, 128), bf16),
        ((around, all_tiles, unit, 128), bf16),
        ((around, slots, unit, LATENT), bf16),
        ((around, slots, unit, LATENT), bf16),
        ((around, slots, 128), f32),
        ((around, slots, 128), f32),
    ]
    scratch += [pltpu.VMEM(*shape) for shape in shapes for _ in range(planes)]
    scratch += [pltpu.VMEM((rows, LATENT), bf16) for _ in range(2 * planes)]
    scratch += [pltpu.VMEM((1, rows), f32) for _ in range(2 * planes)]
    scratch += [pltpu.VMEM((CHUNKS, around, planes * own_tokens, cut), bf16) for _ in range(2)]
    scratch += [pltpu.VMEM((CHUNKS, planes, own_tokens, cut), bf16)]
    dma = pltpu.SemaphoreType.DMA
    scratch += [
        dma((8,)),
        dma((2,)), dma((2,)),
        dma((2, planes, HALVES)), dma((2, planes, HALVES)),
        dma((planes,)), dma((planes,)),
        dma((planes, 2)), dma((planes, 2)),
        dma((2, planes)), dma((2, planes)),
        dma((CHUNKS,)), dma((CHUNKS,)),
        dma((CHUNKS,)), dma((CHUNKS,)),
    ]
    terms = pl.pallas_call(
        body,
        out_shape=jax.ShapeDtypeStruct((planes, own_tokens, width), bf16),
        in_specs=[smem] * 3 + [hbm] * 8,
        out_specs=vmem,
        scratch_shapes=scratch,
        compiler_params=pltpu.CompilerParams(
            collective_id=0, has_side_effects=True, vmem_limit_bytes=VMEM_LIMIT
        ),
        name="fused",
    )(
        context_length, jnp.swapaxes(slot_sequence, 1, 2), jnp.swapaxes(slot_slab, 1, 2),
        q_compressed, draft_kv, w_q_nope, w_q_rope, w_uk, w_uv, w_o, keys_hbm,
    )
    return jnp.sum(terms.astype(f32), axis=0)


def shards(
    q_compressed, w_q_nope, w_q_rope, w_uk, w_uv, w_o, kv_cache, draft_kv,
    context_length, slot_sequence, slot_slab,
):
    args = (
        q_compressed, w_q_nope, w_q_rope, w_uk, w_uv, w_o, kv_cache, draft_kv,
        context_length, slot_sequence, slot_slab,
    )
    groups, count = lax.axis_size("group"), lax.axis_size("dev")
    heads = w_uk.shape[0] // groups
    fits = (
        w_uk.shape[0] % groups == 0
        and count % 2 == 0
        and count // 2 in PLANES
        and q_compressed.shape[0] % count == 0
        and groups * q_compressed.shape[0] // DRAFT % (2 * HALVES) == 0
        and kv_cache.shape[2] % 2 == 0
        and heads * DRAFT == 16
        and w_o.shape[1] % (128 * CHUNKS) == 0
    )
    if not fits:
        return shards_general(*args)
    keys = jnp.swapaxes(kv_cache[0, 0], 1, 2)
    return fused(
        q_compressed, w_q_nope, w_q_rope, w_uk, w_uv, w_o, keys, draft_kv,
        context_length, slot_sequence, slot_slab,
    )


def solution(mesh):
    placed = (
        P("group", None),
        P(None, "dev"),
        P(None, "dev"),
        P("dev", None, None),
        P("dev", None, None),
        P("dev", None),
        P("group", "dev", None, None, None),
        P("group", None),
        P(),
        P(),
        P(),
    )
    return jax.shard_map(
        shards, mesh=mesh, in_specs=placed, out_specs=P(("group", "dev"), None), check_vma=False
    )
```

```python
import jax
import jax.numpy as jnp
from jax import lax
from jax.experimental import pallas as pl
from jax.experimental.pallas import tpu as pltpu
from jax.sharding import PartitionSpec as P

NOPE = 128
ROPE = 64
LATENT = 512
VDIM = 128
DRAFT = 4


EMPTY = -1e30


def exchange(axis, call_id, *blocks):
    count = lax.axis_size(axis)
    number = len(blocks)

    def body(*refs):
        sent, got = refs[:number], refs[number : 2 * number]
        send_sems, recv_sems, local_sems = refs[2 * number :]
        me = lax.axis_index(axis)
        barrier = pltpu.get_barrier_semaphore()
        for step in range(1, count):
            pl.semaphore_signal(
                barrier,
                inc=1,
                device_id={axis: lax.rem(me + step, count)},
                device_id_type=pl.DeviceIdType.MESH,
            )
        pl.semaphore_wait(barrier, count - 1)
        started = []
        for step in range(1, count):
            peer = lax.rem(me + step, count)
            for which in range(number):
                copy = pltpu.make_async_remote_copy(
                    src_ref=sent[which].at[peer],
                    dst_ref=got[which].at[me],
                    send_sem=send_sems.at[which, step],
                    recv_sem=recv_sems.at[which, step],
                    device_id={axis: peer},
                    device_id_type=pl.DeviceIdType.MESH,
                )
                copy.start()
                started.append(copy)
        own = []
        for which in range(number):
            copy = pltpu.make_async_copy(
                sent[which].at[me], got[which].at[me], local_sems.at[which]
            )
            copy.start()
            own.append(copy)
        for copy in own:
            copy.wait()
        for copy in started:
            copy.wait()

    vmem = pl.BlockSpec(memory_space=pltpu.VMEM)
    return pl.pallas_call(
        body,
        out_shape=tuple(jax.ShapeDtypeStruct(block.shape, block.dtype) for block in blocks),
        in_specs=[vmem] * number,
        out_specs=tuple([vmem] * number),
        scratch_shapes=[
            pltpu.SemaphoreType.DMA((number, count)),
            pltpu.SemaphoreType.DMA((number, count)),
            pltpu.SemaphoreType.DMA((number,)),
        ],
        compiler_params=pltpu.CompilerParams(
            collective_id=call_id, has_side_effects=True, vmem_limit_bytes=8 * 1024 * 1024
        ),
        name="exchange_%d" % call_id,
    )(*blocks)


def exchange_partials(axis, call_id, block_log, block_mix):
    count = lax.axis_size(axis)
    flat_log = block_log.reshape(count, 1, -1)
    width = flat_log.shape[2]
    padded = -(-width // 128) * 128
    flat_log = jnp.pad(flat_log, ((0, 0), (0, 0), (0, padded - width)))
    flat_mix = block_mix.astype(jnp.bfloat16).reshape(count, -1, block_mix.shape[-1])
    got_log, got_mix = exchange(axis, call_id, flat_log, flat_mix)
    return (
        got_log[:, :, :width].reshape(block_log.shape),
        got_mix.reshape(block_mix.shape).astype(jnp.float32),
    )


def attend_slots(call_id, every_seq, cache_slots, context_length, slot_sequence, slot_slab):
    count = lax.axis_size("dev")
    slot_count, key_width, slab_length = cache_slots.shape
    seq_total, rows, _ = every_seq.shape
    chunk = min(count, max(1, 128 // rows))
    while count % chunk:
        chunk -= 1
    steps = count // chunk
    lanes = -(-rows // 128) * 128
    log_rows = -(-slot_count // 8) * 8

    def body(
        lengths, owners, slabs, every, cache, got_log, got_mix,
        staged, arrived, keys, log_stage, mix_stage,
        key_sems, send_sems, arrive_sems, back_send, back_recv,
    ):
        group = lax.axis_index("group")
        me = lax.axis_index("dev")
        barrier = pltpu.get_barrier_semaphore()

        def greet(step, carry):
            pl.semaphore_signal(
                barrier,
                inc=1,
                device_id={"dev": lax.rem(me + step, count)},
                device_id_type=pl.DeviceIdType.MESH,
            )
            return carry

        lax.fori_loop(1, count, greet, 0)
        for slot in range(slot_count):
            pltpu.make_async_copy(cache.at[slot], keys.at[slot], key_sems.at[slot]).start()
        pl.semaphore_wait(barrier, count - 1)

        def row_copy(peer, source):
            return pltpu.make_async_remote_copy(
                src_ref=staged.at[peer],
                dst_ref=arrived.at[source],
                send_sem=send_sems.at[peer],
                recv_sem=arrive_sems.at[source],
                device_id={"dev": peer},
                device_id_type=pl.DeviceIdType.MESH,
            )

        def back_copies(peer, source):
            return [
                pltpu.make_async_remote_copy(
                    src_ref=stage.at[peer],
                    dst_ref=target.at[source],
                    send_sem=back_send.at[which, peer],
                    recv_sem=back_recv.at[which, source],
                    device_id={"dev": peer},
                    device_id_type=pl.DeviceIdType.MESH,
                )
                for which, (stage, target) in enumerate([(log_stage, got_log), (mix_stage, got_mix)])
            ]

        def send_rows(step, carry):
            peer = lax.rem(me + step, count)
            for slot in range(slot_count):
                owner = jnp.maximum(owners[group, peer, slot], 0)
                staged[peer, slot] = every[owner]
            row_copy(peer, me).start()
            return carry

        lax.fori_loop(1, count, send_rows, 0)
        limits = []
        for slot in range(slot_count):
            owner = owners[group, me, slot]
            arrived[me, slot] = every[jnp.maximum(owner, 0)]
            left = lengths[jnp.maximum(owner, 0)] - slabs[group, me, slot] * slab_length
            limits.append(jnp.where(owner >= 0, left, 0))
        for slot in range(slot_count):
            pltpu.make_async_copy(cache.at[slot], keys.at[slot], key_sems.at[slot]).wait()

        def one_step(step, carry):
            first = lax.rem(me // chunk + steps - step, steps) * chunk
            for at in range(chunk):
                source = first + at

                @pl.when(source != me)
                def _():
                    row_copy(source, source).wait_recv()

            for slot in range(slot_count):
                block = arrived[pl.ds(first, chunk), slot].reshape(chunk * rows, key_width)
                scores = lax.dot_general(
                    block, keys[slot], (((1,), (0,)), ((), ())), preferred_element_type=jnp.float32
                )
                place = lax.broadcasted_iota(jnp.int32, (1, slab_length), 1)
                is_valid = place < limits[slot]
                masked = jnp.where(is_valid, scores, EMPTY)
                peak = jnp.max(masked, axis=1, keepdims=True)
                weights = jnp.where(is_valid, jnp.exp(masked - peak), 0.0)
                total = jnp.maximum(jnp.sum(weights, axis=1, keepdims=True), 1.0)
                mixture = lax.dot_general(
                    weights.astype(jnp.bfloat16),
                    keys[slot, :LATENT],
                    (((1,), (1,)), ((), ())),
                    preferred_element_type=jnp.float32,
                )
                log = jnp.broadcast_to(peak + jnp.log(total), (chunk * rows, 128))
                mix = (mixture / total).astype(jnp.bfloat16).reshape(chunk, rows, LATENT)
                for at in range(chunk):
                    mix_stage[first + at, slot] = mix[at]
                    turned = jnp.transpose(log[at * rows : (at + 1) * rows])
                    log_stage[first + at, slot : slot + 1, :rows] = turned[:1]
            for at in range(chunk):
                source = first + at

                @pl.when(source != me)
                def _():
                    for copy in back_copies(source, me):
                        copy.start()

            return carry

        lax.fori_loop(0, steps, one_step, 0)
        got_log[me] = log_stage[me]
        got_mix[me] = mix_stage[me]

        def finish(step, carry):
            peer = lax.rem(me + step, count)
            row_copy(peer, peer).wait_send()
            for copy in back_copies(peer, peer):
                copy.wait_send()
                copy.wait_recv()
            return carry

        lax.fori_loop(1, count, finish, 0)

    smem = pl.BlockSpec(memory_space=pltpu.SMEM)
    vmem = pl.BlockSpec(memory_space=pltpu.VMEM)
    log_shape = (count, log_rows, lanes)
    mix_shape = (count, slot_count, rows, LATENT)
    got_log, got_mix = pl.pallas_call(
        body,
        out_shape=(
            jax.ShapeDtypeStruct(log_shape, jnp.float32),
            jax.ShapeDtypeStruct(mix_shape, jnp.bfloat16),
        ),
        in_specs=[smem, smem, smem, vmem, pl.BlockSpec(memory_space=pl.ANY)],
        out_specs=(vmem, vmem),
        scratch_shapes=[
            pltpu.VMEM((count, slot_count, rows, key_width), jnp.bfloat16),
            pltpu.VMEM((count, slot_count, rows, key_width), jnp.bfloat16),
            pltpu.VMEM((slot_count, key_width, slab_length), jnp.bfloat16),
            pltpu.VMEM(log_shape, jnp.float32),
            pltpu.VMEM(mix_shape, jnp.bfloat16),
            pltpu.SemaphoreType.DMA((slot_count,)),
            pltpu.SemaphoreType.DMA((count,)),
            pltpu.SemaphoreType.DMA((count,)),
            pltpu.SemaphoreType.DMA((2, count)),
            pltpu.SemaphoreType.DMA((2, count)),
        ],
        compiler_params=pltpu.CompilerParams(
            collective_id=call_id, has_side_effects=True, vmem_limit_bytes=24 * 1024 * 1024
        ),
        name="attend_slots",
    )(
        context_length,
        slot_sequence,
        slot_slab,
        every_seq,
        cache_slots,
    )
    return got_log[:, :slot_count, :rows], got_mix.astype(jnp.float32)


def merge_blocks(block_log, block_out, block_owner, own_log, own_out):
    owners_count = own_log.shape[0]
    matches = block_owner[None, :] == jnp.arange(owners_count, dtype=jnp.int32)[:, None]
    picked = jnp.where(matches[:, :, None, None], block_log[None], EMPTY)
    top_log = jnp.maximum(jnp.max(picked, axis=1), own_log)
    weights = jnp.where(matches[:, :, None, None], jnp.exp(picked - top_log[:, None]), 0.0)
    own_weight = jnp.exp(own_log - top_log)
    weight_sum = jnp.sum(weights, axis=1) + own_weight
    summed = jnp.einsum("sbtx,btxl->stxl", weights, block_out, precision=lax.Precision.HIGHEST)
    summed = summed + own_weight[..., None] * own_out
    return (top_log + jnp.log(weight_sum), summed / weight_sum[..., None])


def draft_partials(queries_seq, draft_rows):
    scores = jnp.einsum(
        "sthk,suk->sthu", queries_seq, draft_rows, preferred_element_type=jnp.float32
    )
    causal = jnp.arange(DRAFT)[None, :] <= jnp.arange(DRAFT)[:, None]
    masked = jnp.where(causal[None, :, None, :], scores, EMPTY)
    draft_peak = jnp.max(masked, axis=3)
    weights = jnp.where(causal[None, :, None, :], jnp.exp(masked - draft_peak[..., None]), 0.0)
    draft_total = jnp.sum(weights, axis=3)
    mixture = jnp.einsum(
        "sthu,sul->sthl",
        weights.astype(jnp.bfloat16),
        draft_rows[..., :LATENT],
        preferred_element_type=jnp.float32,
    )
    return (draft_peak + jnp.log(draft_total), mixture / draft_total[..., None])


def shards_general(
    q_compressed,
    w_q_nope,
    w_q_rope,
    w_uk,
    w_uv,
    w_o,
    kv_cache,
    draft_kv,
    context_length,
    slot_sequence,
    slot_slab,
):
    group_count = lax.axis_size("group")
    holder_count = lax.axis_size("dev")
    group_index = lax.axis_index("group")
    token_count = q_compressed.shape[0]
    seq_group = token_count // DRAFT
    heads_here = w_uk.shape[0]
    key_width = LATENT + ROPE
    q_nope = jnp.dot(q_compressed, w_q_nope, preferred_element_type=jnp.float32).astype(
        jnp.bfloat16
    )
    q_nope = q_nope.reshape(token_count, heads_here, NOPE)
    q_rope = jnp.dot(q_compressed, w_q_rope, preferred_element_type=jnp.float32).reshape(
        token_count, heads_here, ROPE
    )
    absorbed = jnp.einsum("thn,hnl->thl", q_nope, w_uk, preferred_element_type=jnp.float32)
    queries = (jnp.concatenate([absorbed, q_rope], axis=2) * (NOPE + ROPE) ** (-0.5)).astype(
        jnp.bfloat16
    )
    queries_seq = queries.reshape(seq_group, DRAFT, heads_here, key_width)
    draft_log, draft_mix = draft_partials(
        queries_seq, draft_kv.reshape(seq_group, DRAFT, key_width)
    )
    group_table = lax.dynamic_index_in_dim(slot_sequence, group_index, 0, keepdims=False)
    outgoing = jnp.broadcast_to(
        queries_seq.reshape(1, -1, key_width), (group_count, token_count * heads_here, key_width)
    )
    (gathered,) = exchange("group", 0, outgoing)
    back_log, back_mix = attend_slots(
        1,
        gathered.reshape(group_count * seq_group, DRAFT * heads_here, key_width),
        jnp.swapaxes(kv_cache[0, 0], 1, 2),
        context_length,
        slot_sequence,
        slot_slab,
    )
    seq_total = group_count * seq_group
    group_log, group_mix = merge_blocks(
        back_log.reshape(-1, DRAFT, heads_here),
        back_mix.reshape(-1, DRAFT, heads_here, LATENT),
        group_table.reshape(-1),
        jnp.full((seq_total, DRAFT, heads_here), EMPTY, jnp.float32),
        jnp.zeros((seq_total, DRAFT, heads_here, LATENT), jnp.float32),
    )
    home_log, home_mix = exchange_partials(
        "group",
        3,
        group_log.reshape(group_count, seq_group, DRAFT, heads_here),
        group_mix.reshape(group_count, seq_group, DRAFT, heads_here, LATENT),
    )
    home_owner = jnp.tile(jnp.arange(seq_group, dtype=jnp.int32), group_count)
    final_log, final_mix = merge_blocks(
        home_log.reshape(-1, DRAFT, heads_here),
        home_mix.reshape(-1, DRAFT, heads_here, LATENT),
        home_owner,
        draft_log,
        draft_mix,
    )
    attended = final_mix.astype(jnp.bfloat16).reshape(token_count, heads_here, LATENT)
    head_values = jnp.einsum("thl,hlv->thv", attended, w_uv, preferred_element_type=jnp.float32)
    head_values = head_values.astype(jnp.bfloat16).reshape(token_count, heads_here * VDIM)
    partial = jnp.dot(head_values, w_o, preferred_element_type=jnp.float32)
    (terms,) = exchange(
        "dev", 4, partial.reshape(holder_count, token_count // holder_count, -1)
    )
    return jnp.sum(terms, axis=0)


PLANES = (2, 4)
HALVES = 2
CHUNKS = 4
VMEM_LIMIT = 56 * 1024 * 1024


def flip(value, mask, extent):
    result, bit = 0, 1
    while bit < extent:
        own = lax.rem(lax.div(value, bit), 2)
        result = result + bit * (1 - own if mask & bit else own)
        bit *= 2
    return result


def fused(
    q_compressed, w_q_nope, w_q_rope, w_uk, w_uv, w_o, keys_hbm, draft_kv,
    context_length, slot_sequence, slot_slab,
):
    groups, count = lax.axis_size("group"), lax.axis_size("dev")
    planes = count // 2
    around = groups * 2
    home_tokens, q_rank = q_compressed.shape
    tokens = groups * home_tokens
    seqs = tokens // DRAFT
    heads = w_uk.shape[0] // groups
    unit = heads * DRAFT
    rows = seqs * unit
    slots, key_width, slab_length = keys_hbm.shape
    width = w_o.shape[1]
    nope_cols, rope_cols, out_rows = heads * NOPE, heads * ROPE, heads * VDIM
    cut = width // CHUNKS
    own_tokens = home_tokens // count
    bf16, f32 = jnp.bfloat16, jnp.float32
    tiles = LATENT // 128
    all_tiles = slots * tiles + slots // 2

    def body(
        lengths, owners, slabs, qc, dkv, wqn_hbm, wqr_hbm, wuk_hbm, wuv_hbm, wo_hbm, cache, out,
        qall, dall, wqn, wqr, wuk, wuv, wo, keys, *rest,
    ):
        rest = list(rest)
        take = lambda n: [rest.pop(0) for _ in range(n)]
        lat, rot, sided, staged, arrived, mixs, mixg, logs, logg = (take(planes) for _ in range(9))
        zms, zmg, zls, zlg = (take(planes) for _ in range(4))
        parts, pairg, sums, partg, fin = take(5)
        (
            local, g_send, g_recv, z_send, z_recv, p_send, p_recv, b_send, b_recv,
            y_send, y_recv, e_send, e_recv, r_send, r_recv, f_send, f_recv,
        ) = rest
        g = lax.axis_index("group")
        d = lax.axis_index("dev")
        z, c = lax.div(d, 2), lax.rem(d, 2)
        me = g * 2 + c

        def remote(src, dst, send, recv, to_g, to_d):
            return pltpu.make_async_remote_copy(
                src_ref=src, dst_ref=dst, send_sem=send, recv_sem=recv,
                device_id=(to_g, to_d), device_id_type=pl.DeviceIdType.MESH,
            )

        def plane_peer(step):
            return lax.rem(me + step, around)

        def plane_device(j):
            return lax.div(j, 2), z * 2 + lax.rem(j, 2)

        barrier = pltpu.get_barrier_semaphore()

        def greet(to_g, to_d):
            pl.semaphore_signal(
                barrier, inc=1, device_id=(to_g, to_d), device_id_type=pl.DeviceIdType.MESH
            )

        for step in range(1, around):
            greet(*plane_device(plane_peer(step)))
        for step in range(1, planes):
            greet(g, lax.rem(z + step, planes) * 2 + c)

        columns = lambda size: pl.ds(pl.multiple_of(g * size, size), size)
        early = [
            pltpu.make_async_copy(qc, qall.at[g], local.at[6]),
            pltpu.make_async_copy(dkv, dall.at[g], local.at[7]),
        ]
        for copy in early:
            copy.start()
        loads = [
            pltpu.make_async_copy(wqn_hbm.at[:, columns(nope_cols)], wqn, local.at[0]),
            pltpu.make_async_copy(wqr_hbm.at[:, columns(rope_cols)], wqr, local.at[1]),
            pltpu.make_async_copy(wuk_hbm.at[pl.ds(g * heads, heads)], wuk, local.at[2]),
            pltpu.make_async_copy(cache, keys, local.at[3]),
            pltpu.make_async_copy(wuv_hbm.at[pl.ds(g * heads, heads)], wuv, local.at[4]),
            pltpu.make_async_copy(wo_hbm.at[columns(out_rows)], wo, local.at[5]),
        ]
        for copy in loads:
            copy.start()
        pl.semaphore_wait(barrier, around + planes - 2)

        def group_copy(ref, which, step):
            to = flip(g, step, groups) if groups == 4 else lax.rem(g + step, groups)
            return remote(
                ref.at[g], ref.at[g], g_send.at[which], g_recv.at[which], to, d
            )

        def group_wait(ref, which):
            most = ref.at[pl.ds(0, groups - 1)]
            remote(
                most, most, g_send.at[which], g_recv.at[which], lax.rem(g + 1, groups), d
            ).wait()

        for which, ref in enumerate((qall, dall)):
            early[which].wait()
            for step in reversed(range(1, groups)):
                group_copy(ref, which, step).start()
        group_wait(qall, 0)

        def joined(ref):
            pieces = [ref[i].astype(f32) for i in range(groups)]
            return jnp.concatenate(pieces, axis=0).astype(bf16)

        q_tokens = joined(qall)
        for copy in loads[:3]:
            copy.wait()
        nope = jnp.dot(q_tokens, wqn[...], preferred_element_type=f32).astype(bf16)
        rope = jnp.dot(q_tokens, wqr[...], preferred_element_type=f32)
        by_head = []
        for h in range(heads):
            absorbed = jnp.dot(
                nope[:, h * NOPE : (h + 1) * NOPE], wuk[h], preferred_element_type=f32
            )
            pair = jnp.concatenate([absorbed, rope[:, h * ROPE : (h + 1) * ROPE]], axis=1)
            by_head.append((pair * (NOPE + ROPE) ** (-0.5)).astype(bf16))
        stacked = jnp.concatenate(by_head, axis=0)
        row = lax.broadcasted_iota(jnp.int32, (rows, rows), 0)
        col = lax.broadcasted_iota(jnp.int32, (rows, rows), 1)
        spot = lax.rem(lax.div(row, DRAFT), heads) * tokens
        spot = spot + lax.div(row, unit) * DRAFT + lax.rem(row, DRAFT)
        order = jnp.where(col == spot, 1.0, 0.0).astype(bf16)
        queries = jnp.dot(order, stacked, preferred_element_type=f32).astype(bf16)
        for i in range(tiles):
            lat[0][:, i] = queries[:, i * 128 : (i + 1) * 128].reshape(seqs, unit, 128)
        turned = queries[:, LATENT:].astype(f32)
        for i in range(seqs // 2):
            halves = [turned[(2 * i + j) * unit : (2 * i + j + 1) * unit] for j in range(2)]
            rot[0][i] = jnp.concatenate(halves, axis=1).astype(bf16)

        def z_copies(s, half):
            relay = s & 1 and s > 1
            copies = []
            for which, ref in enumerate((lat, rot)):
                source, over = (ref[s ^ 1], 1) if relay else (ref[0], s)
                size = seqs // HALVES // (1 + which)
                span = pl.ds(half * size, size)
                copies.append(
                    remote(
                        source.at[span], ref[s].at[span], z_send.at[which, s, half],
                        z_recv.at[which, s, half], g, flip(z, over, planes) * 2 + c,
                    )
                )
            return copies

        for half in range(HALVES):
            for s in reversed(range(1, planes)):
                if not (s & 1 and s > 1):
                    for copy in z_copies(s, half):
                        copy.start()

        def p_copy(s, to, source):
            return remote(
                staged[s].at[to], arrived[s].at[source], p_send.at[s], p_recv.at[s],
                *plane_device(to),
            )

        most = pl.ds(0, around - 1)
        next_device = plane_device(plane_peer(1))

        def p_whole(s):
            return remote(
                staged[s].at[most], arrived[s].at[most], p_send.at[s], p_recv.at[s], *next_device
            )

        def b_whole(p):
            return [
                remote(
                    stage.at[most], target.at[most], b_send.at[p, which], b_recv.at[p, which],
                    *next_device,
                )
                for which, (stage, target) in enumerate(((mixs[p], mixg[p]), (logs[p], logg[p])))
            ]

        lane_of = lax.broadcasted_iota(jnp.int32, (unit, 128), 1)

        def spread(s):
            for i in range(seqs // 2):
                tile = rot[s][i].astype(f32)
                swapped = jnp.concatenate([tile[:, ROPE:], tile[:, :ROPE]], axis=1).astype(bf16)
                for side in range(2):
                    sided[s][side, 2 * i + side] = rot[s][i]
                    sided[s][side, 2 * i + 1 - side] = swapped

        def pack(dest, at, s, chosen):
            for k in range(slots):
                dest[at, k * tiles : (k + 1) * tiles] = lat[s][chosen[k]]
            for k in range(0, slots, 2):
                sides = [sided[s][side, chosen[k + side]].astype(f32) for side in range(2)]
                both = jnp.where(lane_of < ROPE, sides[0], sides[1])
                dest[at, slots * tiles + k // 2] = both.astype(bf16)

        def dispatch(s):
            if s > 0 and (s % 2 == 1 or s + 1 == planes):
                for half in range(HALVES):
                    for copy in z_copies(s, half):
                        copy.wait_recv()

            spread(s)
            for step in range(1, around):
                to = plane_peer(step)
                to_g, to_d = plane_device(to)
                chosen = [jnp.maximum(owners[to_g, k, to_d], 0) for k in range(slots)]
                pack(staged[s], to, s, chosen)

            def send(step, carry):
                p_copy(s, plane_peer(step), me).start()
                return carry

            lax.fori_loop(1, around, send, 0)
            pack(arrived[s], me, s, [jnp.maximum(owners[g, k, d], 0) for k in range(slots)])

        def b_copies(p, to, source):
            return [
                remote(
                    stage.at[to], target.at[source], b_send.at[p, which],
                    b_recv.at[p, which], *plane_device(to),
                )
                for which, (stage, target) in enumerate(((mixs[p], mixg[p]), (logs[p], logg[p])))
            ]

        def await_rows(p):
            p_whole(p).wait_recv()

        def attend(p, chosen):
            total_rows = around * unit
            position = lax.broadcasted_iota(jnp.int32, (1, slab_length), 1)
            scored = []
            for k in chosen:
                owner = owners[g, k, d]
                left = lengths[jnp.maximum(owner, 0)] - slabs[g, k, d] * slab_length
                cells = [arrived[p][:, k * tiles + i] for i in range(tiles)]
                cells = [cell.reshape(total_rows, 128) for cell in cells]
                turned = arrived[p][:, slots * tiles + k // 2].reshape(total_rows, 128)
                side = k % 2 * ROPE
                block = jnp.concatenate(cells + [turned[:, side : side + ROPE]], axis=1)
                scores = lax.dot_general(
                    block, keys[k], (((1,), (0,)), ((), ())), preferred_element_type=f32
                )
                scored.append((k, scores, position < jnp.where(owner >= 0, left, 0)))
            weighed = []
            for k, scores, is_valid in scored:
                masked = jnp.where(is_valid, scores, EMPTY)
                peak = jnp.max(masked, axis=1, keepdims=True)
                weights = jnp.where(is_valid, jnp.exp(masked - peak), 0.0)
                total = jnp.maximum(jnp.sum(weights, axis=1, keepdims=True), 1.0)
                weighed.append((k, weights.astype(bf16), peak, total))
            for k, weights, peak, total in weighed:
                mixture = lax.dot_general(
                    weights, keys[k, :LATENT], (((1,), (1,)), ((), ())),
                    preferred_element_type=f32,
                )
                mixs[p][:, k] = (mixture / total).astype(bf16).reshape(around, unit, LATENT)
                log = jnp.broadcast_to(peak + jnp.log(total), (total_rows, 128))
                log = jnp.transpose(log)[:1]
                for j in range(around):
                    logs[p][j, k : k + 1, :unit] = log[:, j * unit : (j + 1) * unit]

        def give_back(p):
            def send(step, carry):
                for copy in b_copies(p, plane_peer(step), me):
                    copy.start()
                return carry

            lax.fori_loop(1, around, send, 0)
            mixg[p][me] = mixs[p][me]
            logg[p][me] = logs[p][me]

        def split_dot(weights, block):
            high = weights.astype(bf16)
            low = (weights - high.astype(f32)).astype(bf16)
            return jnp.dot(high, block, preferred_element_type=f32) + jnp.dot(
                low, block, preferred_element_type=f32
            )

        def y_copy(s):
            to = flip(z, s, planes) * 2 + c
            return [
                remote(zms[s], zmg[s], y_send.at[0, s], y_recv.at[0, s], g, to),
                remote(zls[s], zlg[s], y_send.at[1, s], y_recv.at[1, s], g, to),
            ]

        def column_of(s):
            lane = lax.broadcasted_iota(jnp.int32, (rows, rows), 1)
            line = lax.broadcasted_iota(jnp.int32, (rows, rows), 0)
            return jnp.max(jnp.where(lane == line, zlg[s][...], EMPTY), axis=1, keepdims=True)

        wide = around * slots * unit
        lane = lax.broadcasted_iota(jnp.int32, (1, wide), 1)
        owner = jnp.full((1, wide), -1, jnp.int32)
        for j in range(around):
            for k in range(slots):
                here = owners[j // 2, k, z * 2 + j % 2]
                owner = jnp.where(lax.div(lane, unit) == j * slots + k, here, owner)
        tag = owner * unit + lax.rem(lane, unit)
        match = tag == lax.broadcasted_iota(jnp.int32, (rows, 1), 0)

        def merge_plane(p):
            for copy in b_whole(p):
                copy.wait_recv()
            cells = [logg[p][j, k : k + 1, :unit] for j in range(around) for k in range(slots)]
            log = jnp.concatenate(cells, axis=1)
            picked = jnp.where(match, log, EMPTY)
            top = jnp.max(picked, axis=1, keepdims=True)
            weights = jnp.where(match, jnp.exp(picked - top), 0.0)
            total = jnp.maximum(jnp.sum(weights, axis=1, keepdims=True), 1.0)
            block = mixg[p][...].reshape(wide, LATENT)
            mixed = (split_dot(weights, block) / total).astype(bf16)
            logged = jnp.broadcast_to(top + jnp.log(total), (rows, 128))
            mix_to, log_to = (zms[p], zls[p]) if p > 0 else (zmg[p], zlg[p])
            mix_to[...] = mixed
            log_to[...] = jnp.transpose(logged)[:1]
            if p > 0:
                for copy in y_copy(p):
                    copy.start()

        def relay(half):
            for s in range(2, planes - 1, 2):
                for copy in z_copies(s, half):
                    copy.wait_recv()
                for copy in z_copies(s + 1, half):
                    copy.start()

        dispatch(0)
        group_wait(dall, 1)
        draft = joined(dall)
        scores = lax.dot_general(
            queries, draft, (((1,), (1,)), ((), ())), preferred_element_type=f32
        )
        row = lax.broadcasted_iota(jnp.int32, (rows, tokens), 0)
        col = lax.broadcasted_iota(jnp.int32, (rows, tokens), 1)
        seen = (lax.div(row, unit) == lax.div(col, DRAFT)) & (
            lax.rem(col, DRAFT) <= lax.rem(row, DRAFT)
        )
        masked = jnp.where(seen, scores, EMPTY)
        draft_peak = jnp.max(masked, axis=1, keepdims=True)
        weights = jnp.where(seen, jnp.exp(masked - draft_peak), 0.0)
        draft_total = jnp.sum(weights, axis=1, keepdims=True)
        draft_mix = jnp.dot(weights.astype(bf16), draft[:, :LATENT], preferred_element_type=f32)
        draft_mix = draft_mix / draft_total
        draft_log = draft_peak + jnp.log(draft_total)

        every = range(slots)

        def attend_only(p):
            await_rows(p)
            attend(p, every)

        def attend_all(p):
            attend_only(p)
            give_back(p)

        loads[3].wait()
        await_rows(0)
        attend(0, every)
        for half in range(HALVES):
            relay(half)
        if planes == 4:
            dispatch(2)
            dispatch(1)
            dispatch(3)
            attend_all(2)
            attend_all(1)
            attend_all(3)
            give_back(0)
            merge_plane(2)
            merge_plane(1)
            merge_plane(3)
            merge_plane(0)
        else:
            give_back(0)
            dispatch(1)
            merge_plane(0)
            attend_all(1)
            merge_plane(1)

        for s in range(planes):
            p_whole(s).wait_send()
            for copy in b_whole(s):
                copy.wait_send()
        for s in range(1, planes):
            for half in range(HALVES):
                for copy in z_copies(s, half):
                    copy.wait_send()

        def join(merged, s):
            top, total, summed = merged
            log = column_of(s)
            higher = jnp.maximum(top, log)
            scale, weight = jnp.exp(top - higher), jnp.exp(log - higher)
            block = zmg[s][...].astype(f32)
            return higher, scale * total + weight, scale * summed + weight * block

        merged = join((draft_log, jnp.ones_like(draft_log), draft_mix), 0)
        for s in (1, 2, 3)[: planes - 1]:
            for copy in y_copy(s):
                copy.wait_recv()
            merged = join(merged, s)
        top, total, summed = merged
        attended = (summed / total).astype(bf16)
        row = lax.broadcasted_iota(jnp.int32, (rows, rows), 0)
        col = lax.broadcasted_iota(jnp.int32, (rows, rows), 1)
        rank = lax.rem(row, tokens)
        share = planes * own_tokens
        half = groups * share
        line = lax.rem(lax.div(rank, own_tokens), planes) * 2 + lax.div(rank, half)
        token = lax.rem(lax.div(rank, share), groups) * home_tokens + line * own_tokens
        token = token + lax.rem(rank, own_tokens)
        spot = lax.div(token, DRAFT) * unit + lax.div(row, tokens) * DRAFT + lax.rem(token, DRAFT)
        order = jnp.where(col == spot, 1.0, 0.0).astype(bf16)
        attended = jnp.dot(order, attended, preferred_element_type=f32).astype(bf16)
        loads[4].wait()
        loads[5].wait()
        values = [
            jnp.dot(attended[h * tokens : (h + 1) * tokens], wuv[h], preferred_element_type=f32)
            for h in range(heads)
        ]
        values = jnp.concatenate(values, axis=1).astype(bf16)

        def pair_copy(n):
            return remote(
                parts.at[n, 1 - c], pairg.at[n], e_send.at[n], e_recv.at[n], g, z * 2 + 1 - c
            )

        def r_copy(n, to):
            return remote(
                sums.at[n, to], partg.at[n, g], r_send.at[n], r_recv.at[n], to, d
            )

        def r_whole(n):
            rest = pl.ds(0, groups - 1)
            return remote(
                sums.at[n, rest], partg.at[n, rest], r_send.at[n], r_recv.at[n],
                lax.rem(g + 1, groups), d,
            )

        def project(n):
            span = pl.ds(pl.multiple_of(n * cut, 128), cut)
            part = jnp.dot(values, wo[:, span], preferred_element_type=f32)
            for i in range(2):
                parts[n, i] = part[i * half : (i + 1) * half].astype(bf16)
            pair_copy(n).start()

        def pair_up(n):
            pair_copy(n).wait_recv()
            both = parts[n, c].astype(f32) + pairg[n].astype(f32)
            for i in range(groups):
                sums[n, i] = both[i * share : (i + 1) * share].astype(bf16)
            for step in reversed(range(1, groups)):
                r_copy(n, lax.rem(g + step, groups)).start()
            partg[n, g] = sums[n, g]

        def project_on(n, carry):
            project(n)
            pair_up(n - 1)
            return carry

        project(0)
        lax.fori_loop(1, CHUNKS, project_on, 0)
        pair_up(CHUNKS - 1)

        def lane_span(n):
            return pl.ds(pl.multiple_of(n * cut, 128), cut)

        def f_copy(n, to, source):
            return remote(
                fin.at[n, to], out.at[source, :, lane_span(n)], f_send.at[n], f_recv.at[n],
                g, to * 2 + c,
            )

        def f_whole(n):
            rest = pl.ds(0, planes - 1)
            return remote(
                fin.at[n, rest], out.at[rest, :, lane_span(n)], f_send.at[n], f_recv.at[n],
                g, lax.rem(z + 1, planes) * 2 + c,
            )

        def gather(n, carry):
            r_whole(n).wait_recv()
            summed = partg[n, 0].astype(f32)
            for j in range(1, groups):
                summed = summed + partg[n, j].astype(f32)
            for t in range(planes):
                fin[n, t] = summed[t * own_tokens : (t + 1) * own_tokens].astype(bf16)
            for step in range(1, planes):
                f_copy(n, lax.rem(z + step, planes), z).start()
            out[z, :, lane_span(n)] = fin[n, z]
            return carry

        lax.fori_loop(0, CHUNKS, gather, 0)

        for s in range(1, planes):
            for copy in y_copy(s):
                copy.wait_send()
        for n in range(CHUNKS):
            pair_copy(n).wait_send()
            r_whole(n).wait_send()
            f_whole(n).wait_send()
        for n in range(CHUNKS):
            f_whole(n).wait_recv()

    smem = pl.BlockSpec(memory_space=pltpu.SMEM)
    vmem = pl.BlockSpec(memory_space=pltpu.VMEM)
    hbm = pl.BlockSpec(memory_space=pl.ANY)
    scratch = [
        pltpu.VMEM((groups, home_tokens, q_rank), bf16),
        pltpu.VMEM((groups, home_tokens, key_width), bf16),
        pltpu.VMEM((q_rank, nope_cols), bf16),
        pltpu.VMEM((q_rank, rope_cols), bf16),
        pltpu.VMEM((heads, NOPE, LATENT), bf16),
        pltpu.VMEM((heads, LATENT, VDIM), bf16),
        pltpu.VMEM((out_rows, width), bf16),
        pltpu.VMEM((slots, key_width, slab_length), bf16),
    ]
    shapes = [
        ((seqs, tiles, unit, 128), bf16),
        ((seqs // 2, unit, 128), bf16),
        ((2, seqs, unit, 128), bf16),
        ((around, all_tiles, unit, 128), bf16),
        ((around, all_tiles, unit, 128), bf16),
        ((around, slots, unit, LATENT), bf16),
        ((around, slots, unit, LATENT), bf16),
        ((around, slots, 128), f32),
        ((around, slots, 128), f32),
    ]
    scratch += [pltpu.VMEM(*shape) for shape in shapes for _ in range(planes)]
    scratch += [pltpu.VMEM((rows, LATENT), bf16) for _ in range(2 * planes)]
    scratch += [pltpu.VMEM((1, rows), f32) for _ in range(2 * planes)]
    scratch += [
        pltpu.VMEM((CHUNKS, 2, groups * planes * own_tokens, cut), bf16),
        pltpu.VMEM((CHUNKS, groups * planes * own_tokens, cut), bf16),
        pltpu.VMEM((CHUNKS, groups, planes * own_tokens, cut), bf16),
        pltpu.VMEM((CHUNKS, groups, planes * own_tokens, cut), bf16),
    ]
    scratch += [pltpu.VMEM((CHUNKS, planes, own_tokens, cut), bf16)]
    dma = pltpu.SemaphoreType.DMA
    scratch += [
        dma((8,)),
        dma((2,)), dma((2,)),
        dma((2, planes, HALVES)), dma((2, planes, HALVES)),
        dma((planes,)), dma((planes,)),
        dma((planes, 2)), dma((planes, 2)),
        dma((2, planes)), dma((2, planes)),
        dma((CHUNKS,)), dma((CHUNKS,)),
        dma((CHUNKS,)), dma((CHUNKS,)),
        dma((CHUNKS,)), dma((CHUNKS,)),
    ]
    terms = pl.pallas_call(
        body,
        out_shape=jax.ShapeDtypeStruct((planes, own_tokens, width), bf16),
        in_specs=[smem] * 3 + [hbm] * 8,
        out_specs=vmem,
        scratch_shapes=scratch,
        compiler_params=pltpu.CompilerParams(
            collective_id=0, has_side_effects=True, vmem_limit_bytes=VMEM_LIMIT
        ),
        name="fused",
    )(
        context_length, jnp.swapaxes(slot_sequence, 1, 2), jnp.swapaxes(slot_slab, 1, 2),
        q_compressed, draft_kv, w_q_nope, w_q_rope, w_uk, w_uv, w_o, keys_hbm,
    )
    return jnp.sum(terms.astype(f32), axis=0)


def shards(
    q_compressed, w_q_nope, w_q_rope, w_uk, w_uv, w_o, kv_cache, draft_kv,
    context_length, slot_sequence, slot_slab,
):
    args = (
        q_compressed, w_q_nope, w_q_rope, w_uk, w_uv, w_o, kv_cache, draft_kv,
        context_length, slot_sequence, slot_slab,
    )
    groups, count = lax.axis_size("group"), lax.axis_size("dev")
    heads = w_uk.shape[0] // groups
    fits = (
        w_uk.shape[0] % groups == 0
        and count % 2 == 0
        and count // 2 in PLANES
        and q_compressed.shape[0] % count == 0
        and groups * q_compressed.shape[0] // DRAFT % (2 * HALVES) == 0
        and kv_cache.shape[2] % 2 == 0
        and heads * DRAFT == 16
        and w_o.shape[1] % (128 * CHUNKS) == 0
    )
    if not fits:
        return shards_general(*args)
    keys = jnp.swapaxes(kv_cache[0, 0], 1, 2)
    return fused(
        q_compressed, w_q_nope, w_q_rope, w_uk, w_uv, w_o, keys, draft_kv,
        context_length, slot_sequence, slot_slab,
    )


def solution(mesh):
    placed = (
        P("group", None),
        P(None, "dev"),
        P(None, "dev"),
        P("dev", None, None),
        P("dev", None, None),
        P("dev", None),
        P("group", "dev", None, None, None),
        P("group", None),
        P(),
        P(),
        P(),
    )
    return jax.shard_map(
        shards, mesh=mesh, in_specs=placed, out_specs=P(("group", "dev"), None), check_vma=False
    )
```
